32 devices in a mesh: batch: 8 (over z, x), shard: 4 (over y, core).
Axes of the slice: x: 2, y: 2, z: 4, core: 2. Of those that a mesh axis runs over, the one named last changes fastest.
Arguments:
- windows: bfloat16 [32, 1500, 512], P(('batch', 'shard')), may hold values from -6 to 6
- cotangent: bfloat16 [32, 1500, 512], P(('batch', 'shard')), may hold values from -6 to 6
- valid: int32 [32], P(('batch', 'shard')), may hold values 0 or 1
- query_weight: bfloat16 [512, 512], P(('batch', 'shard')), may hold values from -0.375 to 0.375
- key_weight: bfloat16 [512, 512], P(('batch', 'shard')), may hold values from -0.375 to 0.375
- value_weight: bfloat16 [512, 512], P(('batch', 'shard')), may hold values from -0.25 to 0.25
- out_weight: bfloat16 [512, 512], P(('batch', 'shard')), may hold values from -1.5 to 1.5
- up_weight: bfloat16 [512, 2048], P(('batch', 'shard')), may hold values from -0.25 to 0.25
- down_weight: bfloat16 [2048, 512], P(('batch', 'shard')), may hold values from -0.1875 to 0.1875
- query_bias: bfloat16 [512], P(('batch', 'shard')), may hold values from -3 to 3
- value_bias: bfloat16 [512], P(('batch', 'shard')), may hold values from -3 to 3
- out_bias: bfloat16 [512], P(('batch', 'shard')), may hold values from -3 to 3
- up_bias: bfloat16 [2048], P(('batch', 'shard')), may hold values from -3 to 3
- down_bias: bfloat16 [512], P(('batch', 'shard')), may hold values from -3 to 3
- norm_gain: bfloat16 [512], P(('batch', 'shard')), may hold values from 0.5 to 1.5
- norm_shift: bfloat16 [512], P(('batch', 'shard')), may hold values from -2 to 2
- mlp_gain: bfloat16 [512], P(('batch', 'shard')), may hold values from 0.5 to 1.5
- mlp_shift: bfloat16 [512], P(('batch', 'shard')), may hold values from -2 to 2
Outputs:
- output: float32 [32, 1500, 512], P(('batch', 'shard'))
- input_grad: float32 [32, 1500, 512], P(('batch', 'shard'))
- grad_query_weight: float32 [512, 512], P(('batch', 'shard'))
- grad_key_weight: float32 [512, 512], P(('batch', 'shard'))
- grad_value_weight: float32 [512, 512], P(('batch', 'shard'))
- grad_out_weight: float32 [512, 512], P(('batch', 'shard'))
- grad_up_weight: float32 [512, 2048], P(('batch', 'shard'))
- grad_down_weight: float32 [2048, 512], P(('batch', 'shard'))
- grad_query_bias: float32 [512], P(('batch', 'shard'))
- grad_value_bias: float32 [512], P(('batch', 'shard'))
- grad_out_bias: float32 [512], P(('batch', 'shard'))
- grad_up_bias: float32 [2048], P(('batch', 'shard'))
- grad_down_bias: float32 [512], P(('batch', 'shard'))
- grad_norm_gain: float32 [512], P(('batch', 'shard'))
- grad_norm_shift: float32 [512], P(('batch', 'shard'))
- grad_mlp_gain: float32 [512], P(('batch', 'shard'))
- grad_mlp_shift: float32 [512], P(('batch', 'shard'))
The draws below stay inside these ranges and needn't reach their ends.
Inputs may be any that keep to these rules, and one draw needn't show every extreme that they name: `valid`: 1 marks a slot that holds a window, 0 an empty slot.
All inputs are finite; a program needn't handle non-finite values. No bound on the sum of `valid` on one device may be relied on, other than what follows from the above.
Results may differ from the reference program's by a relative error of at most 0.012.
The reference program's roundings to bfloat16 on the way count: a program that leaves them out, or rounds other values in their place, can miss the bound.
Values may be sent and summed in bfloat16 or wider, within the bound.
A program may use at most 192 MiB of HBM per device.

```python
import math
import jax
import jax.numpy as jnp
from jax import lax

D = 512
FF = 2048
HEADS = 8
FRAMES = 1500
WINDOWS = 32


def place_ends(entries, stream_key, least, largest):
    spot = [jax.random.randint(jax.random.fold_in(stream_key, axis), (), 0, length) for axis, length in enumerate(entries.shape)]
    main_axis = entries.shape.index(max(entries.shape))
    next_to = spot[:main_axis] + [(spot[main_axis] + 1) % entries.shape[main_axis]] + spot[main_axis + 1:]
    return entries.at[tuple(spot)].set(least).at[tuple(next_to)].set(largest)


def raised(entries, rng, source, target, shards_of, factor):
    owner, partner = [(jnp.arange(entries.shape[dim]) // (entries.shape[dim] // shards_of)).reshape([-1 if axis == dim else 1 for axis in range(entries.ndim)]) for dim in (source, target)]
    chosen = jax.random.permutation(rng, shards_of)[partner]
    strong = (owner == chosen) | (owner == (partner + shards_of // 2) % shards_of)
    return jnp.where(strong, factor * entries, entries)


def level_of(own_key, extent, pieces, smallest, largest):
    level = 1.0
    for axis_at, parts in pieces:
        steps = jax.random.uniform(jax.random.fold_in(jax.random.fold_in(own_key, 6), axis_at), (parts,), jnp.float32, smallest / len(pieces), largest / len(pieces))
        level = level * jnp.repeat(jnp.exp(steps), extent[axis_at] // parts).reshape((-1,) + (1,) * (len(extent) - 1 - axis_at))
    return level


def gaussian(own_key, shape, spread, most, shards=(), dtype=jnp.bfloat16):
    drawn = jax.random.normal(own_key, shape, jnp.float32) * spread
    if len(shards) > 0:
        drawn = level_of(own_key, shape, shards, -0.22, 0.18) * drawn
    return jnp.clip(drawn, min=-most, max=most).astype(dtype)


def gaussian_with(key, dims, spread, reach, shards, heavy, kind=jnp.bfloat16):
    array = spread * jax.random.normal(key, dims, jnp.float32)
    if shards:
        array = array * level_of(key, dims, shards, -0.22, 0.18)
    return jnp.clip(raised(array, jax.random.fold_in(key, 3), *heavy), -reach, reach).astype(kind)


def setup_inputs(seed: int = 0) -> dict:
    keys = jax.random.split(jax.random.key(seed), 19)
    return {
        "windows": gaussian(keys[0], (WINDOWS, FRAMES, D), 1.0, 6.0, ((0, 32),)),
        "cotangent": gaussian_with(keys[1], (WINDOWS, FRAMES, D), 1.0, 6.0, ((0, 32),), (0, 2, 32, 2.75)),
        "valid": place_ends((jax.random.randint(keys[2], (WINDOWS,), 0, 4) < 3).astype(jnp.int32), jax.random.fold_in(keys[2], 1), 0, 1),
        "query_weight": gaussian(keys[3], (D, D), (D // 2) ** -0.5, 0.375, ((0, 32),)),
        "key_weight": gaussian(keys[4], (D, D), (D // 2) ** -0.5, 0.375, ((0, 32),)),
        "value_weight": gaussian(keys[5], (D, D), D ** -0.5, 0.25, ((0, 32),)),
        "out_weight": gaussian(keys[6], (D, D), (D // 32) ** -0.5, 1.5, ((0, 32),)),
        "up_weight": gaussian(keys[7], (D, FF), D ** -0.5, 0.25, ((0, 32),)),
        "down_weight": gaussian(keys[8], (FF, D), (FF // 2) ** -0.5, 0.1875, ((0, 32),)),
        "query_bias": gaussian(keys[9], (D,), 0.5, 3.0, ((0, 32),)),
        "value_bias": gaussian(keys[10], (D,), 0.5, 3.0, ((0, 32),)),
        "out_bias": gaussian(keys[11], (D,), 0.5, 3.0, ((0, 32),)),
        "up_bias": gaussian(keys[12], (FF,), 0.5, 3.0, ((0, 32),)),
        "down_bias": gaussian(keys[13], (D,), 0.5, 3.0, ((0, 32),)),
        "norm_gain": jnp.clip(1.0 + 0.1 * jax.random.normal(keys[14], (D,), jnp.float32), 0.5, 1.5).astype(jnp.bfloat16),
        "norm_shift": gaussian(keys[15], (D,), 0.3, 2.0, ((0, 32),)),
        "mlp_gain": jnp.clip(1.0 + 0.1 * jax.random.normal(keys[16], (D,), jnp.float32), 0.5, 1.5).astype(jnp.bfloat16),
        "mlp_shift": gaussian(keys[17], (D,), 0.3, 2.0, ((0, 32),)),
    }


NORM_EPS = 1e-05
PRECISE = lax.Precision.HIGHEST

@jax.custom_vjp
def low(v):
    return lax.optimization_barrier(v.astype(jnp.bfloat16)).astype(jnp.float32)

@jax.custom_vjp
def low_back(v):
    return v

def low_keep(v):
    return (low(v), None)

def low_pass(kept, grad):
    return (grad,)

def back_keep(v):
    return (v, None)

def back_low(kept, grad):
    return (low(grad),)
low.defvjp(low_keep, low_pass)
low_back.defvjp(back_keep, back_low)

def matmul(left, right):
    return jnp.dot(left, right, precision=PRECISE, preferred_element_type=jnp.float32)

def layer_norm(values, gain, shift):
    row_mean = lax.optimization_barrier(jnp.mean(values, axis=-1, keepdims=True))
    centred = values - row_mean
    variance = lax.optimization_barrier(jnp.mean(centred * centred, axis=-1, keepdims=True))
    return centred * lax.rsqrt(variance + NORM_EPS) * gain + shift

def head_attention(inputs):
    query_rows, key_rows, value_rows = inputs
    score_scale = 1.0 / math.sqrt(D // HEADS)
    scores = low_back(matmul(query_rows, key_rows.T) * score_scale)
    probabilities = jax.nn.softmax(scores, axis=-1)
    return matmul(low(probabilities), value_rows)

def encoder_layer(inputs, query_weight, key_weight, value_weight, out_weight, up_weight, down_weight, query_bias, value_bias, out_bias, up_bias, down_bias, norm_gain, norm_shift, mlp_gain, mlp_shift):
    frame_count = inputs.shape[0]
    normed = low(layer_norm(inputs, norm_gain, norm_shift))
    query_rows = low(low_back(matmul(normed, query_weight) + query_bias))
    key_rows = low(low_back(matmul(normed, key_weight)))
    value_rows = low(low_back(matmul(normed, value_weight) + value_bias))

    def split_heads(table):
        return table.reshape(frame_count, HEADS, D // HEADS).transpose(1, 0, 2)
    mixed_heads = lax.map(jax.checkpoint(head_attention), (split_heads(query_rows), split_heads(key_rows), split_heads(value_rows)))
    attended = low(low_back(mixed_heads.transpose(1, 0, 2).reshape(frame_count, D)))
    branch = low_back(matmul(attended, out_weight) + out_bias)
    residual = inputs + branch
    normed_two = low(layer_norm(residual, mlp_gain, mlp_shift))
    hidden = low_back(matmul(normed_two, up_weight) + up_bias)
    active = low(jax.nn.gelu(hidden, approximate=False))
    return residual + matmul(active, down_weight) + down_bias

def reference(windows, cotangent, valid, query_weight, key_weight, value_weight, out_weight, up_weight, down_weight, query_bias, value_bias, out_bias, up_bias, down_bias, norm_gain, norm_shift, mlp_gain, mlp_shift):
    parameters = tuple((weight_arg.astype(jnp.float32) for weight_arg in (query_weight, key_weight, value_weight, out_weight, up_weight, down_weight, query_bias, value_bias, out_bias, up_bias, down_bias, norm_gain, norm_shift, mlp_gain, mlp_shift)))
    zero_grads = tuple((jnp.zeros_like(weight_arg) for weight_arg in parameters))

    def window_step(totals, slot_item):
        window_rows, grad_rows, slot_flag = slot_item
        slot_mask = slot_flag.astype(jnp.float32)
        layer_out, pullback = jax.vjp(encoder_layer, window_rows.astype(jnp.float32), *parameters)
        grads = pullback(grad_rows.astype(jnp.float32) * slot_mask)
        totals = tuple((carry_term + new_term for carry_term, new_term in zip(totals, grads[1:])))
        return (totals, (layer_out * slot_mask, grads[0]))
    totals, (outputs, input_grads) = lax.scan(window_step, zero_grads, (windows, cotangent, valid))
    return (outputs, input_grads, totals[0], totals[1], totals[2], totals[3], totals[4], totals[5], totals[6], totals[7], totals[8], totals[9], totals[10], totals[11], totals[12], totals[13], totals[14])
```

```python
import functools
import math

import jax
import jax.numpy as jnp
from jax import lax
from jax.experimental import pallas as pl
from jax.experimental.pallas import tpu as pltpu
from jax.sharding import PartitionSpec as P

HEADS = 8
NORM_EPS = 1e-05
LOG2E = math.log2(math.e)
LN2 = math.log(2.0)
F32 = jnp.float32
BF16 = jnp.bfloat16
ROWS = 256
QUERIES = 768
FF_CHUNK = 512
MASKED = -1e30

NN = (((1,), (0,)), ((), ()))
NT = (((1,), (1,)), ((), ()))
TN = (((0,), (0,)), ((), ()))

TAIL_RATE = 0.2625
TAIL = (
    0.10474836168174968,
    0.10416468281706748,
    0.10263486984927783,
    0.056568077030165455,
    0.14744499390073365,
    -0.13092736820325213,
    0.23259357413631826,
    -0.14775373854130247,
    0.03052653723595064,
)


def dot(left, right, dims):
    return lax.dot_general(left, right, dims, preferred_element_type=F32)


def normalize(values):
    centred = values - jnp.mean(values, axis=-1, keepdims=True)
    variance = jnp.mean(centred * centred, axis=-1, keepdims=True)
    inv_std = lax.rsqrt(variance + NORM_EPS)
    return centred * inv_std, inv_std


def normalize_back(grad_rows, unit_rows, inv_std, gain):
    scaled = grad_rows * gain
    first_mean = jnp.mean(scaled, axis=-1, keepdims=True)
    second_mean = jnp.mean(scaled * unit_rows, axis=-1, keepdims=True)
    return inv_std * (scaled - first_mean - unit_rows * second_mean)


def column_sums(rows):
    return jnp.sum(rows, axis=0, keepdims=True)


def in_three(values):
    high = values.astype(BF16).astype(F32)
    rest = values - high
    middle = rest.astype(BF16).astype(F32)
    return high, middle, rest - middle


def gelu_and_slope(z):
    size = jnp.abs(z)
    t = 1.0 / (1.0 + TAIL_RATE * size)
    poly = jnp.full_like(t, TAIL[-1])
    for coefficient in TAIL[-2::-1]:
        poly = poly * t + coefficient
    bell = jnp.exp2(z * z * (-0.5 * LOG2E))
    tail = poly * t * bell
    cdf = jnp.where(z > 0, 1.0 - tail, tail)
    return z * cdf, cdf + z * bell * (1.0 / math.sqrt(2.0 * math.pi))


def key_extra(head, keys, frames, masked):
    row = lax.broadcasted_iota(jnp.int32, (keys, 128), 0)
    lane = lax.broadcasted_iota(jnp.int32, (keys, 128), 1) - head * 16
    mask = jnp.where(row < frames, 0.0, MASKED)
    ones = jnp.where((lane > 0) & (lane < 4), 1.0, 0.0)
    return jnp.where(lane == 0, mask, ones).astype(BF16)


def attend_kernel(
    frames,
    x_ref,
    wq_ref,
    wk_ref,
    wv_ref,
    bq_ref,
    bv_ref,
    gain_ref,
    shift_ref,
    qa_ref,
    ka_ref,
    vt_ref,
    ht_ref,
    ot_ref,
    qe_ref,
    xs,
    scores,
    peaks,
    key_ext,
    log_rows,
):
    padded, width = xs.shape
    depth = width // HEADS
    xs[pl.ds(0, frames), :] = x_ref[...]
    xs[pl.ds(frames, padded - frames), :] = jnp.zeros((padded - frames, width), BF16)
    gain = gain_ref[...].astype(F32)
    shift = shift_ref[...].astype(F32)
    bq = bq_ref[...].astype(F32)
    bv = bv_ref[...].astype(F32)

    def project(i, carry):
        rows = pl.ds(pl.multiple_of(i * ROWS, ROWS), ROWS)
        unit, _ = normalize(xs[rows, :].astype(F32))
        h1 = (unit * gain + shift).astype(BF16)
        ht_ref[:, rows] = h1.T
        q = (dot(h1, wq_ref[...], NN) + bq).astype(BF16)
        k = dot(h1, wk_ref[...], NN).astype(BF16).astype(F32) * (LOG2E / math.sqrt(depth))
        v = (dot(h1, wv_ref[...], NN) + bv).astype(BF16)
        k_high = k.astype(BF16)
        k_low = (k - k_high.astype(F32)).astype(BF16)
        vt = v.T
        for h in range(HEADS):
            cols = slice(h * depth, (h + 1) * depth)
            qa_ref[h, rows, :] = jnp.concatenate([q[:, cols], q[:, cols]], axis=1)
            ka_ref[h, rows, :] = jnp.concatenate([k_high[:, cols], k_low[:, cols]], axis=1)
            vt_ref[h, 0:depth, rows] = vt[cols, :]
            vt_ref[h, depth : depth + 16, rows] = jnp.ones((16, ROWS), BF16)
        return carry

    lax.fori_loop(0, padded // ROWS, project, 0)

    blocks = padded // QUERIES
    steps = HEADS * blocks
    lane = lax.broadcasted_iota(jnp.int32, (QUERIES, 128), 1)
    query_ext = jnp.where(lane % 16 == 0, 1.0, 0.0).astype(BF16)

    def score(step, slot):
        head = step // blocks
        rows = pl.ds(pl.multiple_of((step % blocks) * QUERIES, QUERIES), QUERIES)
        key_ext[slot] = key_extra(head, padded, frames, True)
        left = jnp.concatenate([ka_ref[head], key_ext[slot]], axis=1)
        right = jnp.concatenate([qa_ref[head, rows, :], query_ext], axis=1)
        s = dot(left, right, NT)
        scores[slot] = s
        peaks[slot] = jnp.max(s, axis=0, keepdims=True)

    def finish(step, slot):
        head = step // blocks
        cols = pl.ds(pl.multiple_of((step % blocks) * QUERIES, QUERIES), QUERIES)
        peak = peaks[slot]
        weights = jnp.exp2(scores[slot] - peak).astype(BF16)
        mixed = dot(vt_ref[head], weights, NN)
        total = mixed[depth : depth + 1, :]
        rows = pl.ds(pl.multiple_of(head * depth, depth), depth)
        ot_ref[rows, cols] = (mixed[:depth, :] * (1.0 / total)).astype(BF16)
        log_rows[head, :, cols] = peak + jnp.log2(total)

    score(0, 0)

    def pair(i, carry):
        score(i * 2 + 1, 1)
        finish(i * 2, 0)
        score(jnp.minimum(i * 2 + 2, steps - 1), 0)
        finish(i * 2 + 1, 1)
        return carry

    lax.fori_loop(0, steps // 2, pair, 0)

    def extend(i, carry):
        rows = pl.ds(pl.multiple_of(i * ROWS, ROWS), ROWS)
        pieces = []
        for h in range(HEADS):
            high, middle, low = in_three(-log_rows[h, :, rows])
            pieces += [jnp.ones((1, ROWS), F32), high, middle, low, jnp.zeros((12, ROWS), F32)]
        qe_ref[rows, :] = jnp.concatenate(pieces, axis=0).T.astype(BF16)
        return carry

    lax.fori_loop(0, padded // ROWS, extend, 0)


def attend(x, wq, wk, wv, bq, bv, gain, shift):
    frames, width = x.shape
    padded = -(-frames // QUERIES) * QUERIES
    vmem = pl.BlockSpec(memory_space=pltpu.VMEM)
    return pl.pallas_call(
        functools.partial(attend_kernel, frames),
        out_shape=[
            jax.ShapeDtypeStruct((HEADS, padded, 128), BF16),
            jax.ShapeDtypeStruct((HEADS, padded, 128), BF16),
            jax.ShapeDtypeStruct((HEADS, 80, padded), BF16),
            jax.ShapeDtypeStruct((width, padded), BF16),
            jax.ShapeDtypeStruct((width, padded), BF16),
            jax.ShapeDtypeStruct((padded, 128), BF16),
        ],
        in_specs=[vmem] * 8,
        out_specs=[vmem] * 6,
        scratch_shapes=[
            pltpu.VMEM((padded, width), BF16),
            pltpu.VMEM((2, padded, QUERIES), F32),
            pltpu.VMEM((2, 1, QUERIES), F32),
            pltpu.VMEM((2, padded, 128), BF16),
            pltpu.VMEM((HEADS, 1, padded), F32),
        ],
        compiler_params=pltpu.CompilerParams(vmem_limit_bytes=60 << 20),
        name="attend",
    )(x, wq, wk, wv, bq, bv, gain, shift)


def mlp_kernel(
    frames,
    flag_ref,
    x_ref,
    cot_ref,
    ot_ref,
    wo_ref,
    wu_ref,
    wd_ref,
    bo_ref,
    bu_ref,
    bd_ref,
    gain_ref,
    shift_ref,
    out_ref,
    dx_ref,
    da_ref,
    gwo_ref,
    gwu_ref,
    gwd_ref,
    gbu_ref,
    small_ref,
):
    step = pl.program_id(0)
    rows, width = x_ref.shape
    hidden = wu_ref.shape[1]
    depth = width // HEADS

    @pl.when(step == 0)
    def _():
        gwo_ref[...] = jnp.zeros_like(gwo_ref)
        gwu_ref[...] = jnp.zeros_like(gwu_ref)
        gwd_ref[...] = jnp.zeros_like(gwd_ref)
        gbu_ref[...] = jnp.zeros_like(gbu_ref)
        small_ref[...] = jnp.zeros_like(small_ref)

    flag = flag_ref[0].astype(F32)
    inside = step * rows + lax.broadcasted_iota(jnp.int32, (rows, width), 0) < frames
    x = jnp.where(inside, x_ref[...].astype(F32), 0.0)
    dy = jnp.where(inside, cot_ref[...].astype(F32), 0.0) * flag
    dy_low = dy.astype(BF16)
    ot = ot_ref[...]
    o = ot.T
    x1 = x + (dot(o, wo_ref[...], NN) + bo_ref[...].astype(F32))
    unit, inv_std = normalize(x1)
    gain = gain_ref[...].astype(F32)
    h2 = (unit * gain + shift_ref[...].astype(F32)).astype(BF16)
    h2t = h2.T
    chunks = hidden // FF_CHUNK
    col = [slice(j * FF_CHUNK, (j + 1) * FF_CHUNK) for j in range(chunks)]
    z_next = dot(h2, wu_ref[:, col[0]], NN)
    out = x1 + bd_ref[...].astype(F32)
    dh2 = jnp.zeros((rows, width), F32)
    for j in range(chunks):
        z = z_next + bu_ref[:, col[j]].astype(F32)
        if j + 1 < chunks:
            z_next = dot(h2, wu_ref[:, col[j + 1]], NN)
        dg = dot(dy_low, wd_ref[col[j], :], NT)
        g, slope = gelu_and_slope(z)
        g = g.astype(BF16)
        dz = (dg * slope).astype(BF16)
        out = out + dot(g, wd_ref[col[j], :], NN)
        gwd_ref[col[j], :] += dot(g, dy_low, TN)
        gwu_ref[:, col[j]] += dot(h2t, dz, NN)
        gbu_ref[:, col[j]] += column_sums(dz.astype(F32))
        dh2 = dh2 + dot(dz, wu_ref[:, col[j]], NT)
    out_ref[...] = out * flag
    dx1 = dy + normalize_back(dh2, unit, inv_std, gain)
    dx_ref[...] = dx1
    da = dx1.astype(BF16)
    gwo_ref[...] += dot(ot, da, NN)
    do = dot(da, wo_ref[...], NT).astype(BF16)
    small_ref[0:1, :] += column_sums(da.astype(F32))
    small_ref[1:2, :] += column_sums(dy)
    small_ref[2:3, :] += column_sums(dh2 * unit)
    small_ref[3:4, :] += column_sums(dh2)
    prod = do.astype(F32) * o.astype(F32)
    lane = lax.broadcasted_iota(jnp.int32, (rows, 64), 1)
    for h in range(HEADS):
        cols = slice(h * depth, (h + 1) * depth)
        high, middle, low = in_three(-jnp.sum(prod[:, cols], axis=1, keepdims=True))
        extra = jnp.where(
            lane == 0, high, jnp.where(lane == 1, middle, jnp.where(lane == 2, low, 0.0))
        ).astype(BF16)
        da_ref[h, :, :] = jnp.concatenate([do[:, cols], extra], axis=1)


def mlp(flag, x, cot, ot, wo, wu, wd, bo, bu, bd, gain, shift):
    frames, width = x.shape
    hidden = wu.shape[1]
    padded = ot.shape[1]
    by_rows = pl.BlockSpec((ROWS, width), lambda i: (i, 0))
    whole = lambda shape: pl.BlockSpec(shape, lambda i: (0,) * len(shape))
    fixed = lambda shape: pl.BlockSpec(
        shape, lambda i: (0,) * len(shape), pipeline_mode=pl.Buffered(1)
    )
    return pl.pallas_call(
        functools.partial(mlp_kernel, frames),
        grid=(padded // ROWS,),
        out_shape=[
            jax.ShapeDtypeStruct((frames, width), F32),
            jax.ShapeDtypeStruct((frames, width), F32),
            jax.ShapeDtypeStruct((HEADS, padded, 128), BF16),
            jax.ShapeDtypeStruct((width, width), F32),
            jax.ShapeDtypeStruct((width, hidden), F32),
            jax.ShapeDtypeStruct((hidden, width), F32),
            jax.ShapeDtypeStruct((1, hidden), F32),
            jax.ShapeDtypeStruct((8, width), F32),
        ],
        in_specs=[
            pl.BlockSpec(memory_space=pltpu.SMEM),
            by_rows,
            by_rows,
            pl.BlockSpec((width, ROWS), lambda i: (0, i)),
            fixed((width, width)),
            fixed((width, hidden)),
            fixed((hidden, width)),
            fixed((1, width)),
            fixed((1, hidden)),
            fixed((1, width)),
            fixed((1, width)),
            fixed((1, width)),
        ],
        out_specs=[
            by_rows,
            by_rows,
            pl.BlockSpec((HEADS, ROWS, 128), lambda i: (0, i, 0)),
            fixed((width, width)),
            fixed((width, hidden)),
            fixed((hidden, width)),
            fixed((1, hidden)),
            fixed((8, width)),
        ],
        compiler_params=pltpu.CompilerParams(
            vmem_limit_bytes=60 << 20, dimension_semantics=("arbitrary",)
        ),
        name="mlp",
    )(flag, x, cot, ot, wo, wu, wd, bo, bu, bd, gain, shift)


def attend_back_kernel(
    frames,
    x_ref,
    dx_ref,
    qa_ref,
    ka_ref,
    vt_ref,
    ht_ref,
    qe_ref,
    da_ref,
    wq_ref,
    wk_ref,
    wv_ref,
    gain_ref,
    shift_ref,
    dinput_ref,
    gwq_ref,
    gwk_ref,
    gwv_ref,
    small_ref,
    dq,
    dkt,
    dvt,
    sum_k,
    sum_v,
    key_ext,
):
    padded = qa_ref.shape[1]
    width = ht_ref.shape[0]
    depth = width // HEADS

    def one_head(head, carry):
        key_ext[...] = key_extra(head, padded, frames, True)
        for i in range(padded // ROWS):
            rows = slice(i * ROWS, (i + 1) * ROWS)
            q = qa_ref[head, rows, :]
            d = da_ref[head, rows, :]
            s = dot(
                jnp.concatenate([q, qe_ref[rows, :]], axis=1),
                jnp.concatenate([ka_ref[head], key_ext[...]], axis=1),
                NT,
            )
            p = jnp.exp2(s)
            dp = dot(d[:, :80], vt_ref[head], NN)
            ds = (p * dp).astype(BF16)
            p = p.astype(BF16)
            new_v = dot(d[:, :depth], p, TN)
            new_k = dot(q[:, :depth], ds, TN)
            if i == 0:
                sum_v[...] = new_v
                sum_k[...] = new_k
            else:
                sum_v[...] += new_v
                sum_k[...] += new_k
            both = dot(ds, ka_ref[head], NN)
            both = both + pltpu.roll(both, depth, 1)
            dq[head, rows, :] = (both * LN2).astype(BF16)
        out_rows = pl.ds(pl.multiple_of(head * depth, depth), depth)
        dkt[out_rows, :] = (sum_k[...] * (1.0 / math.sqrt(depth))).astype(BF16)
        dvt[out_rows, :] = sum_v[...].astype(BF16)
        return carry

    lax.fori_loop(0, HEADS, one_head, 0)

    half = lax.broadcasted_iota(jnp.int32, (padded, 128), 1) < depth
    gwk_ref[...] = dot(ht_ref[...], dkt[...], NT)
    gwv_ref[...] = dot(ht_ref[...], dvt[...], NT)
    for h in range(0, HEADS, 2):
        both = jnp.where(half, dq[h], dq[h + 1])
        gwq_ref[:, h * depth : (h + 2) * depth] = dot(ht_ref[...], both, NN)

    gain = gain_ref[...].astype(F32)
    small_ref[...] = jnp.zeros_like(small_ref)
    for start in range(0, frames, ROWS):
        count = min(ROWS, frames - start)
        rows = slice(start, start + count)
        wide = slice(start, start + ROWS)
        some = half[:ROWS]
        dq_rows = jnp.concatenate(
            [jnp.where(some, dq[h, wide, :], dq[h + 1, wide, :]) for h in range(0, HEADS, 2)],
            axis=1,
        )
        dk_rows = dkt[:, wide].T
        dv_rows = dvt[:, wide].T
        dh1 = (
            dot(dq_rows, wq_ref[...], NT)
            + dot(dk_rows, wk_ref[...], NT)
            + dot(dv_rows, wv_ref[...], NT)
        )
        small_ref[0:1, :] += column_sums(dq_rows.astype(F32))
        small_ref[1:2, :] += column_sums(dv_rows.astype(F32))
        dh1 = dh1[:count]
        unit, inv_std = normalize(x_ref[rows, :].astype(F32))
        small_ref[2:3, :] += column_sums(dh1 * unit)
        small_ref[3:4, :] += column_sums(dh1)
        dinput_ref[rows, :] = dx_ref[rows, :] + normalize_back(dh1, unit, inv_std, gain)


def attend_back(x, dx, qa, ka, vt, ht, qe, da, wq, wk, wv, gain, shift):
    frames, width = x.shape
    padded = ht.shape[1]
    vmem = pl.BlockSpec(memory_space=pltpu.VMEM)
    return pl.pallas_call(
        functools.partial(attend_back_kernel, frames),
        out_shape=[
            jax.ShapeDtypeStruct((frames, width), F32),
            jax.ShapeDtypeStruct((width, width), F32),
            jax.ShapeDtypeStruct((width, width), F32),
            jax.ShapeDtypeStruct((width, width), F32),
            jax.ShapeDtypeStruct((8, width), F32),
        ],
        in_specs=[vmem] * 13,
        out_specs=[vmem] * 5,
        scratch_shapes=[
            pltpu.VMEM((HEADS, padded, 128), BF16),
            pltpu.VMEM((width, padded), BF16),
            pltpu.VMEM((width, padded), BF16),
            pltpu.VMEM((width // HEADS, padded), F32),
            pltpu.VMEM((width // HEADS, padded), F32),
            pltpu.VMEM((padded, 128), BF16),
        ],
        compiler_params=pltpu.CompilerParams(vmem_limit_bytes=60 << 20),
        name="attend_back",
    )(x, dx, qa, ka, vt, ht, qe, da, wq, wk, wv, gain, shift)


def per_device(windows, cotangent, valid, *owned):
    axes = ("batch", "shard")
    full = [lax.all_gather(part, axes, axis=0, tiled=True) for part in owned]
    wq, wk, wv, wo, wu, wd = full[:6]
    bq, bv, bo, bu, bd, gain_one, shift_one, gain_two, shift_two = [
        vector[None, :] for vector in full[6:]
    ]
    x, cot = windows[0], cotangent[0]
    qa, ka, vt, ht, ot, qe = attend(x, wq, wk, wv, bq, bv, gain_one, shift_one)
    out, dx, da, gwo, gwu, gwd, gbu, small_two = mlp(
        valid, x, cot, ot, wo, wu, wd, bo, bu, bd, gain_two, shift_two
    )
    dinput, gwq, gwk, gwv, small_one = attend_back(
        x, dx, qa, ka, vt, ht, qe, da, wq, wk, wv, gain_one, shift_one
    )
    totals = (
        gwq,
        gwk,
        gwv,
        gwo,
        gwu,
        gwd,
        small_one[0],
        small_one[1],
        small_two[0],
        gbu[0],
        small_two[1],
        small_one[2],
        small_one[3],
        small_two[2],
        small_two[3],
    )
    grads = [lax.psum_scatter(total, axes, scatter_dimension=0, tiled=True) for total in totals]
    return (out[None], dinput[None], *grads)


def solution(mesh):
    both = ("batch", "shard")
    windows_spec, matrix, vector = P(both, None, None), P(both, None), P(both)
    params = (matrix,) * 6 + (vector,) * 9
    return jax.shard_map(
        per_device,
        mesh=mesh,
        in_specs=(windows_spec, windows_spec, vector) + params,
        out_specs=(windows_spec, windows_spec) + params,
        check_vma=False,
    )
```

```python
import functools
import math

import jax
import jax.numpy as jnp
from jax import lax
from jax.experimental import pallas as pl
from jax.experimental.pallas import tpu as pltpu
from jax.sharding import PartitionSpec as P

HEADS = 8
NORM_EPS = 1e-05
LOG2E = math.log2(math.e)
LN2 = math.log(2.0)
F32 = jnp.float32
BF16 = jnp.bfloat16
MESH = pl.DeviceIdType.MESH
ROWS = 256
QUERIES = 768
FF_CHUNK = 512
MASKED = -1e30

NN = (((1,), (0,)), ((), ()))
NT = (((1,), (1,)), ((), ()))
TN = (((0,), (0,)), ((), ()))

TAIL_RATE = 0.2625
TAIL = (
    0.10474836168174968,
    0.10416468281706748,
    0.10263486984927783,
    0.056568077030165455,
    0.14744499390073365,
    -0.13092736820325213,
    0.23259357413631826,
    -0.14775373854130247,
    0.03052653723595064,
)


def dot(left, right, dims):
    return lax.dot_general(left, right, dims, preferred_element_type=F32)


def normalize(values):
    centred = values - jnp.mean(values, axis=-1, keepdims=True)
    variance = jnp.mean(centred * centred, axis=-1, keepdims=True)
    inv_std = lax.rsqrt(variance + NORM_EPS)
    return centred * inv_std, inv_std


def normalize_back(grad_rows, unit_rows, inv_std, gain):
    scaled = grad_rows * gain
    first_mean = jnp.mean(scaled, axis=-1, keepdims=True)
    second_mean = jnp.mean(scaled * unit_rows, axis=-1, keepdims=True)
    return inv_std * (scaled - first_mean - unit_rows * second_mean)


def column_sums(rows):
    return jnp.sum(rows, axis=0, keepdims=True)


def in_three(values):
    high = values.astype(BF16).astype(F32)
    rest = values - high
    middle = rest.astype(BF16).astype(F32)
    return high, middle, rest - middle


def gelu_and_slope(z):
    size = jnp.abs(z)
    t = 1.0 / (1.0 + TAIL_RATE * size)
    poly = jnp.full_like(t, TAIL[-1])
    for coefficient in TAIL[-2::-1]:
        poly = poly * t + coefficient
    bell = jnp.exp2(z * z * (-0.5 * LOG2E))
    tail = poly * t * bell
    cdf = jnp.where(z > 0, 1.0 - tail, tail)
    return z * cdf, cdf + z * bell * (1.0 / math.sqrt(2.0 * math.pi))


def key_extra(head, keys, frames):
    row = lax.broadcasted_iota(jnp.int32, (keys, 128), 0)
    lane = lax.broadcasted_iota(jnp.int32, (keys, 128), 1) - head * 16
    mask = jnp.where(row < frames, 0.0, MASKED)
    ones = jnp.where((lane > 0) & (lane < 4), 1.0, 0.0)
    return jnp.where(lane == 0, mask, ones).astype(BF16)


class Place:
    def __init__(self, mesh_shape):
        self.batch, self.shard = mesh_shape
        self.deep = self.batch // 2
        b, s = lax.axis_index("batch"), lax.axis_index("shard")
        self.z, self.x, self.y, self.core = b // 2, b % 2, s // 2, s % 2
        self.me = b * self.shard + s
        self.square = self.x * 2 + self.y

    def moved(self, dz=0, dxy=0, flip=0):
        dx, dy = dxy // 2, dxy % 2
        x = 1 - self.x if dx else self.x
        y = 1 - self.y if dy else self.y
        core = 1 - self.core if flip else self.core
        return (self.z + self.deep + dz) % self.deep * 2 + x, y * 2 + core

    def block(self, dz=0, dxy=0, flip=0):
        b, s = self.moved(-dz, dxy, flip)
        return b * self.shard + s

    def partners(self):
        far = [self.moved(dz=dz) for dz in range(1, self.deep)]
        near = [self.moved(dxy=dxy) for dxy in range(1, 4)]
        return far + near + [self.moved(flip=1)]

    def meet(self):
        barrier = pltpu.get_barrier_semaphore()
        for partner in self.partners():
            pl.semaphore_signal(barrier, inc=1, device_id=partner, device_id_type=MESH)
        pl.semaphore_wait(barrier, self.deep + 3)


class Spread:
    def __init__(self, place, own, table, send_sem, recv_sem):
        self.place, self.own, self.table = place, own, table
        self.send_sem, self.recv_sem = send_sem, recv_sem
        self.started = []

    def copy(self, slot, dz, dxy, device):
        block = self.place.block(dz, dxy)
        here = dz == 0 and dxy == 0
        return pltpu.make_async_remote_copy(
            src_ref=self.own if here else self.table.at[block],
            dst_ref=self.table.at[block],
            send_sem=self.send_sem.at[slot],
            recv_sem=self.recv_sem.at[slot],
            device_id=device,
            device_id_type=MESH,
        )

    def far(self, dz):
        return self.copy(dz - 1, 0, 0, self.place.moved(dz=dz))

    def near(self, dz, dxy):
        slot = self.place.deep - 1 + dz * 3 + dxy - 1
        return self.copy(slot, dz, 0, self.place.moved(dxy=dxy))

    def across(self, dz, dxy):
        slot = self.place.deep * 4 - 1 + dz * 4 + dxy
        return self.copy(slot, dz, dxy, self.place.moved(flip=1))

    def launch(self, copy):
        copy.start()
        self.started.append(copy)

    def begin(self):
        for dz in range(1, self.place.deep):
            self.launch(self.far(dz))
        for dxy in range(1, 4):
            self.launch(self.near(0, dxy))
        self.launch(self.across(0, 0))

    def relay_far(self):
        for dz in range(1, self.place.deep):
            self.far(dz).wait_recv()
            for dxy in range(1, 4):
                self.launch(self.near(dz, dxy))
            self.launch(self.across(dz, 0))

    def relay_near(self):
        for dz in range(self.place.deep):
            for dxy in range(1, 4):
                self.near(dz, dxy).wait_recv()
                self.launch(self.across(dz, dxy))

    def arrive(self):
        for dz in range(self.place.deep):
            for dxy in range(4):
                self.across(dz, dxy).wait_recv()

    def drain(self):
        deep = self.place.deep
        for dz in range(1, deep):
            self.far(dz).wait_send()
        for dz in range(deep):
            for dxy in range(1, 4):
                self.near(dz, dxy).wait_send()
        for dz in range(deep):
            for dxy in range(4):
                self.across(dz, dxy).wait_send()


def spread_small(vector, place):
    row = vector.astype(F32)
    width = 2 * row.shape[1]
    row = jnp.broadcast_to(jnp.concatenate([row, row], axis=1), (8, width))
    lane = lax.broadcasted_iota(jnp.int32, (8, width), 1)
    line = lax.broadcasted_iota(jnp.int32, (8, width), 0)
    short = row
    for p in range(1, 8):
        short = jnp.where(line == p, pltpu.roll(row, width - 16 * p, 1), short)
    start = place.me * 16
    short = pltpu.roll(short, start, 1)
    short = jnp.where((lane >= start) & (lane < start + 16), short, 0.0)
    start = place.me % 8 * 64
    long = pltpu.roll(pltpu.roll(row, width - 128, 1), start, 1)
    long = jnp.where((lane >= start) & (lane < start + 64) & (line == place.me // 8), long, 0.0)
    return jnp.concatenate([long, short], axis=0).astype(BF16)


def matrix(table, first, count=16):
    part = table[:, first : first + count, :]
    return part.reshape(part.shape[0] * count, part.shape[2])


def attend_kernel(frames, mesh_shape, *refs):
    if mesh_shape is None:
        x_ref, table, small_ref = refs[:3]
        qa_ref, ka_ref, vt_ref, ht_ref, ot_ref, qe_ref = refs[3:9]
        xs, scores, peaks, key_ext, log_rows = refs[9:]
    else:
        x_ref, vec_ref, wq_own, wk_own, wv_own, wo_own, wu_own, wd_own = refs[:8]
        qa_ref, ka_ref, vt_ref, ht_ref, ot_ref, qe_ref, small_ref, first_ref, second_ref = refs[
            8:17
        ]
        xs, scores, peaks, key_ext, log_rows, table, own, send_1, recv_1, send_2, recv_2, keep = (
            refs[17:]
        )
        place = Place(mesh_shape)
        first = Spread(place, table.at[place.me], table, send_1, recv_1)
        second = Spread(place, own, second_ref, send_2, recv_2)
        table[place.me, 0:16, :] = wq_own[...]
        table[place.me, 16:32, :] = wk_own[...]
        table[place.me, 32:48, :] = wv_own[...]
        table[place.me, 48:64, :] = spread_small(vec_ref[...], place)
        own[0:16, :] = wo_own[...]
        chunks = wu_own.shape[1] // FF_CHUNK
        for j in range(chunks):
            own[16 + 16 * j : 32 + 16 * j, :] = wu_own[:, j * FF_CHUNK : (j + 1) * FF_CHUNK]
        own[16 + 16 * chunks :, :] = wd_own[...]
        place.meet()
        first.begin()
        first.relay_far()
        first.relay_near()
        second.begin()
        keep_own = pltpu.make_async_copy(own, second_ref.at[place.me], keep.at[0])
        keep_own.start()

    padded, width = xs.shape
    depth = width // HEADS
    xs[pl.ds(0, frames), :] = x_ref[...]
    xs[pl.ds(frames, padded - frames), :] = jnp.zeros((padded - frames, width), BF16)
    if mesh_shape is not None:
        first.arrive()
        keep_first = pltpu.make_async_copy(table, first_ref, keep.at[1])
        keep_first.start()
        small_ref[...] = jnp.sum(table[:, 48:64, :].astype(F32), axis=0)
    bq, bv, gain, shift = (small_ref[r : r + 1, :] for r in (8, 9, 12, 13))

    def project(i, carry):
        rows = pl.ds(pl.multiple_of(i * ROWS, ROWS), ROWS)
        unit, _ = normalize(xs[rows, :].astype(F32))
        h1 = (unit * gain + shift).astype(BF16)
        ht_ref[:, rows] = h1.T
        q = (dot(h1, matrix(table, 0), NN) + bq).astype(BF16)
        k = dot(h1, matrix(table, 16), NN).astype(BF16).astype(F32)
        k = k * (LOG2E / math.sqrt(depth))
        v = (dot(h1, matrix(table, 32), NN) + bv).astype(BF16)
        k_high = k.astype(BF16)
        k_low = (k - k_high.astype(F32)).astype(BF16)
        vt = v.T
        for h in range(HEADS):
            cols = slice(h * depth, (h + 1) * depth)
            qa_ref[h, rows, :] = jnp.concatenate([q[:, cols], q[:, cols]], axis=1)
            ka_ref[h, rows, :] = jnp.concatenate([k_high[:, cols], k_low[:, cols]], axis=1)
            vt_ref[h, 0:depth, rows] = vt[cols, :]
            vt_ref[h, depth : depth + 16, rows] = jnp.ones((16, ROWS), BF16)
        return carry

    lax.fori_loop(0, padded // ROWS, project, 0)

    blocks = padded // QUERIES
    steps = HEADS * blocks
    lane = lax.broadcasted_iota(jnp.int32, (QUERIES, 128), 1)
    query_ext = jnp.where(lane % 16 == 0, 1.0, 0.0).astype(BF16)

    def score(step, slot):
        head = step // blocks
        rows = pl.ds(pl.multiple_of((step % blocks) * QUERIES, QUERIES), QUERIES)
        key_ext[slot] = key_extra(head, padded, frames)
        left = jnp.concatenate([ka_ref[head], key_ext[slot]], axis=1)
        right = jnp.concatenate([qa_ref[head, rows, :], query_ext], axis=1)
        s = dot(left, right, NT)
        scores[slot] = s
        peaks[slot] = jnp.max(s, axis=0, keepdims=True)

    def finish(step, slot):
        head = step // blocks
        cols = pl.ds(pl.multiple_of((step % blocks) * QUERIES, QUERIES), QUERIES)
        peak = peaks[slot]
        weights = jnp.exp2(scores[slot] - peak).astype(BF16)
        mixed = dot(vt_ref[head], weights, NN)
        total = mixed[depth : depth + 1, :]
        rows = pl.ds(pl.multiple_of(head * depth, depth), depth)
        ot_ref[rows, cols] = (mixed[:depth, :] * (1.0 / total)).astype(BF16)
        log_rows[head, :, cols] = peak + jnp.log2(total)

    score(0, 0)

    def pair(i, carry):
        if mesh_shape is not None:
            pl.when(i == 1)(second.relay_far)
            pl.when(i == 5)(second.relay_near)
        score(i * 2 + 1, 1)
        finish(i * 2, 0)
        score(jnp.minimum(i * 2 + 2, steps - 1), 0)
        finish(i * 2 + 1, 1)
        return carry

    lax.fori_loop(0, steps // 2, pair, 0)

    def extend(i, carry):
        rows = pl.ds(pl.multiple_of(i * ROWS, ROWS), ROWS)
        pieces = []
        for h in range(HEADS):
            high, middle, low = in_three(-log_rows[h, :, rows])
            pieces += [jnp.ones((1, ROWS), F32), high, middle, low, jnp.zeros((12, ROWS), F32)]
        qe_ref[rows, :] = jnp.concatenate(pieces, axis=0).T.astype(BF16)
        return carry

    lax.fori_loop(0, padded // ROWS, extend, 0)
    if mesh_shape is not None:
        second.arrive()
        keep_own.wait()
        keep_first.wait()
        first.drain()
        second.drain()


def attend(mesh_shape, x, *rest):
    frames, width = x.shape
    padded = -(-frames // QUERIES) * QUERIES
    blocks = width // 16
    vmem = pl.BlockSpec(memory_space=pltpu.VMEM)
    anywhere = pl.BlockSpec(memory_space=pl.ANY)
    out_shape = [
        jax.ShapeDtypeStruct((HEADS, padded, 128), BF16),
        jax.ShapeDtypeStruct((HEADS, padded, 128), BF16),
        jax.ShapeDtypeStruct((HEADS, 80, padded), BF16),
        jax.ShapeDtypeStruct((width, padded), BF16),
        jax.ShapeDtypeStruct((width, padded), BF16),
        jax.ShapeDtypeStruct((padded, 128), BF16),
    ]
    scratch = [
        pltpu.VMEM((padded, width), BF16),
        pltpu.VMEM((2, padded, QUERIES), F32),
        pltpu.VMEM((2, 1, QUERIES), F32),
        pltpu.VMEM((2, padded, 128), BF16),
        pltpu.VMEM((HEADS, 1, padded), F32),
    ]
    out_specs = [vmem] * 6
    options = {}
    if mesh_shape is not None:
        hidden = rest[5].shape[1]
        own_rows = 16 + hidden // FF_CHUNK * 16 + rest[6].shape[0]
        out_shape += [
            jax.ShapeDtypeStruct((16, width), F32),
            jax.ShapeDtypeStruct((blocks, 64, width), BF16),
            jax.ShapeDtypeStruct((blocks, own_rows, width), BF16),
        ]
        out_specs += [vmem, anywhere, anywhere]
        scratch += [
            pltpu.VMEM((blocks, 64, width), BF16),
            pltpu.VMEM((own_rows, width), BF16),
        ]
        scratch += [pltpu.SemaphoreType.DMA((blocks - 1,)) for _ in range(4)]
        scratch += [pltpu.SemaphoreType.DMA((2,))]
        options = dict(collective_id=0, has_side_effects=True)
    return pl.pallas_call(
        functools.partial(attend_kernel, frames, mesh_shape),
        out_shape=out_shape,
        in_specs=[vmem] * (1 + len(rest)),
        out_specs=out_specs,
        scratch_shapes=scratch,
        compiler_params=pltpu.CompilerParams(vmem_limit_bytes=60 << 20, **options),
        name="attend",
    )(x, *rest)


def mlp_kernel(
    frames,
    flag_ref,
    x_ref,
    cot_ref,
    ot_ref,
    table,
    vec_ref,
    out_ref,
    dx_ref,
    da_ref,
    grads_ref,
    small_ref,
    gwo,
    gwu,
    gwd,
):
    step = pl.program_id(0)
    rows, width = x_ref.shape
    chunks = gwu.shape[0]
    depth = width // HEADS
    down = table.shape[1] - 16 - 16 * chunks
    per_chunk = FF_CHUNK // down

    def up_part(j):
        return matrix(table, 16 + 16 * j)

    def down_part(j):
        part = table[j * per_chunk : (j + 1) * per_chunk, 16 + 16 * chunks :, :]
        return part.reshape(FF_CHUNK, width)

    @pl.when(step == 0)
    def _():
        gwo[...] = jnp.zeros_like(gwo)
        gwu[...] = jnp.zeros_like(gwu)
        gwd[...] = jnp.zeros_like(gwd)
        small_ref[...] = jnp.zeros_like(small_ref)

    flag = flag_ref[0].astype(F32)
    inside = step * rows + lax.broadcasted_iota(jnp.int32, (rows, width), 0) < frames
    x = jnp.where(inside, x_ref[...].astype(F32), 0.0)
    dy = jnp.where(inside, cot_ref[...].astype(F32), 0.0) * flag
    dy_low = dy.astype(BF16)
    bo, bd, gain, shift = (vec_ref[r : r + 1, :] for r in (10, 11, 14, 15))
    wo = matrix(table, 0)
    ot = ot_ref[...]
    o = ot.T
    x1 = x + (dot(o, wo, NN) + bo)
    unit, inv_std = normalize(x1)
    h2 = (unit * gain + shift).astype(BF16)
    h2t = h2.T
    z_next = dot(h2, up_part(0), NN)
    out = x1 + bd
    dh2 = jnp.zeros((rows, width), F32)
    for j in range(chunks):
        z = z_next + vec_ref[j : j + 1, :]
        if j + 1 < chunks:
            z_next = dot(h2, up_part(j + 1), NN)
        dg = dot(dy_low, down_part(j), NT)
        g, slope = gelu_and_slope(z)
        g = g.astype(BF16)
        dz = (dg * slope).astype(BF16)
        out = out + dot(g, down_part(j), NN)
        gwd[j] += dot(g, dy_low, TN)
        gwu[j] += dot(h2t, dz, NN)
        small_ref[j : j + 1, :] += column_sums(dz.astype(F32))
        dh2 = dh2 + dot(dz, up_part(j), NT)
    out_ref[...] = out * flag
    dx1 = dy + normalize_back(dh2, unit, inv_std, gain)
    dx_ref[...] = dx1
    da = dx1.astype(BF16)
    gwo[...] += dot(ot, da, NN)
    do = dot(da, wo, NT).astype(BF16)
    small_ref[10:11, :] += column_sums(da.astype(F32))
    small_ref[11:12, :] += column_sums(dy)
    small_ref[14:15, :] += column_sums(dh2 * unit)
    small_ref[15:16, :] += column_sums(dh2)
    prod = do.astype(F32) * o.astype(F32)
    lane = lax.broadcasted_iota(jnp.int32, (rows, 64), 1)
    for h in range(HEADS):
        cols = slice(h * depth, (h + 1) * depth)
        high, middle, low = in_three(-jnp.sum(prod[:, cols], axis=1, keepdims=True))
        extra = jnp.where(
            lane == 0, high, jnp.where(lane == 1, middle, jnp.where(lane == 2, low, 0.0))
        ).astype(BF16)
        da_ref[h, :, :] = jnp.concatenate([do[:, cols], extra], axis=1)

    @pl.when(step == pl.num_programs(0) - 1)
    def _():
        split = lambda part, count: part.astype(BF16).reshape(-1, count, width)
        grads_ref[:, 0:16, :] = split(gwo[...], 16)
        for j in range(chunks):
            grads_ref[:, 16 + 16 * j : 32 + 16 * j, :] = split(gwu[j], 16)
            grads_ref[j * per_chunk : (j + 1) * per_chunk, 16 + 16 * chunks :, :] = split(
                gwd[j], down
            )


def mlp(flag, x, cot, ot, table, vectors):
    frames, width = x.shape
    padded = ot.shape[1]
    blocks, rows = table.shape[:2]
    chunks = (rows - 16) * blocks // (2 * FF_CHUNK)
    by_rows = pl.BlockSpec((ROWS, width), lambda i: (i, 0))
    fixed = lambda shape: pl.BlockSpec(
        shape, lambda i: (0,) * len(shape), pipeline_mode=pl.Buffered(1)
    )
    return pl.pallas_call(
        functools.partial(mlp_kernel, frames),
        grid=(padded // ROWS,),
        out_shape=[
            jax.ShapeDtypeStruct((frames, width), F32),
            jax.ShapeDtypeStruct((frames, width), F32),
            jax.ShapeDtypeStruct((HEADS, padded, 128), BF16),
            jax.ShapeDtypeStruct(table.shape, BF16),
            jax.ShapeDtypeStruct((16, width), F32),
        ],
        in_specs=[
            pl.BlockSpec(memory_space=pltpu.SMEM),
            by_rows,
            by_rows,
            pl.BlockSpec((width, ROWS), lambda i: (0, i)),
            fixed(table.shape),
            fixed((16, width)),
        ],
        out_specs=[
            by_rows,
            by_rows,
            pl.BlockSpec((HEADS, ROWS, 128), lambda i: (0, i, 0)),
            fixed(table.shape),
            fixed((16, width)),
        ],
        scratch_shapes=[
            pltpu.VMEM((width, width), F32),
            pltpu.VMEM((chunks, width, FF_CHUNK), F32),
            pltpu.VMEM((chunks, FF_CHUNK, width), F32),
        ],
        compiler_params=pltpu.CompilerParams(
            vmem_limit_bytes=60 << 20, dimension_semantics=("arbitrary",)
        ),
        name="mlp",
    )(flag, x, cot, ot, table, vectors)


class Gather:
    def __init__(self, place, source, from_core, halves, from_near, quarter, from_far, sems):
        self.place, self.source = place, source
        self.from_core, self.halves = from_core, halves
        self.from_near, self.quarter = from_near, quarter
        self.from_far = from_far
        self.send_sem, self.recv_sem = sems

    def copy(self, slot, src, dst, device):
        return pltpu.make_async_remote_copy(
            src_ref=src,
            dst_ref=dst,
            send_sem=self.send_sem.at[slot],
            recv_sem=self.recv_sem.at[slot],
            device_id=device,
            device_id_type=MESH,
        )

    def across(self):
        place = self.place
        return [
            self.copy(
                z, self.source.at[z, :, 1 - place.core], self.from_core.at[z], place.moved(flip=1)
            )
            for z in range(place.deep)
        ]

    def near(self):
        place = self.place
        copies = []
        for dxy in range(1, 4):
            b, s = place.moved(dxy=dxy)
            square = b % 2 * 2 + s // 2
            copies.append(
                self.copy(
                    place.deep + dxy - 1,
                    self.halves.at[:, square],
                    self.from_near.at[dxy - 1],
                    (b, s),
                )
            )
        return copies

    def far(self):
        place = self.place
        copies = []
        for dz in range(1, place.deep):
            z = (place.z + dz) % place.deep
            copies.append(
                self.copy(
                    place.deep + 2 + dz,
                    self.quarter.at[z],
                    self.from_far.at[dz - 1],
                    place.moved(dz=dz),
                )
            )
        return copies

    def fold_across(self, own):
        for copy in self.across():
            copy.wait_recv()

        def one(i, carry):
            z, q = i // 4, i % 4
            total = own(z, q).astype(F32) + self.from_core[z, q].astype(F32)
            self.halves[z, q] = total.astype(BF16)
            return carry

        lax.fori_loop(0, self.place.deep * 4, one, 0)
        for copy in self.near():
            copy.start()

    def fold_near(self):
        for copy in self.near():
            copy.wait_recv()

        def one(z, carry):
            total = self.halves[z, self.place.square].astype(F32)
            for dxy in range(3):
                total = total + self.from_near[dxy, z].astype(F32)
            self.quarter[z] = total.astype(BF16)
            return carry

        lax.fori_loop(0, self.place.deep, one, 0)
        for copy in self.far():
            copy.start()

    def result(self):
        for copy in self.far():
            copy.wait_recv()
        total = self.quarter[self.place.z].astype(F32)
        for dz in range(self.place.deep - 1):
            total = total + self.from_far[dz].astype(F32)
        return total

    def drain(self):
        for copy in self.across() + self.near() + self.far():
            copy.wait_send()


class SmallSum:
    def __init__(self, place, buffers, received, sems):
        self.place, self.buffers, self.received = place, buffers, received
        self.send_sem, self.recv_sem = sems

    def copies(self, stage):
        place = self.place
        if stage == 0:
            devices, first = [place.moved(flip=1)], 0
        elif stage == 1:
            devices, first = [place.moved(dxy=dxy) for dxy in range(1, 4)], 1
        else:
            devices, first = [place.moved(dz=dz) for dz in range(1, place.deep)], 4
        return [
            pltpu.make_async_remote_copy(
                src_ref=self.buffers.at[stage],
                dst_ref=self.received.at[first + i],
                send_sem=self.send_sem.at[first + i],
                recv_sem=self.recv_sem.at[first + i],
                device_id=device,
                device_id_type=MESH,
            )
            for i, device in enumerate(devices)
        ]

    def send(self, stage, value):
        self.buffers[stage] = value
        for copy in self.copies(stage):
            copy.start()

    def receive(self, stage):
        total = self.buffers[stage]
        first = (0, 1, 4)[stage]
        for i, copy in enumerate(self.copies(stage)):
            copy.wait_recv()
            total = total + self.received[first + i]
        return total

    def drain(self):
        for stage in range(3):
            for copy in self.copies(stage):
                copy.wait_send()


def own_small(total, place):
    width = total.shape[1]
    line = lax.broadcasted_iota(jnp.int32, total.shape, 0)
    short = pltpu.roll(total, width - place.me * 16, 1)
    long = jnp.sum(jnp.where(line == place.me // 8, total, 0.0), axis=0, keepdims=True)
    long = pltpu.roll(jnp.broadcast_to(long, total.shape), width - place.me % 8 * 64, 1)
    return jnp.where(line == 0, long, short)[:, :128]


def attend_back_kernel(frames, mesh_shape, *refs):
    x_ref, dx_ref, qa_ref, ka_ref, vt_ref, ht_ref, qe_ref, da_ref, table, vec_ref, small_in = refs[
        :11
    ]
    if mesh_shape is None:
        dinput_ref, first_source, small_ref = refs[11:14]
        dq, dkt, dvt, sum_k, sum_v, key_ext, small = refs[14:]
    else:
        grads_ref = refs[11]
        dinput_ref, first_own, second_own, small_ref = refs[12:16]
        dq, dkt, dvt, sum_k, sum_v, key_ext, small, first_source = refs[16:24]
        place = Place(mesh_shape)
        first = Gather(place, first_source, *refs[24:29], refs[29:31])
        second = Gather(place, grads_ref, *refs[31:36], refs[36:38])
        shorts = SmallSum(place, refs[38], refs[39], refs[40:42])
        second_half, keep = refs[42:]
        place.meet()
        for copy in second.across():
            copy.start()
        keep_half = pltpu.make_async_copy(grads_ref.at[:, :, place.core], second_half, keep)
        keep_half.start()

    padded = qa_ref.shape[1]
    width = ht_ref.shape[0]
    depth = width // HEADS

    def second_across():
        keep_half.wait()
        second.fold_across(lambda z, q: second_half[z, q])

    def one_head(head, carry):
        if mesh_shape is not None:
            pl.when(head == 1)(second_across)
            pl.when(head == 5)(second.fold_near)
        key_ext[...] = key_extra(head, padded, frames)
        for i in range(padded // ROWS):
            rows = slice(i * ROWS, (i + 1) * ROWS)
            q = qa_ref[head, rows, :]
            d = da_ref[head, rows, :]
            s = dot(
                jnp.concatenate([q, qe_ref[rows, :]], axis=1),
                jnp.concatenate([ka_ref[head], key_ext[...]], axis=1),
                NT,
            )
            p = jnp.exp2(s)
            dp = dot(d[:, :80], vt_ref[head], NN)
            ds = (p * dp).astype(BF16)
            p = p.astype(BF16)
            new_v = dot(d[:, :depth], p, TN)
            new_k = dot(q[:, :depth], ds, TN)
            if i == 0:
                sum_v[...] = new_v
                sum_k[...] = new_k
            else:
                sum_v[...] += new_v
                sum_k[...] += new_k
            both = dot(ds, ka_ref[head], NN)
            both = both + pltpu.roll(both, depth, 1)
            dq[head, rows, :] = (both * LN2).astype(BF16)
        out_rows = pl.ds(pl.multiple_of(head * depth, depth), depth)
        dkt[out_rows, :] = (sum_k[...] * (1.0 / math.sqrt(depth))).astype(BF16)
        dvt[out_rows, :] = sum_v[...].astype(BF16)
        return carry

    lax.fori_loop(0, HEADS, one_head, 0)

    half = lax.broadcasted_iota(jnp.int32, (padded, 128), 1) < depth

    def keep_grad(first_row, cols, value):
        shape = first_source.shape[:-2] + (16, value.shape[1])
        index = (slice(None),) * (len(shape) - 2)
        first_source[index + (slice(first_row, first_row + 16), cols)] = value.astype(BF16).reshape(
            shape
        )

    for h in range(0, HEADS, 2):
        both = jnp.where(half, dq[h], dq[h + 1])
        keep_grad(0, slice(h * depth, (h + 2) * depth), dot(ht_ref[...], both, NN))
    keep_grad(16, slice(0, width), dot(ht_ref[...], dkt[...], NT))
    keep_grad(32, slice(0, width), dot(ht_ref[...], dvt[...], NT))
    if mesh_shape is not None:
        for copy in first.across():
            copy.start()
        second_own[...] = second.result()

    gain = vec_ref[12:13, :]
    small[...] = small_in[...]
    for index, start in enumerate(range(0, frames, ROWS)):
        if mesh_shape is not None and index == 2:
            first.fold_across(lambda z, q: first_source[z, q, place.core])
        count = min(ROWS, frames - start)
        rows = slice(start, start + count)
        wide = slice(start, start + ROWS)
        some = half[:ROWS]
        dq_rows = jnp.concatenate(
            [jnp.where(some, dq[h, wide, :], dq[h + 1, wide, :]) for h in range(0, HEADS, 2)],
            axis=1,
        )
        dk_rows = dkt[:, wide].T
        dv_rows = dvt[:, wide].T
        dh1 = (
            dot(dq_rows, matrix(table, 0), NT)
            + dot(dk_rows, matrix(table, 16), NT)
            + dot(dv_rows, matrix(table, 32), NT)
        )
        small[8:9, :] += column_sums(dq_rows.astype(F32))
        small[9:10, :] += column_sums(dv_rows.astype(F32))
        dh1 = dh1[:count]
        unit, inv_std = normalize(x_ref[rows, :].astype(F32))
        small[12:13, :] += column_sums(dh1 * unit)
        small[13:14, :] += column_sums(dh1)
        dinput_ref[rows, :] = dx_ref[rows, :] + normalize_back(dh1, unit, inv_std, gain)
    if mesh_shape is None:
        small_ref[...] = small[...]
    else:
        shorts.send(0, small[...])
        first.fold_near()
        shorts.send(1, shorts.receive(0))
        shorts.send(2, shorts.receive(1))
        first_own[...] = first.result()
        small_ref[...] = own_small(shorts.receive(2), place)
        second.drain()
        first.drain()
        shorts.drain()


def attend_back(mesh_shape, x, dx, qa, ka, vt, ht, qe, da, table, vectors, small, grads):
    frames, width = x.shape
    padded = ht.shape[1]
    blocks = width // 16
    vmem = pl.BlockSpec(memory_space=pltpu.VMEM)
    args = [x, dx, qa, ka, vt, ht, qe, da, table, vectors, small]
    in_specs = [vmem] * len(args)
    out_shape = [jax.ShapeDtypeStruct((frames, width), F32)]
    scratch = [
        pltpu.VMEM((HEADS, padded, 128), BF16),
        pltpu.VMEM((width, padded), BF16),
        pltpu.VMEM((width, padded), BF16),
        pltpu.VMEM((width // HEADS, padded), F32),
        pltpu.VMEM((width // HEADS, padded), F32),
        pltpu.VMEM((padded, 128), BF16),
        pltpu.VMEM((16, width), F32),
    ]
    options = {}
    if mesh_shape is None:
        out_shape += [
            jax.ShapeDtypeStruct((blocks, 48, width), BF16),
            jax.ShapeDtypeStruct((16, width), F32),
        ]
    else:
        deep = mesh_shape[0] // 2
        rows = grads.shape[1]
        args.append(grads.reshape(deep, 4, 2, rows, width))
        in_specs.append(pl.BlockSpec(memory_space=pl.ANY))
        out_shape += [
            jax.ShapeDtypeStruct((48, width), F32),
            jax.ShapeDtypeStruct((rows, width), F32),
            jax.ShapeDtypeStruct((16, 128), F32),
        ]
        scratch.append(pltpu.VMEM((deep, 4, 2, 48, width), BF16))
        for count in (48, rows):
            scratch += [
                pltpu.VMEM((deep, 4, count, width), BF16),
                pltpu.VMEM((deep, 4, count, width), BF16),
                pltpu.VMEM((3, deep, count, width), BF16),
                pltpu.VMEM((deep, count, width), BF16),
                pltpu.VMEM((deep - 1, count, width), BF16),
                pltpu.SemaphoreType.DMA((2 * deep + 2,)),
                pltpu.SemaphoreType.DMA((2 * deep + 2,)),
            ]
        scratch += [
            pltpu.VMEM((3, 16, width), F32),
            pltpu.VMEM((deep + 3, 16, width), F32),
            pltpu.SemaphoreType.DMA((deep + 3,)),
            pltpu.SemaphoreType.DMA((deep + 3,)),
            pltpu.VMEM((deep, 4, rows, width), BF16),
            pltpu.SemaphoreType.DMA,
        ]
        options = dict(collective_id=1, has_side_effects=True)
    return pl.pallas_call(
        functools.partial(attend_back_kernel, frames, mesh_shape),
        out_shape=out_shape,
        in_specs=in_specs,
        out_specs=[vmem] * len(out_shape),
        scratch_shapes=scratch,
        compiler_params=pltpu.CompilerParams(vmem_limit_bytes=60 << 20, **options),
        name="attend_back",
    )(*args)


def staged(mesh_shape, windows, cotangent, valid, *owned):
    x, cot = windows[0], cotangent[0]
    bq, bv, bo, bu, bd, gain_one, shift_one, gain_two, shift_two = owned[6:]
    short = [bq, bv, bo, bd, gain_one, shift_one, gain_two, shift_two, bu]
    width = x.shape[1]
    vector = jnp.concatenate(short + [jnp.zeros((width // 2 - 192,), BF16)])[None]
    qa, ka, vt, ht, ot, qe, vectors, first, second = attend(mesh_shape, x, vector, *owned[:6])
    out, dx, da, grads, small = mlp(valid, x, cot, ot, second, vectors)
    dinput, first_own, second_own, small_own = attend_back(
        mesh_shape, x, dx, qa, ka, vt, ht, qe, da, first, vectors, small, grads
    )
    hidden = owned[4].shape[1]
    ups = second_own[16 : 16 + hidden // FF_CHUNK * 16]
    up = ups.reshape(-1, 16, FF_CHUNK).transpose(1, 0, 2).reshape(16, hidden)
    down = second_own[16 + hidden // FF_CHUNK * 16 :]
    line = lambda r: small_own[r, :16]
    return (
        out[None],
        dinput[None],
        first_own[0:16],
        first_own[16:32],
        first_own[32:48],
        second_own[0:16],
        up,
        down,
        line(8),
        line(9),
        line(10),
        small_own[0, :64],
        line(11),
        line(12),
        line(13),
        line(14),
        line(15),
    )


def collective(windows, cotangent, valid, *owned):
    axes = ("batch", "shard")
    wq, wk, wv, wo, wu, wd, bq, bv, bo, bu, bd, gain_one, shift_one, gain_two, shift_two = [
        lax.all_gather(part, axes, axis=0, tiled=True) for part in owned
    ]
    x, cot = windows[0], cotangent[0]
    width, hidden = wu.shape
    blocks, chunks = width // 16, hidden // FF_CHUNK
    split = lambda part: part.reshape(blocks, -1, width)
    vectors = jnp.concatenate(
        [jnp.pad(bu.reshape(chunks, FF_CHUNK), ((0, 8 - chunks), (0, 0)))]
        + [v[None] for v in (bq, bv, bo, bd, gain_one, shift_one, gain_two, shift_two)]
    ).astype(F32)
    first = jnp.concatenate([split(wq), split(wk), split(wv)], axis=1)
    ups = wu.reshape(blocks, 16, chunks, FF_CHUNK).transpose(0, 2, 1, 3)
    ups = ups.reshape(blocks, 16 * chunks, FF_CHUNK)
    second = jnp.concatenate([split(wo), ups, split(wd)], axis=1)
    qa, ka, vt, ht, ot, qe = attend(None, x, first, vectors)
    out, dx, da, grads, small = mlp(valid, x, cot, ot, second, vectors)
    dinput, first_grads, small = attend_back(
        None, x, dx, qa, ka, vt, ht, qe, da, first, vectors, small, None
    )
    first_grads, grads = first_grads.astype(F32), grads.astype(F32)
    joined = lambda part: part.reshape(-1, width)
    gwu = grads[:, 16 : 16 + 16 * chunks].reshape(blocks, chunks, 16, FF_CHUNK)
    gwu = gwu.transpose(0, 2, 1, 3).reshape(width, hidden)
    totals = (
        joined(first_grads[:, 0:16]),
        joined(first_grads[:, 16:32]),
        joined(first_grads[:, 32:48]),
        joined(grads[:, 0:16]),
        gwu,
        joined(grads[:, 16 + 16 * chunks :]),
        small[8],
        small[9],
        small[10],
        small[:chunks].reshape(hidden),
        small[11],
        small[12],
        small[13],
        small[14],
        small[15],
    )
    grads = [lax.psum_scatter(total, axes, scatter_dimension=0, tiled=True) for total in totals]
    return (out[None], dinput[None], *grads)


def solution(mesh):
    both = ("batch", "shard")
    windows_spec, matrix_spec, vector_spec = P(both, None, None), P(both, None), P(both)
    params = (matrix_spec,) * 6 + (vector_spec,) * 9
    mesh_shape = (mesh.shape["batch"], mesh.shape["shard"])

    def per_device(windows, cotangent, valid, *owned):
        if mesh_shape[1] == 4 and mesh_shape[0] % 2 == 0 and owned[0].shape[0] == 16:
            return staged(mesh_shape, windows, cotangent, valid, *owned)
        return collective(windows, cotangent, valid, *owned)

    return jax.shard_map(
        per_device,
        mesh=mesh,
        in_specs=(windows_spec, windows_spec, vector_spec) + params,
        out_specs=(windows_spec, windows_spec) + params,
        check_vma=False,
    )
```

```python
import functools
import math

import jax
import jax.numpy as jnp
from jax import lax
from jax.experimental import pallas as pl
from jax.experimental.pallas import tpu as pltpu
from jax.sharding import PartitionSpec as P

HEADS = 8
NORM_EPS = 1e-05
LOG2E = math.log2(math.e)
LN2 = math.log(2.0)
F32 = jnp.float32
BF16 = jnp.bfloat16
MESH = pl.DeviceIdType.MESH
ROWS = 256
MLP_ROWS = 512
QUERIES = 768
FF_CHUNK = 512
MASKED = -1e30

NN = (((1,), (0,)), ((), ()))
NT = (((1,), (1,)), ((), ()))
TN = (((0,), (0,)), ((), ()))

TAIL_RATE = 0.2625
TAIL = (
    0.10474836168174968,
    0.10416468281706748,
    0.10263486984927783,
    0.056568077030165455,
    0.14744499390073365,
    -0.13092736820325213,
    0.23259357413631826,
    -0.14775373854130247,
    0.03052653723595064,
)


def dot(left, right, dims):
    return lax.dot_general(left, right, dims, preferred_element_type=F32)


def normalize(values):
    centred = values - jnp.mean(values, axis=-1, keepdims=True)
    variance = jnp.mean(centred * centred, axis=-1, keepdims=True)
    inv_std = lax.rsqrt(variance + NORM_EPS)
    return centred * inv_std, inv_std


def normalize_back(grad_rows, unit_rows, inv_std, gain):
    scaled = grad_rows * gain
    first_mean = jnp.mean(scaled, axis=-1, keepdims=True)
    second_mean = jnp.mean(scaled * unit_rows, axis=-1, keepdims=True)
    return inv_std * (scaled - first_mean - unit_rows * second_mean)


def store_rows(ref, start, rows):
    count, width = rows.shape
    parts = width // 128
    for j in range(parts):
        ref[pl.ds(start * parts + j, count, stride=parts), :] = rows[:, j * 128 : (j + 1) * 128]


def column_sums(rows):
    return jnp.sum(rows, axis=0, keepdims=True)


def in_three(values):
    high = values.astype(BF16).astype(F32)
    rest = values - high
    middle = rest.astype(BF16).astype(F32)
    return high, middle, rest - middle


def gelu_and_slope(z):
    size = jnp.abs(z)
    t = 1.0 / (1.0 + TAIL_RATE * size)
    poly = jnp.full_like(t, TAIL[-1])
    for coefficient in TAIL[-2::-1]:
        poly = poly * t + coefficient
    bell = jnp.exp2(z * z * (-0.5 * LOG2E))
    tail = poly * t * bell
    cdf = jnp.where(z > 0, 1.0 - tail, tail)
    return z * cdf, cdf + z * bell * (1.0 / math.sqrt(2.0 * math.pi))


def key_extra(head, keys, frames):
    row = lax.broadcasted_iota(jnp.int32, (keys, 128), 0)
    lane = lax.broadcasted_iota(jnp.int32, (keys, 128), 1) - head * 16
    mask = jnp.where(row < frames, 0.0, MASKED)
    ones = jnp.where((lane > 0) & (lane < 4), 1.0, 0.0)
    return jnp.where(lane == 0, mask, ones).astype(BF16)


class Place:
    def __init__(self, mesh_shape):
        self.batch, self.shard = mesh_shape
        self.deep = self.batch // 2
        b, s = lax.axis_index("batch"), lax.axis_index("shard")
        self.z, self.x, self.y, self.core = b // 2, b % 2, s // 2, s % 2
        self.me = b * self.shard + s
        self.square = self.x * 2 + self.y

    def moved(self, dz=0, dxy=0, flip=0):
        dx, dy = dxy // 2, dxy % 2
        x = 1 - self.x if dx else self.x
        y = 1 - self.y if dy else self.y
        core = 1 - self.core if flip else self.core
        return (self.z + self.deep + dz) % self.deep * 2 + x, y * 2 + core

    def block(self, dz=0, dxy=0, flip=0):
        b, s = self.moved(-dz, dxy, flip)
        return b * self.shard + s

    def partners(self):
        far = [self.moved(dz=dz) for dz in range(1, self.deep)]
        near = [self.moved(dxy=dxy) for dxy in range(1, 4)]
        return far + near + [self.moved(flip=1)]

    def meet(self):
        barrier = pltpu.get_barrier_semaphore()
        for partner in self.partners():
            pl.semaphore_signal(barrier, inc=1, device_id=partner, device_id_type=MESH)
        pl.semaphore_wait(barrier, self.deep + 3)


class Spread:
    def __init__(self, place, own, table, send_sem, recv_sem):
        self.place, self.own, self.table = place, own, table
        self.send_sem, self.recv_sem = send_sem, recv_sem
        self.started = []

    def copy(self, slot, dz, dxy, device):
        block = self.place.block(dz, dxy)
        here = dz == 0 and dxy == 0
        return pltpu.make_async_remote_copy(
            src_ref=self.own if here else self.table.at[block],
            dst_ref=self.table.at[block],
            send_sem=self.send_sem.at[slot],
            recv_sem=self.recv_sem.at[slot],
            device_id=device,
            device_id_type=MESH,
        )

    def far(self, dz):
        return self.copy(dz - 1, 0, 0, self.place.moved(dz=dz))

    def near(self, dz, dxy):
        slot = self.place.deep - 1 + dz * 3 + dxy - 1
        return self.copy(slot, dz, 0, self.place.moved(dxy=dxy))

    def across(self, dz, dxy):
        slot = self.place.deep * 4 - 1 + dz * 4 + dxy
        return self.copy(slot, dz, dxy, self.place.moved(flip=1))

    def launch(self, copy):
        copy.start()
        self.started.append(copy)

    def begin(self):
        for dz in range(1, self.place.deep):
            self.launch(self.far(dz))
        for dxy in range(1, 4):
            self.launch(self.near(0, dxy))
        self.launch(self.across(0, 0))

    def relay_far(self):
        for dz in range(1, self.place.deep):
            self.far(dz).wait_recv()
            for dxy in range(1, 4):
                self.launch(self.near(dz, dxy))
            self.launch(self.across(dz, 0))

    def relay_near(self):
        for dz in range(self.place.deep):
            for dxy in range(1, 4):
                self.near(dz, dxy).wait_recv()
                self.launch(self.across(dz, dxy))

    def arrive(self):
        for dz in range(self.place.deep):
            for dxy in range(4):
                self.across(dz, dxy).wait_recv()

    def drain(self):
        deep = self.place.deep
        for dz in range(1, deep):
            self.far(dz).wait_send()
        for dz in range(deep):
            for dxy in range(1, 4):
                self.near(dz, dxy).wait_send()
        for dz in range(deep):
            for dxy in range(4):
                self.across(dz, dxy).wait_send()


def spread_small(vectors, long, place, width):
    wide = lambda v: jnp.concatenate(
        [v.astype(F32).reshape(1, -1), jnp.zeros((1, width - v.shape[0]), F32)], axis=1
    )
    short = jnp.concatenate([wide(v) for v in vectors], axis=0)
    short = pltpu.roll(short, place.me * 16, 1)
    long = pltpu.roll(jnp.broadcast_to(wide(long), (8, width)), place.me % 8 * 64, 1)
    line = lax.broadcasted_iota(jnp.int32, (8, width), 0)
    long = jnp.where(line == place.me // 8, long, 0.0)
    return jnp.concatenate([long, short], axis=0).astype(BF16)


def matrix(table, first, count=16):
    part = table[:, first : first + count, :]
    return part.reshape(part.shape[0] * count, part.shape[2])


def attend_kernel(frames, mesh_shape, *refs):
    if mesh_shape is None:
        x_ref, table, small_ref = refs[:3]
        qa_ref, ka_ref, vt_ref, ht_ref, ot_ref, qe_ref = refs[3:9]
        xs, scores, peaks, key_ext, log_rows = refs[9:]
    else:
        x_ref, wq_own, wk_own, wv_own, wo_own, wu_own, wd_own = refs[:7]
        short_own = refs[7:16]
        qa_ref, ka_ref, vt_ref, ht_ref, ot_ref, qe_ref, small_ref, first_ref, second_ref = refs[
            16:25
        ]
        xs, scores, peaks, key_ext, log_rows, table, own, send_1, recv_1, send_2, recv_2, keep = (
            refs[25:]
        )
        place = Place(mesh_shape)
        first = Spread(place, table.at[place.me], table, send_1, recv_1)
        second = Spread(place, own, second_ref, send_2, recv_2)
        table[place.me, 0:16, :] = wq_own[...]
        table[place.me, 16:32, :] = wk_own[...]
        table[place.me, 32:48, :] = wv_own[...]
        table[place.me, 48:64, :] = spread_small(
            [ref[...] for ref in short_own[:8]], short_own[8][...], place, x_ref.shape[1]
        )
        own[0:16, :] = wo_own[...]
        chunks = wu_own.shape[1] // FF_CHUNK
        for j in range(chunks):
            own[16 + 16 * j : 32 + 16 * j, :] = wu_own[:, j * FF_CHUNK : (j + 1) * FF_CHUNK]
        own[16 + 16 * chunks :, :] = wd_own[...]
        place.meet()
        first.begin()
        first.relay_far()
        first.relay_near()
        second.begin()
        keep_own = pltpu.make_async_copy(own, second_ref.at[place.me], keep.at[0])
        keep_own.start()

    padded, width = xs.shape
    depth = width // HEADS
    xs[pl.ds(0, frames), :] = x_ref[...]
    xs[pl.ds(frames, padded - frames), :] = jnp.zeros((padded - frames, width), BF16)
    if mesh_shape is not None:
        first.arrive()
        keep_first = pltpu.make_async_copy(table, first_ref, keep.at[1])
        keep_first.start()
        small_ref[...] = jnp.sum(table[:, 48:64, :].astype(F32), axis=0)
    bq, bv, gain, shift = (small_ref[r : r + 1, :] for r in (8, 9, 12, 13))

    def project(i, carry):
        rows = pl.ds(pl.multiple_of(i * ROWS, ROWS), ROWS)
        unit, _ = normalize(xs[rows, :].astype(F32))
        h1 = (unit * gain + shift).astype(BF16)
        ht_ref[:, rows] = h1.T
        q = (dot(h1, matrix(table, 0), NN) + bq).astype(BF16)
        k = dot(h1, matrix(table, 16), NN).astype(BF16).astype(F32)
        k = k * (LOG2E / math.sqrt(depth))
        v = (dot(h1, matrix(table, 32), NN) + bv).astype(BF16)
        k_high = k.astype(BF16)
        k_low = (k - k_high.astype(F32)).astype(BF16)
        vt_ref[:, rows] = v.T
        for h in range(HEADS):
            cols = slice(h * depth, (h + 1) * depth)
            qa_ref[h, rows, :] = jnp.concatenate([q[:, cols], q[:, cols]], axis=1)
            ka_ref[h, rows, :] = jnp.concatenate([k_high[:, cols], k_low[:, cols]], axis=1)
        return carry

    lax.fori_loop(0, padded // ROWS, project, 0)

    blocks = padded // QUERIES
    steps = HEADS * blocks
    lane = lax.broadcasted_iota(jnp.int32, (QUERIES, 128), 1)
    query_ext = jnp.where(lane % 16 == 0, 1.0, 0.0).astype(BF16)

    def score(step, slot):
        head = step // blocks
        rows = pl.ds(pl.multiple_of((step % blocks) * QUERIES, QUERIES), QUERIES)
        key_ext[slot] = key_extra(head, padded, frames)
        left = jnp.concatenate([ka_ref[head], key_ext[slot]], axis=1)
        right = jnp.concatenate([qa_ref[head, rows, :], query_ext], axis=1)
        s = dot(left, right, NT)
        scores[slot] = s
        peaks[slot] = jnp.max(s, axis=0, keepdims=True)

    def finish(step, slot):
        head = step // blocks
        cols = pl.ds(pl.multiple_of((step % blocks) * QUERIES, QUERIES), QUERIES)
        peak = peaks[slot]
        weights = jnp.exp2(scores[slot] - peak).astype(BF16)
        rows = pl.ds(pl.multiple_of(head * depth, depth), depth)
        ones = jnp.ones((16, padded), BF16)
        mixed = dot(jnp.concatenate([vt_ref[rows, :], ones], axis=0), weights, NN)
        total = mixed[depth : depth + 1, :]
        ot_ref[rows, cols] = (mixed[:depth, :] * (1.0 / total)).astype(BF16)
        log_rows[head, :, cols] = peak + jnp.log2(total)

    score(0, 0)

    def pair(i, carry):
        if mesh_shape is not None:
            pl.when(i == 1)(second.relay_far)
            pl.when(i == 5)(second.relay_near)
        score(i * 2 + 1, 1)
        finish(i * 2, 0)
        score(jnp.minimum(i * 2 + 2, steps - 1), 0)
        finish(i * 2 + 1, 1)
        return carry

    lax.fori_loop(0, steps // 2, pair, 0)

    def extend(i, carry):
        rows = pl.ds(pl.multiple_of(i * ROWS, ROWS), ROWS)
        pieces = []
        for h in range(HEADS):
            high, middle, low = in_three(-log_rows[h, :, rows])
            pieces += [jnp.ones((1, ROWS), F32), high, middle, low, jnp.zeros((12, ROWS), F32)]
        qe_ref[rows, :] = jnp.concatenate(pieces, axis=0).T.astype(BF16)
        return carry

    lax.fori_loop(0, padded // ROWS, extend, 0)
    if mesh_shape is not None:
        second.arrive()
        keep_own.wait()
        keep_first.wait()
        first.drain()
        second.drain()


def attend(mesh_shape, x, *rest):
    frames, width = x.shape
    padded = -(-frames // QUERIES) * QUERIES
    blocks = width // 16
    vmem = pl.BlockSpec(memory_space=pltpu.VMEM)
    anywhere = pl.BlockSpec(memory_space=pl.ANY)
    out_shape = [
        jax.ShapeDtypeStruct((HEADS, padded, 128), BF16),
        jax.ShapeDtypeStruct((HEADS, padded, 128), BF16),
        jax.ShapeDtypeStruct((width, padded), BF16),
        jax.ShapeDtypeStruct((width, padded), BF16),
        jax.ShapeDtypeStruct((width, padded), BF16),
        jax.ShapeDtypeStruct((padded, 128), BF16),
    ]
    scratch = [
        pltpu.VMEM((padded, width), BF16),
        pltpu.VMEM((2, padded, QUERIES), F32),
        pltpu.VMEM((2, 1, QUERIES), F32),
        pltpu.VMEM((2, padded, 128), BF16),
        pltpu.VMEM((HEADS, 1, padded), F32),
    ]
    out_specs = [vmem] * 6
    options = {}
    if mesh_shape is not None:
        hidden = rest[4].shape[1]
        own_rows = 16 + hidden // FF_CHUNK * 16 + rest[5].shape[0]
        out_shape += [
            jax.ShapeDtypeStruct((16, width), F32),
            jax.ShapeDtypeStruct((blocks, 64, width), BF16),
            jax.ShapeDtypeStruct((blocks, own_rows, width), BF16),
        ]
        out_specs += [vmem, anywhere, anywhere]
        scratch += [
            pltpu.VMEM((blocks, 64, width), BF16),
            pltpu.VMEM((own_rows, width), BF16),
        ]
        scratch += [pltpu.SemaphoreType.DMA((blocks - 1,)) for _ in range(4)]
        scratch += [pltpu.SemaphoreType.DMA((2,))]
        options = dict(collective_id=0, has_side_effects=True)
    return pl.pallas_call(
        functools.partial(attend_kernel, frames, mesh_shape),
        out_shape=out_shape,
        in_specs=[vmem] * (1 + len(rest)),
        out_specs=out_specs,
        scratch_shapes=scratch,
        compiler_params=pltpu.CompilerParams(vmem_limit_bytes=60 << 20, **options),
        name="attend",
    )(x, *rest)


def mlp_kernel(
    frames,
    flag_ref,
    x_ref,
    cot_ref,
    ot_ref,
    table,
    vec_ref,
    out_ref,
    dx_ref,
    do_ref,
    de_ref,
    grads_ref,
    small_ref,
    gwo,
    gwu,
    gwd,
):
    step = pl.program_id(0)
    rows, width = x_ref.shape
    chunks = gwu.shape[0]
    depth = width // HEADS
    down = table.shape[1] - 16 - 16 * chunks
    per_chunk = FF_CHUNK // down

    def up_part(j):
        return matrix(table, 16 + 16 * j)

    def down_part(j):
        part = table[j * per_chunk : (j + 1) * per_chunk, 16 + 16 * chunks :, :]
        return part.reshape(FF_CHUNK, width)

    @pl.when(step == 0)
    def _():
        gwo[...] = jnp.zeros_like(gwo)
        gwu[...] = jnp.zeros_like(gwu)
        gwd[...] = jnp.zeros_like(gwd)
        small_ref[...] = jnp.zeros_like(small_ref)

    flag = flag_ref[0].astype(F32)
    inside = step * rows + lax.broadcasted_iota(jnp.int32, (rows, width), 0) < frames
    x = jnp.where(inside, x_ref[...].astype(F32), 0.0)
    dy = jnp.where(inside, cot_ref[...].astype(F32), 0.0) * flag
    dy_low = dy.astype(BF16)
    bo, bd, gain, shift = (vec_ref[r : r + 1, :] for r in (10, 11, 14, 15))
    wo = matrix(table, 0)
    ot = ot_ref[...]
    o = ot.T
    x1 = x + (dot(o, wo, NN) + bo)
    unit, inv_std = normalize(x1)
    h2 = (unit * gain + shift).astype(BF16)
    h2t = h2.T
    z_next = dot(h2, up_part(0), NN)
    out = x1 + bd
    dh2 = jnp.zeros((rows, width), F32)
    for j in range(chunks):
        z = z_next + vec_ref[j : j + 1, :]
        if j + 1 < chunks:
            z_next = dot(h2, up_part(j + 1), NN)
        dg = dot(dy_low, down_part(j), NT)
        g, slope = gelu_and_slope(z)
        g = g.astype(BF16)
        dz = (dg * slope).astype(BF16)
        out = out + dot(g, down_part(j), NN)
        gwd[j] += dot(g, dy_low, TN)
        gwu[j] += dot(h2t, dz, NN)
        small_ref[j : j + 1, :] += column_sums(dz.astype(F32))
        dh2 = dh2 + dot(dz, up_part(j), NT)
    store_rows(out_ref, 0, out * flag)
    dx1 = dy + normalize_back(dh2, unit, inv_std, gain)
    dx_ref[...] = dx1
    da = dx1.astype(BF16)
    gwo[...] += dot(ot, da, NN)
    do = dot(da, wo, NT).astype(BF16)
    small_ref[10:11, :] += column_sums(da.astype(F32))
    small_ref[11:12, :] += column_sums(dy)
    small_ref[14:15, :] += column_sums(dh2 * unit)
    small_ref[15:16, :] += column_sums(dh2)
    do_ref[...] = do
    prod = do.astype(F32) * o.astype(F32)
    high = prod.astype(BF16)
    low = (prod - high.astype(F32)).astype(BF16)
    owner = lax.broadcasted_iota(jnp.int32, (width, 128), 0) // depth
    pick = lax.broadcasted_iota(jnp.int32, (width, 128), 1) // 16
    pick = jnp.where(owner == pick, 1.0, 0.0).astype(BF16)
    high, middle, low = in_three(-(dot(high, pick, NN) + dot(low, pick, NN)))
    lane = lax.broadcasted_iota(jnp.int32, (rows, 128), 1) % 16
    extra = jnp.where(lane == 1, middle, jnp.where(lane == 2, low, 0.0))
    de_ref[...] = jnp.where(lane == 0, high, extra).astype(BF16)

    @pl.when(step == pl.num_programs(0) - 1)
    def _():
        split = lambda part, count: part.astype(BF16).reshape(-1, count, width)
        grads_ref[:, 0:16, :] = split(gwo[...], 16)
        for j in range(chunks):
            grads_ref[:, 16 + 16 * j : 32 + 16 * j, :] = split(gwu[j], 16)
            grads_ref[j * per_chunk : (j + 1) * per_chunk, 16 + 16 * chunks :, :] = split(
                gwd[j], down
            )


def mlp(flag, x, cot, ot, table, vectors):
    frames, width = x.shape
    padded = ot.shape[1]
    blocks, rows = table.shape[:2]
    chunks = (rows - 16) * blocks // (2 * FF_CHUNK)
    by_rows = pl.BlockSpec((MLP_ROWS, width), lambda i: (i, 0))
    fixed = lambda shape: pl.BlockSpec(
        shape, lambda i: (0,) * len(shape), pipeline_mode=pl.Buffered(1)
    )
    return pl.pallas_call(
        functools.partial(mlp_kernel, frames),
        grid=(padded // MLP_ROWS,),
        out_shape=[
            jax.ShapeDtypeStruct((frames * width // 128, 128), F32),
            jax.ShapeDtypeStruct((frames, width), F32),
            jax.ShapeDtypeStruct((padded, width), BF16),
            jax.ShapeDtypeStruct((padded, 128), BF16),
            jax.ShapeDtypeStruct(table.shape, BF16),
            jax.ShapeDtypeStruct((16, width), F32),
        ],
        in_specs=[
            pl.BlockSpec(memory_space=pltpu.SMEM),
            by_rows,
            by_rows,
            pl.BlockSpec((width, MLP_ROWS), lambda i: (0, i)),
            fixed(table.shape),
            fixed((16, width)),
        ],
        out_specs=[
            pl.BlockSpec((MLP_ROWS * width // 128, 128), lambda i: (i, 0)),
            by_rows,
            by_rows,
            pl.BlockSpec((MLP_ROWS, 128), lambda i: (i, 0)),
            fixed(table.shape),
            fixed((16, width)),
        ],
        scratch_shapes=[
            pltpu.VMEM((width, width), F32),
            pltpu.VMEM((chunks, width, FF_CHUNK), F32),
            pltpu.VMEM((chunks, FF_CHUNK, width), F32),
        ],
        compiler_params=pltpu.CompilerParams(
            vmem_limit_bytes=60 << 20, dimension_semantics=("arbitrary",)
        ),
        name="mlp",
    )(flag, x, cot, ot, table, vectors)


class Gather:
    def __init__(self, place, source, from_core, halves, from_near, quarter, from_far, sems):
        self.place, self.source = place, source
        self.from_core, self.halves = from_core, halves
        self.from_near, self.quarter = from_near, quarter
        self.from_far = from_far
        self.send_sem, self.recv_sem = sems

    def copy(self, slot, src, dst, device):
        return pltpu.make_async_remote_copy(
            src_ref=src,
            dst_ref=dst,
            send_sem=self.send_sem.at[slot],
            recv_sem=self.recv_sem.at[slot],
            device_id=device,
            device_id_type=MESH,
        )

    def across(self):
        place = self.place
        return [
            self.copy(
                z, self.source.at[z, :, 1 - place.core], self.from_core.at[z], place.moved(flip=1)
            )
            for z in range(place.deep)
        ]

    def near(self):
        place = self.place
        copies = []
        for dxy in range(1, 4):
            b, s = place.moved(dxy=dxy)
            square = b % 2 * 2 + s // 2
            copies.append(
                self.copy(
                    place.deep + dxy - 1,
                    self.halves.at[:, square],
                    self.from_near.at[dxy - 1],
                    (b, s),
                )
            )
        return copies

    def far(self):
        place = self.place
        copies = []
        for dz in range(1, place.deep):
            z = (place.z + dz) % place.deep
            copies.append(
                self.copy(
                    place.deep + 2 + dz,
                    self.quarter.at[z],
                    self.from_far.at[dz - 1],
                    place.moved(dz=dz),
                )
            )
        return copies

    def fold_across(self, own):
        for copy in self.across():
            copy.wait_recv()

        def one(i, carry):
            z, q = i // 4, i % 4
            total = own(z, q).astype(F32) + self.from_core[z, q].astype(F32)
            self.halves[z, q] = total.astype(BF16)
            return carry

        lax.fori_loop(0, self.place.deep * 4, one, 0)
        for copy in self.near():
            copy.start()

    def fold_near(self):
        for copy in self.near():
            copy.wait_recv()

        def one(z, carry):
            total = self.halves[z, self.place.square].astype(F32)
            for dxy in range(3):
                total = total + self.from_near[dxy, z].astype(F32)
            self.quarter[z] = total.astype(BF16)
            return carry

        lax.fori_loop(0, self.place.deep, one, 0)
        for copy in self.far():
            copy.start()

    def result(self):
        for copy in self.far():
            copy.wait_recv()
        total = self.quarter[self.place.z].astype(F32)
        for dz in range(self.place.deep - 1):
            total = total + self.from_far[dz].astype(F32)
        return total

    def drain(self):
        for copy in self.across() + self.near() + self.far():
            copy.wait_send()


class SmallSum:
    def __init__(self, place, buffers, received, sems):
        self.place, self.buffers, self.received = place, buffers, received
        self.send_sem, self.recv_sem = sems

    def copies(self, stage):
        place = self.place
        if stage == 0:
            devices, first = [place.moved(flip=1)], 0
        elif stage == 1:
            devices, first = [place.moved(dxy=dxy) for dxy in range(1, 4)], 1
        else:
            devices, first = [place.moved(dz=dz) for dz in range(1, place.deep)], 4
        return [
            pltpu.make_async_remote_copy(
                src_ref=self.buffers.at[stage],
                dst_ref=self.received.at[first + i],
                send_sem=self.send_sem.at[first + i],
                recv_sem=self.recv_sem.at[first + i],
                device_id=device,
                device_id_type=MESH,
            )
            for i, device in enumerate(devices)
        ]

    def send(self, stage, value):
        self.buffers[stage] = value
        for copy in self.copies(stage):
            copy.start()

    def receive(self, stage):
        total = self.buffers[stage]
        first = (0, 1, 4)[stage]
        for i, copy in enumerate(self.copies(stage)):
            copy.wait_recv()
            total = total + self.received[first + i]
        return total

    def drain(self):
        for stage in range(3):
            for copy in self.copies(stage):
                copy.wait_send()


def own_small(total, place):
    width = total.shape[1]
    line = lax.broadcasted_iota(jnp.int32, total.shape, 0)
    short = pltpu.roll(total, width - place.me * 16, 1)
    long = jnp.sum(jnp.where(line == place.me // 8, total, 0.0), axis=0, keepdims=True)
    long = pltpu.roll(jnp.broadcast_to(long, total.shape), width - place.me % 8 * 64, 1)
    return jnp.where(line == 0, long, short)[:, :128]


def attend_back_kernel(frames, mesh_shape, *refs):
    x_ref, dx_ref, qa_ref, ka_ref, vt_ref, ht_ref, qe_ref, do_ref, de_ref = refs[:9]
    refs = refs[9:]
    table, vec_ref, small_in = refs[:3]
    if mesh_shape is None:
        dinput_ref, first_source, small_ref = refs[3:6]
        dq, dkt, dvt, sum_k, sum_v, key_ext, value_ext, small = refs[6:]
    else:
        grads_ref = refs[3]
        dinput_ref, gq_ref, gk_ref, gv_ref, go_ref, gu_ref, gd_ref = refs[4:11]
        short_refs = refs[11:20]
        refs = refs[20:]
        dq, dkt, dvt, sum_k, sum_v, key_ext, value_ext, small, first_source = refs[:9]
        refs = refs[9:]
        place = Place(mesh_shape)
        first = Gather(place, first_source, *refs[:5], refs[5:7])
        second = Gather(place, grads_ref, *refs[7:12], refs[12:14])
        shorts = SmallSum(place, refs[14], refs[15], refs[16:18])
        second_half, keep = refs[18:]
        place.meet()
        for copy in second.across():
            copy.start()
        keep_half = pltpu.make_async_copy(grads_ref.at[:, :, place.core], second_half, keep)
        keep_half.start()

    padded = qa_ref.shape[1]
    width = ht_ref.shape[0]
    depth = width // HEADS

    def second_across():
        keep_half.wait()
        second.fold_across(lambda z, q: second_half[z, q])

    def one_head(head, carry):
        if mesh_shape is not None:
            pl.when(head == 1)(second_across)
            pl.when(head == 5)(second.fold_near)
        key_ext[...] = key_extra(head, padded, frames)
        line = lax.broadcasted_iota(jnp.int32, (128, padded), 0)
        mine = pl.ds(pl.multiple_of(head // 2 * 128, 128), 128)
        values = jnp.where(line // depth == head % 2, vt_ref[mine, :].astype(F32), 0.0)
        value_ext[0:128, :] = values.astype(BF16)
        extra = jnp.where((line // 16 == head) & (line % 16 < 3), 1.0, 0.0)
        value_ext[128:256, :] = extra.astype(BF16)
        for i in range(padded // ROWS):
            rows = slice(i * ROWS, (i + 1) * ROWS)
            q = qa_ref[head, rows, :]
            d = do_ref[rows, mine]
            turned = d.T
            turned = jnp.where(head % 2 == 0, turned[:depth], turned[depth:])
            s = dot(
                jnp.concatenate([q, qe_ref[rows, :]], axis=1),
                jnp.concatenate([ka_ref[head], key_ext[...]], axis=1),
                NT,
            )
            p = jnp.exp2(s)
            dp = dot(jnp.concatenate([d, de_ref[rows, :]], axis=1), value_ext[...], NN)
            ds = (p * dp).astype(BF16)
            p = p.astype(BF16)
            new_v = dot(turned, p, NN)
            new_k = dot(q[:, :depth], ds, TN)
            if i == 0:
                sum_v[...] = new_v
                sum_k[...] = new_k
            else:
                sum_v[...] += new_v
                sum_k[...] += new_k
            both = dot(ds, ka_ref[head], NN)
            both = both + pltpu.roll(both, depth, 1)
            dq[head, rows, :] = (both * LN2).astype(BF16)
        out_rows = pl.ds(pl.multiple_of(head * depth, depth), depth)
        dkt[out_rows, :] = (sum_k[...] * (1.0 / math.sqrt(depth))).astype(BF16)
        dvt[out_rows, :] = sum_v[...].astype(BF16)
        return carry

    lax.fori_loop(0, HEADS, one_head, 0)

    half = lax.broadcasted_iota(jnp.int32, (padded, 128), 1) < depth

    def keep_grad(first_row, cols, value):
        shape = first_source.shape[:-2] + (16, value.shape[1])
        index = (slice(None),) * (len(shape) - 2)
        first_source[index + (slice(first_row, first_row + 16), cols)] = value.astype(BF16).reshape(
            shape
        )

    for h in range(0, HEADS, 2):
        both = jnp.where(half, dq[h], dq[h + 1])
        keep_grad(0, slice(h * depth, (h + 2) * depth), dot(ht_ref[...], both, NN))
    keep_grad(16, slice(0, width), dot(ht_ref[...], dkt[...], NT))
    keep_grad(32, slice(0, width), dot(ht_ref[...], dvt[...], NT))
    if mesh_shape is not None:
        for copy in first.across():
            copy.start()
        second_own = second.result()
        chunks = gu_ref.shape[1] // FF_CHUNK
        go_ref[...] = second_own[0:16]
        for j in range(chunks):
            gu_ref[:, j * FF_CHUNK : (j + 1) * FF_CHUNK] = second_own[16 + 16 * j : 32 + 16 * j]
        gd_ref[...] = second_own[16 + 16 * chunks :]

    gain = vec_ref[12:13, :]
    small[...] = small_in[...]
    for index, start in enumerate(range(0, frames, ROWS)):
        if mesh_shape is not None and index == 2:
            first.fold_across(lambda z, q: first_source[z, q, place.core])
        count = min(ROWS, frames - start)
        rows = slice(start, start + count)
        wide = slice(start, start + ROWS)
        some = half[:ROWS]
        dq_rows = jnp.concatenate(
            [jnp.where(some, dq[h, wide, :], dq[h + 1, wide, :]) for h in range(0, HEADS, 2)],
            axis=1,
        )
        dk_rows = dkt[:, wide].T
        dv_rows = dvt[:, wide].T
        dh1 = (
            dot(dq_rows, matrix(table, 0), NT)
            + dot(dk_rows, matrix(table, 16), NT)
            + dot(dv_rows, matrix(table, 32), NT)
        )
        small[8:9, :] += column_sums(dq_rows.astype(F32))
        small[9:10, :] += column_sums(dv_rows.astype(F32))
        dh1 = dh1[:count]
        unit, inv_std = normalize(x_ref[rows, :].astype(F32))
        small[12:13, :] += column_sums(dh1 * unit)
        small[13:14, :] += column_sums(dh1)
        dinput = dx_ref[rows, :] + normalize_back(dh1, unit, inv_std, gain)
        store_rows(dinput_ref, start, dinput)
    if mesh_shape is None:
        small_ref[...] = small[...]
    else:
        shorts.send(0, small[...])
        first.fold_near()
        shorts.send(1, shorts.receive(0))
        shorts.send(2, shorts.receive(1))
        first_own = first.result()
        for i, ref in enumerate((gq_ref, gk_ref, gv_ref)):
            ref[...] = first_own[16 * i : 16 * i + 16]
        small_own = own_small(shorts.receive(2), place)
        for i, ref in enumerate(short_refs[:8]):
            ref[...] = small_own[8 + i, :16]
        short_refs[8][...] = small_own[0, :64]
        second.drain()
        first.drain()
        shorts.drain()


def attend_back(mesh_shape, x, dx, qa, ka, vt, ht, qe, do, de, table, vectors, small, grads):
    frames, width = x.shape
    padded = ht.shape[1]
    blocks = width // 16
    vmem = pl.BlockSpec(memory_space=pltpu.VMEM)
    args = [x, dx, qa, ka, vt, ht, qe, do, de, table, vectors, small]
    in_specs = [vmem] * len(args)
    out_shape = [jax.ShapeDtypeStruct((frames * width // 128, 128), F32)]
    scratch = [
        pltpu.VMEM((HEADS, padded, 128), BF16),
        pltpu.VMEM((width, padded), BF16),
        pltpu.VMEM((width, padded), BF16),
        pltpu.VMEM((width // HEADS, padded), F32),
        pltpu.VMEM((width // HEADS, padded), F32),
        pltpu.VMEM((padded, 128), BF16),
        pltpu.VMEM((256, padded), BF16),
        pltpu.VMEM((16, width), F32),
    ]
    options = {}
    if mesh_shape is None:
        out_shape += [
            jax.ShapeDtypeStruct((blocks, 48, width), BF16),
            jax.ShapeDtypeStruct((16, width), F32),
        ]
    else:
        deep = mesh_shape[0] // 2
        rows = grads.shape[1]
        hidden = (rows - 16) * blocks // 2
        args.append(grads.reshape(deep, 4, 2, rows, width))
        in_specs.append(pl.BlockSpec(memory_space=pl.ANY))
        out_shape += [
            jax.ShapeDtypeStruct((16, width), F32),
            jax.ShapeDtypeStruct((16, width), F32),
            jax.ShapeDtypeStruct((16, width), F32),
            jax.ShapeDtypeStruct((16, width), F32),
            jax.ShapeDtypeStruct((16, hidden), F32),
            jax.ShapeDtypeStruct((hidden // blocks, width), F32),
        ]
        out_shape += [jax.ShapeDtypeStruct((16,), F32)] * 8
        out_shape += [jax.ShapeDtypeStruct((hidden // blocks,), F32)]
        scratch.append(pltpu.VMEM((deep, 4, 2, 48, width), BF16))
        for count in (48, rows):
            scratch += [
                pltpu.VMEM((deep, 4, count, width), BF16),
                pltpu.VMEM((deep, 4, count, width), BF16),
                pltpu.VMEM((3, deep, count, width), BF16),
                pltpu.VMEM((deep, count, width), BF16),
                pltpu.VMEM((deep - 1, count, width), BF16),
                pltpu.SemaphoreType.DMA((2 * deep + 2,)),
                pltpu.SemaphoreType.DMA((2 * deep + 2,)),
            ]
        scratch += [
            pltpu.VMEM((3, 16, width), F32),
            pltpu.VMEM((deep + 3, 16, width), F32),
            pltpu.SemaphoreType.DMA((deep + 3,)),
            pltpu.SemaphoreType.DMA((deep + 3,)),
            pltpu.VMEM((deep, 4, rows, width), BF16),
            pltpu.SemaphoreType.DMA,
        ]
        options = dict(collective_id=1, has_side_effects=True)
    return pl.pallas_call(
        functools.partial(attend_back_kernel, frames, mesh_shape),
        out_shape=out_shape,
        in_specs=in_specs,
        out_specs=[vmem] * len(out_shape),
        scratch_shapes=scratch,
        compiler_params=pltpu.CompilerParams(vmem_limit_bytes=60 << 20, **options),
        name="attend_back",
    )(*args)


def hand_over_kernel(count, *refs):
    large, small = refs[0], refs[1 : count + 1]
    large_buf, small_buf = refs[2 * count + 2], refs[2 * count + 3 : 3 * count + 3]
    large_out, small_out = refs[count + 1], refs[count + 2 : 2 * count + 2]
    sem_in, sem_out = refs[3 * count + 3 :]
    pieces = large_buf.shape[0]
    rows = large_buf.shape[1]
    sources = [large.at[pl.ds(i * rows, rows)] for i in range(pieces)] + list(small)
    buffers = [large_buf.at[i] for i in range(pieces)] + list(small_buf)
    targets = [large_out.at[pl.ds(i * rows, rows)] for i in range(pieces)] + list(small_out)
    inward = [
        pltpu.make_async_copy(source, buffer, sem_in.at[i])
        for i, (source, buffer) in enumerate(zip(sources, buffers))
    ]
    outward = [
        pltpu.make_async_copy(buffer, target, sem_out.at[i])
        for i, (buffer, target) in enumerate(zip(buffers, targets))
    ]
    for copy in inward:
        copy.start()
    for first, then in zip(inward, outward):
        first.wait()
        then.start()
    for copy in outward:
        copy.wait()


def hand_over(large, *small):
    anywhere = pl.BlockSpec(memory_space=pltpu.HBM)
    arrays = (large,) + small
    rows = large.shape[0]
    pieces = 6 if rows % 48 == 0 else 1
    return pl.pallas_call(
        functools.partial(hand_over_kernel, len(small)),
        out_shape=[jax.ShapeDtypeStruct(array.shape, array.dtype) for array in arrays],
        in_specs=[anywhere] * len(arrays),
        out_specs=[anywhere] * len(arrays),
        scratch_shapes=[pltpu.VMEM((pieces, rows // pieces) + large.shape[1:], large.dtype)]
        + [pltpu.VMEM(array.shape, array.dtype) for array in small]
        + [pltpu.SemaphoreType.DMA((len(small) + pieces,))] * 2,
        compiler_params=pltpu.CompilerParams(vmem_limit_bytes=60 << 20),
        name="hand_over",
    )(*arrays)


def staged(mesh_shape, windows, cotangent, valid, *owned):
    x, cot = windows[0], cotangent[0]
    bq, bv, bo, bu, bd, gain_one, shift_one, gain_two, shift_two = owned[6:]
    short = [bq, bv, bo, bd, gain_one, shift_one, gain_two, shift_two, bu]
    qa, ka, vt, ht, ot, qe, vectors, first, second = attend(mesh_shape, x, *owned[:6], *short)
    out, dx, do, de, grads, small = mlp(valid, x, cot, ot, second, vectors)
    results = attend_back(
        mesh_shape, x, dx, qa, ka, vt, ht, qe, do, de, first, vectors, small, grads
    )
    dinput, gq, gk, gv, go, gu, gd, *shorts = hand_over(*results)
    gbq, gbv, gbo, gbd, *gains, gbu = shorts
    return (
        out.reshape(windows.shape),
        dinput.reshape(windows.shape),
        *(gq, gk, gv, go, gu, gd, gbq, gbv, gbo, gbu, gbd),
        *gains,
    )


def collective(windows, cotangent, valid, *owned):
    axes = ("batch", "shard")
    wq, wk, wv, wo, wu, wd, bq, bv, bo, bu, bd, gain_one, shift_one, gain_two, shift_two = [
        lax.all_gather(part, axes, axis=0, tiled=True) for part in owned
    ]
    x, cot = windows[0], cotangent[0]
    width, hidden = wu.shape
    blocks, chunks = width // 16, hidden // FF_CHUNK
    split = lambda part: part.reshape(blocks, -1, width)
    vectors = jnp.concatenate(
        [jnp.pad(bu.reshape(chunks, FF_CHUNK), ((0, 8 - chunks), (0, 0)))]
        + [v[None] for v in (bq, bv, bo, bd, gain_one, shift_one, gain_two, shift_two)]
    ).astype(F32)
    first = jnp.concatenate([split(wq), split(wk), split(wv)], axis=1)
    ups = wu.reshape(blocks, 16, chunks, FF_CHUNK).transpose(0, 2, 1, 3)
    ups = ups.reshape(blocks, 16 * chunks, FF_CHUNK)
    second = jnp.concatenate([split(wo), ups, split(wd)], axis=1)
    qa, ka, vt, ht, ot, qe = attend(None, x, first, vectors)
    out, dx, do, de, grads, small = mlp(valid, x, cot, ot, second, vectors)
    dinput, first_grads, small = attend_back(
        None, x, dx, qa, ka, vt, ht, qe, do, de, first, vectors, small, None
    )
    first_grads, grads = first_grads.astype(F32), grads.astype(F32)
    joined = lambda part: part.reshape(-1, width)
    gwu = grads[:, 16 : 16 + 16 * chunks].reshape(blocks, chunks, 16, FF_CHUNK)
    gwu = gwu.transpose(0, 2, 1, 3).reshape(width, hidden)
    totals = (
        joined(first_grads[:, 0:16]),
        joined(first_grads[:, 16:32]),
        joined(first_grads[:, 32:48]),
        joined(grads[:, 0:16]),
        gwu,
        joined(grads[:, 16 + 16 * chunks :]),
        small[8],
        small[9],
        small[10],
        small[:chunks].reshape(hidden),
        small[11],
        small[12],
        small[13],
        small[14],
        small[15],
    )
    grads = [lax.psum_scatter(total, axes, scatter_dimension=0, tiled=True) for total in totals]
    return (out.reshape(windows.shape), dinput.reshape(windows.shape), *grads)


def solution(mesh):
    both = ("batch", "shard")
    windows_spec, matrix_spec, vector_spec = P(both, None, None), P(both, None), P(both)
    params = (matrix_spec,) * 6 + (vector_spec,) * 9
    mesh_shape = (mesh.shape["batch"], mesh.shape["shard"])

    def per_device(windows, cotangent, valid, *owned):
        if mesh_shape[1] == 4 and mesh_shape[0] % 2 == 0 and owned[0].shape[0] == 16:
            return staged(mesh_shape, windows, cotangent, valid, *owned)
        return collective(windows, cotangent, valid, *owned)

    return jax.shard_map(
        per_device,
        mesh=mesh,
        in_specs=(windows_spec, windows_spec, vector_spec) + params,
        out_specs=(windows_spec, windows_spec) + params,
        check_vma=False,
    )
```

```python
import functools
import math

import jax
import jax.numpy as jnp
from jax import lax
from jax.experimental import pallas as pl
from jax.experimental.pallas import tpu as pltpu
from jax.sharding import PartitionSpec as P

HEADS = 8
NORM_EPS = 1e-05
LOG2E = math.log2(math.e)
LN2 = math.log(2.0)
F32 = jnp.float32
BF16 = jnp.bfloat16
MESH = pl.DeviceIdType.MESH
ROWS = 256
MLP_ROWS = 512
FAR_AT = 0
NEAR_AT = 7
FOLD_AT = 2
QUERIES = 768
FF_CHUNK = 512
MASKED = -1e30

NN = (((1,), (0,)), ((), ()))
NT = (((1,), (1,)), ((), ()))
TN = (((0,), (0,)), ((), ()))

TAIL_RATE = 0.2625
TAIL = (
    0.10474836168174968,
    0.10416468281706748,
    0.10263486984927783,
    0.056568077030165455,
    0.14744499390073365,
    -0.13092736820325213,
    0.23259357413631826,
    -0.14775373854130247,
    0.03052653723595064,
)


def dot(left, right, dims):
    return lax.dot_general(left, right, dims, preferred_element_type=F32)


def normalize(values):
    centred = values - jnp.mean(values, axis=-1, keepdims=True)
    variance = jnp.mean(centred * centred, axis=-1, keepdims=True)
    inv_std = lax.rsqrt(variance + NORM_EPS)
    return centred * inv_std, inv_std


def normalize_back(grad_rows, unit_rows, inv_std, gain):
    scaled = grad_rows * gain
    first_mean = jnp.mean(scaled, axis=-1, keepdims=True)
    second_mean = jnp.mean(scaled * unit_rows, axis=-1, keepdims=True)
    return inv_std * (scaled - first_mean - unit_rows * second_mean)


def store_rows(ref, start, rows):
    count, width = rows.shape
    parts = width // 128
    for j in range(parts):
        ref[pl.ds(start * parts + j, count, stride=parts), :] = rows[:, j * 128 : (j + 1) * 128]


def column_sums(rows):
    return jnp.sum(rows, axis=0, keepdims=True)


def in_three(values):
    high = values.astype(BF16).astype(F32)
    rest = values - high
    middle = rest.astype(BF16).astype(F32)
    return high, middle, rest - middle


def gelu_and_slope(z):
    size = jnp.abs(z)
    t = 1.0 / (1.0 + TAIL_RATE * size)
    poly = jnp.full_like(t, TAIL[-1])
    for coefficient in TAIL[-2::-1]:
        poly = poly * t + coefficient
    bell = jnp.exp2(z * z * (-0.5 * LOG2E))
    tail = poly * t * bell
    cdf = jnp.where(z > 0, 1.0 - tail, tail)
    return z * cdf, cdf + z * bell * (1.0 / math.sqrt(2.0 * math.pi))


def key_extra(head, keys, frames):
    row = lax.broadcasted_iota(jnp.int32, (keys, 128), 0)
    lane = lax.broadcasted_iota(jnp.int32, (keys, 128), 1) - head * 16
    mask = jnp.where(row < frames, 0.0, MASKED)
    ones = jnp.where((lane > 0) & (lane < 4), 1.0, 0.0)
    return jnp.where(lane == 0, mask, ones).astype(BF16)


class Place:
    def __init__(self, mesh_shape):
        self.batch, self.shard = mesh_shape
        self.deep = self.batch // 2
        b, s = lax.axis_index("batch"), lax.axis_index("shard")
        self.z, self.x, self.y, self.core = b // 2, b % 2, s // 2, s % 2
        self.me = b * self.shard + s
        self.square = self.x * 2 + self.y

    def moved(self, dz=0, dxy=0, flip=0):
        dx, dy = dxy // 2, dxy % 2
        x = 1 - self.x if dx else self.x
        y = 1 - self.y if dy else self.y
        core = 1 - self.core if flip else self.core
        return (self.z + self.deep + dz) % self.deep * 2 + x, y * 2 + core

    def block(self, dz=0, dxy=0, flip=0):
        b, s = self.moved(-dz, dxy, flip)
        return b * self.shard + s

    def partners(self):
        far = [self.moved(dz=dz) for dz in range(1, self.deep)]
        near = [self.moved(dxy=dxy) for dxy in range(1, 4)]
        return far + near + [self.moved(flip=1)]

    def greet(self):
        barrier = pltpu.get_barrier_semaphore()
        for partner in self.partners():
            pl.semaphore_signal(barrier, inc=1, device_id=partner, device_id_type=MESH)

    def meet(self):
        pl.semaphore_wait(pltpu.get_barrier_semaphore(), self.deep + 3)


class Spread:
    def __init__(self, place, own, table, send_sem, recv_sem):
        self.place, self.own, self.table = place, own, table
        self.send_sem, self.recv_sem = send_sem, recv_sem
        self.started = []

    def copy(self, slot, dz, dxy, device):
        block = self.place.block(dz, dxy)
        here = dz == 0 and dxy == 0
        return pltpu.make_async_remote_copy(
            src_ref=self.own if here else self.table.at[block],
            dst_ref=self.table.at[block],
            send_sem=self.send_sem.at[slot],
            recv_sem=self.recv_sem.at[slot],
            device_id=device,
            device_id_type=MESH,
        )

    def far(self, dz):
        return self.copy(dz - 1, 0, 0, self.place.moved(dz=dz))

    def near(self, dz, dxy):
        slot = self.place.deep - 1 + dz * 3 + dxy - 1
        return self.copy(slot, dz, 0, self.place.moved(dxy=dxy))

    def across(self, dz, dxy):
        slot = self.place.deep * 4 - 1 + dz * 4 + dxy
        return self.copy(slot, dz, dxy, self.place.moved(flip=1))

    def launch(self, copy):
        copy.start()
        self.started.append(copy)

    def begin(self):
        for dz in range(1, self.place.deep):
            self.launch(self.far(dz))
        for dxy in range(1, 4):
            self.launch(self.near(0, dxy))
        self.launch(self.across(0, 0))

    def relay_far(self):
        for dz in range(1, self.place.deep):
            self.far(dz).wait_recv()
            for dxy in range(1, 4):
                self.launch(self.near(dz, dxy))
            self.launch(self.across(dz, 0))

    def relay_near(self):
        for dz in range(self.place.deep):
            for dxy in range(1, 4):
                self.near(dz, dxy).wait_recv()
                self.launch(self.across(dz, dxy))

    def arrive(self):
        for dz in range(self.place.deep):
            for dxy in range(4):
                self.across(dz, dxy).wait_recv()

    def drain(self):
        deep = self.place.deep
        for dz in range(1, deep):
            self.far(dz).wait_send()
        for dz in range(deep):
            for dxy in range(1, 4):
                self.near(dz, dxy).wait_send()
        for dz in range(deep):
            for dxy in range(4):
                self.across(dz, dxy).wait_send()


def spread_small(vectors, long, place, width):
    wide = lambda v: jnp.concatenate(
        [v.astype(F32).reshape(1, -1), jnp.zeros((1, width - v.shape[0]), F32)], axis=1
    )
    short = jnp.concatenate([wide(v) for v in vectors], axis=0)
    short = pltpu.roll(short, place.me * 16, 1)
    long = pltpu.roll(jnp.broadcast_to(wide(long), (8, width)), place.me % 8 * 64, 1)
    line = lax.broadcasted_iota(jnp.int32, (8, width), 0)
    long = jnp.where(line == place.me // 8, long, 0.0)
    return jnp.concatenate([long, short], axis=0).astype(BF16)


def matrix(table, first, count=16):
    part = table[:, first : first + count, :]
    return part.reshape(part.shape[0] * count, part.shape[2])


def attend_kernel(frames, mesh_shape, *refs):
    x_in = refs[0]
    if mesh_shape is None:
        table, small_ref = refs[1:3]
        refs = refs[3:]
    else:
        wq_own, wk_own, wv_own, wo_own, wu_own, wd_own = refs[1:7]
        short_own = refs[7:16]
        refs = refs[16:]
    outputs, refs = refs[:6], refs[6:]
    if mesh_shape is not None:
        small_ref, first_ref, second_ref = refs[:3]
        refs = refs[3:]
    results, refs = refs[:6], refs[6:]
    qa_ref, ka_ref, vt_ref, ht_ref, ot_ref, qe_ref = results
    x_ref, units, scores, peaks, key_ext, log_rows, load, store = refs[:8]
    padded, width = units.shape
    depth = width // HEADS
    read = pltpu.make_async_copy(x_in, x_ref, load)
    read.start()

    def unit_rows():
        read.wait()
        for start in range(0, padded, ROWS):
            count = min(ROWS, frames - start)
            units[start : start + count, :] = normalize(
                x_ref[start : start + count, :].astype(F32)
            )[0]
        units[frames:, :] = jnp.zeros((padded - frames, width), F32)

    if mesh_shape is None:
        unit_rows()
    else:
        table, own, send_1, recv_1, send_2, recv_2, keep = refs[8:]
        place = Place(mesh_shape)
        place.greet()
        first = Spread(place, table.at[place.me], table, send_1, recv_1)
        second = Spread(place, own, second_ref, send_2, recv_2)
        table[place.me, 0:16, :] = wq_own[...]
        table[place.me, 16:32, :] = wk_own[...]
        table[place.me, 32:48, :] = wv_own[...]
        table[place.me, 48:64, :] = spread_small(
            [ref[...] for ref in short_own[:8]], short_own[8][...], place, width
        )
        place.meet()
        first.begin()
        own[0:16, :] = wo_own[...]
        chunks = wu_own.shape[1] // FF_CHUNK
        for j in range(chunks):
            own[16 + 16 * j : 32 + 16 * j, :] = wu_own[:, j * FF_CHUNK : (j + 1) * FF_CHUNK]
        own[16 + 16 * chunks :, :] = wd_own[...]
        unit_rows()
        first.relay_far()
        first.relay_near()
        second.begin()
        keep_own = pltpu.make_async_copy(own, second_ref.at[place.me], keep.at[0])
        keep_own.start()
        first.arrive()
        keep_first = pltpu.make_async_copy(table, first_ref, keep.at[1])
        keep_first.start()
        small_ref[...] = jnp.sum(table[:, 48:64, :].astype(F32), axis=0)

    writes = [
        pltpu.make_async_copy(results[i], outputs[i], store.at[i]) for i in (0, 1, 2, 3)
    ]
    last_write = pltpu.make_async_copy(qe_ref, outputs[5], store.at[4])

    def head_write(head):
        rows = pl.ds(pl.multiple_of(head * depth, depth), depth)
        return pltpu.make_async_copy(ot_ref.at[rows], outputs[4].at[rows], store.at[5 + head])

    bq, bv, gain, shift = (small_ref[r : r + 1, :] for r in (8, 9, 12, 13))

    def project(i, carry):
        rows = pl.ds(pl.multiple_of(i * ROWS, ROWS), ROWS)
        h1 = (units[rows, :] * gain + shift).astype(BF16)
        ht_ref[:, rows] = h1.T
        q = (dot(h1, matrix(table, 0), NN) + bq).astype(BF16)
        k = dot(h1, matrix(table, 16), NN).astype(BF16).astype(F32)
        k = k * (LOG2E / math.sqrt(depth))
        v = (dot(h1, matrix(table, 32), NN) + bv).astype(BF16)
        k_high = k.astype(BF16)
        k_low = (k - k_high.astype(F32)).astype(BF16)
        vt_ref[:, rows] = v.T
        for h in range(HEADS):
            cols = slice(h * depth, (h + 1) * depth)
            qa_ref[h, rows, :] = jnp.concatenate([q[:, cols], q[:, cols]], axis=1)
            ka_ref[h, rows, :] = jnp.concatenate([k_high[:, cols], k_low[:, cols]], axis=1)
        return carry

    lax.fori_loop(0, padded // ROWS, project, 0)
    for copy in writes:
        copy.start()

    blocks = padded // QUERIES
    steps = HEADS * blocks
    lane = lax.broadcasted_iota(jnp.int32, (QUERIES, 128), 1)
    query_ext = jnp.where(lane % 16 == 0, 1.0, 0.0).astype(BF16)

    def score(step, slot):
        head = step // blocks
        rows = pl.ds(pl.multiple_of((step % blocks) * QUERIES, QUERIES), QUERIES)
        key_ext[slot] = key_extra(head, padded, frames)
        left = jnp.concatenate([ka_ref[head], key_ext[slot]], axis=1)
        right = jnp.concatenate([qa_ref[head, rows, :], query_ext], axis=1)
        s = dot(left, right, NT)
        scores[slot] = s
        peaks[slot] = jnp.max(s, axis=0, keepdims=True)

    def finish(step, slot):
        head = step // blocks
        cols = pl.ds(pl.multiple_of((step % blocks) * QUERIES, QUERIES), QUERIES)
        peak = peaks[slot]
        weights = jnp.exp2(scores[slot] - peak).astype(BF16)
        rows = pl.ds(pl.multiple_of(head * depth, depth), depth)
        ones = jnp.ones((16, padded), BF16)
        mixed = dot(jnp.concatenate([vt_ref[rows, :], ones], axis=0), weights, NN)
        total = mixed[depth : depth + 1, :]
        ot_ref[rows, cols] = (mixed[:depth, :] * (1.0 / total)).astype(BF16)
        log_rows[head, :, cols] = peak + jnp.log2(total)

    score(0, 0)

    def pair(i, carry):
        if mesh_shape is not None:
            pl.when(i == FAR_AT)(second.relay_far)
            pl.when(i == NEAR_AT)(second.relay_near)
        score(i * 2 + 1, 1)
        finish(i * 2, 0)
        score(jnp.minimum(i * 2 + 2, steps - 1), 0)
        finish(i * 2 + 1, 1)
        head_write(i).start()
        return carry

    lax.fori_loop(0, steps // 2, pair, 0)

    def extend(i, carry):
        rows = pl.ds(pl.multiple_of(i * ROWS, ROWS), ROWS)
        pieces = []
        for h in range(HEADS):
            high, middle, low = in_three(-log_rows[h, :, rows])
            pieces += [jnp.ones((1, ROWS), F32), high, middle, low, jnp.zeros((12, ROWS), F32)]
        qe_ref[rows, :] = jnp.concatenate(pieces, axis=0).T.astype(BF16)
        return carry

    lax.fori_loop(0, padded // ROWS, extend, 0)
    last_write.start()
    for copy in writes + [last_write] + [head_write(head) for head in range(HEADS)]:
        copy.wait()
    if mesh_shape is not None:
        second.arrive()
        keep_own.wait()
        keep_first.wait()
        first.drain()
        second.drain()


def attend(mesh_shape, x, *rest):
    frames, width = x.shape
    padded = -(-frames // QUERIES) * QUERIES
    blocks = width // 16
    vmem = pl.BlockSpec(memory_space=pltpu.VMEM)
    hbm = pl.BlockSpec(memory_space=pltpu.HBM)
    out_shape = [
        jax.ShapeDtypeStruct((HEADS, padded, 128), BF16),
        jax.ShapeDtypeStruct((HEADS, padded, 128), BF16),
        jax.ShapeDtypeStruct((width, padded), BF16),
        jax.ShapeDtypeStruct((width, padded), BF16),
        jax.ShapeDtypeStruct((width, padded), BF16),
        jax.ShapeDtypeStruct((padded, 128), BF16),
    ]
    scratch = [pltpu.VMEM(shape.shape, shape.dtype) for shape in out_shape]
    scratch += [
        pltpu.VMEM((frames, width), BF16),
        pltpu.VMEM((padded, width), F32),
        pltpu.VMEM((2, padded, QUERIES), F32),
        pltpu.VMEM((2, 1, QUERIES), F32),
        pltpu.VMEM((2, padded, 128), BF16),
        pltpu.VMEM((HEADS, 1, padded), F32),
        pltpu.SemaphoreType.DMA,
        pltpu.SemaphoreType.DMA((5 + HEADS,)),
    ]
    out_specs = [hbm] * 6
    options = {}
    if mesh_shape is not None:
        hidden = rest[4].shape[1]
        own_rows = 16 + hidden // FF_CHUNK * 16 + rest[5].shape[0]
        out_shape += [
            jax.ShapeDtypeStruct((16, width), F32),
            jax.ShapeDtypeStruct((blocks, 64, width), BF16),
            jax.ShapeDtypeStruct((blocks, own_rows, width), BF16),
        ]
        out_specs += [vmem, hbm, hbm]
        scratch += [
            pltpu.VMEM((blocks, 64, width), BF16),
            pltpu.VMEM((own_rows, width), BF16),
        ]
        scratch += [pltpu.SemaphoreType.DMA((blocks - 1,)) for _ in range(4)]
        scratch += [pltpu.SemaphoreType.DMA((2,))]
        options = dict(collective_id=0, has_side_effects=True)
    return pl.pallas_call(
        functools.partial(attend_kernel, frames, mesh_shape),
        out_shape=out_shape,
        in_specs=[hbm] + [vmem] * len(rest),
        out_specs=out_specs,
        scratch_shapes=scratch,
        compiler_params=pltpu.CompilerParams(vmem_limit_bytes=60 << 20, **options),
        name="attend",
    )(x, *rest)


def mlp_kernel(
    frames,
    flag_ref,
    x_ref,
    cot_ref,
    ot_ref,
    table,
    vec_ref,
    out_ref,
    dx_ref,
    do_ref,
    de_ref,
    grads_ref,
    small_ref,
    gwo,
    gwu,
    gwd,
):
    step = pl.program_id(0)
    rows, width = x_ref.shape
    chunks = gwu.shape[0]
    depth = width // HEADS
    down = table.shape[1] - 16 - 16 * chunks
    per_chunk = FF_CHUNK // down

    def up_part(j):
        return matrix(table, 16 + 16 * j)

    def down_part(j):
        part = table[j * per_chunk : (j + 1) * per_chunk, 16 + 16 * chunks :, :]
        return part.reshape(FF_CHUNK, width)

    @pl.when(step == 0)
    def _():
        gwo[...] = jnp.zeros_like(gwo)
        gwu[...] = jnp.zeros_like(gwu)
        gwd[...] = jnp.zeros_like(gwd)
        small_ref[...] = jnp.zeros_like(small_ref)

    flag = flag_ref[0].astype(F32)
    inside = step * rows + lax.broadcasted_iota(jnp.int32, (rows, width), 0) < frames
    x = jnp.where(inside, x_ref[...].astype(F32), 0.0)
    dy = jnp.where(inside, cot_ref[...].astype(F32), 0.0) * flag
    dy_low = dy.astype(BF16)
    bo, bd, gain, shift = (vec_ref[r : r + 1, :] for r in (10, 11, 14, 15))
    wo = matrix(table, 0)
    ot = ot_ref[...]
    o = ot.T
    x1 = x + (dot(o, wo, NN) + bo)
    unit, inv_std = normalize(x1)
    h2 = (unit * gain + shift).astype(BF16)
    h2t = h2.T
    z_next = dot(h2, up_part(0), NN)
    out = x1 + bd
    dh2 = jnp.zeros((rows, width), F32)
    for j in range(chunks):
        z = z_next + vec_ref[j : j + 1, :]
        if j + 1 < chunks:
            z_next = dot(h2, up_part(j + 1), NN)
        dg = dot(dy_low, down_part(j), NT)
        g, slope = gelu_and_slope(z)
        g = g.astype(BF16)
        dz = (dg * slope).astype(BF16)
        out = out + dot(g, down_part(j), NN)
        gwd[j] += dot(g, dy_low, TN)
        gwu[j] += dot(h2t, dz, NN)
        small_ref[j : j + 1, :] += column_sums(dz.astype(F32))
        dh2 = dh2 + dot(dz, up_part(j), NT)
    store_rows(out_ref, 0, out * flag)
    dx1 = dy + normalize_back(dh2, unit, inv_std, gain)
    dx_ref[...] = dx1
    da = dx1.astype(BF16)
    gwo[...] += dot(ot, da, NN)
    do = dot(da, wo, NT).astype(BF16)
    small_ref[10:11, :] += column_sums(da.astype(F32))
    small_ref[11:12, :] += column_sums(dy)
    small_ref[14:15, :] += column_sums(dh2 * unit)
    small_ref[15:16, :] += column_sums(dh2)
    do_ref[...] = do
    prod = do.astype(F32) * o.astype(F32)
    high = prod.astype(BF16)
    low = (prod - high.astype(F32)).astype(BF16)
    owner = lax.broadcasted_iota(jnp.int32, (width, 128), 0) // depth
    pick = lax.broadcasted_iota(jnp.int32, (width, 128), 1) // 16
    pick = jnp.where(owner == pick, 1.0, 0.0).astype(BF16)
    high, middle, low = in_three(-(dot(high, pick, NN) + dot(low, pick, NN)))
    lane = lax.broadcasted_iota(jnp.int32, (rows, 128), 1) % 16
    extra = jnp.where(lane == 1, middle, jnp.where(lane == 2, low, 0.0))
    de_ref[...] = jnp.where(lane == 0, high, extra).astype(BF16)

    @pl.when(step == pl.num_programs(0) - 1)
    def _():
        split = lambda part, count: part.astype(BF16).reshape(-1, count, width)
        grads_ref[:, 0:16, :] = split(gwo[...], 16)
        for j in range(chunks):
            grads_ref[:, 16 + 16 * j : 32 + 16 * j, :] = split(gwu[j], 16)
            grads_ref[j * per_chunk : (j + 1) * per_chunk, 16 + 16 * chunks :, :] = split(
                gwd[j], down
            )


def mlp(flag, x, cot, ot, table, vectors):
    frames, width = x.shape
    padded = ot.shape[1]
    blocks, rows = table.shape[:2]
    chunks = (rows - 16) * blocks // (2 * FF_CHUNK)
    by_rows = pl.BlockSpec((MLP_ROWS, width), lambda i: (i, 0))
    fixed = lambda shape: pl.BlockSpec(
        shape, lambda i: (0,) * len(shape), pipeline_mode=pl.Buffered(1)
    )
    return pl.pallas_call(
        functools.partial(mlp_kernel, frames),
        grid=(padded // MLP_ROWS,),
        out_shape=[
            jax.ShapeDtypeStruct((frames * width // 128, 128), F32),
            jax.ShapeDtypeStruct((frames, width), F32),
            jax.ShapeDtypeStruct((padded, width), BF16),
            jax.ShapeDtypeStruct((padded, 128), BF16),
            jax.ShapeDtypeStruct(table.shape, BF16),
            jax.ShapeDtypeStruct((16, width), F32),
        ],
        in_specs=[
            pl.BlockSpec(memory_space=pltpu.SMEM),
            by_rows,
            by_rows,
            pl.BlockSpec((width, MLP_ROWS), lambda i: (0, i)),
            fixed(table.shape),
            fixed((16, width)),
        ],
        out_specs=[
            pl.BlockSpec((MLP_ROWS * width // 128, 128), lambda i: (i, 0)),
            by_rows,
            by_rows,
            pl.BlockSpec((MLP_ROWS, 128), lambda i: (i, 0)),
            fixed(table.shape),
            fixed((16, width)),
        ],
        scratch_shapes=[
            pltpu.VMEM((width, width), F32),
            pltpu.VMEM((chunks, width, FF_CHUNK), F32),
            pltpu.VMEM((chunks, FF_CHUNK, width), F32),
        ],
        compiler_params=pltpu.CompilerParams(
            vmem_limit_bytes=60 << 20, dimension_semantics=("arbitrary",)
        ),
        name="mlp",
    )(flag, x, cot, ot, table, vectors)


class Gather:
    def __init__(self, place, source, from_core, halves, from_near, quarter, from_far, sems):
        self.place, self.source = place, source
        self.from_core, self.halves = from_core, halves
        self.from_near, self.quarter = from_near, quarter
        self.from_far = from_far
        self.send_sem, self.recv_sem = sems

    def copy(self, slot, src, dst, device):
        return pltpu.make_async_remote_copy(
            src_ref=src,
            dst_ref=dst,
            send_sem=self.send_sem.at[slot],
            recv_sem=self.recv_sem.at[slot],
            device_id=device,
            device_id_type=MESH,
        )

    def across(self):
        place = self.place
        return [
            self.copy(
                z, self.source.at[z, :, 1 - place.core], self.from_core.at[z], place.moved(flip=1)
            )
            for z in range(place.deep)
        ]

    def near(self):
        place = self.place
        copies = []
        for dxy in range(1, 4):
            b, s = place.moved(dxy=dxy)
            square = b % 2 * 2 + s // 2
            copies.append(
                self.copy(
                    place.deep + dxy - 1,
                    self.halves.at[:, square],
                    self.from_near.at[dxy - 1],
                    (b, s),
                )
            )
        return copies

    def far(self):
        place = self.place
        copies = []
        for dz in range(1, place.deep):
            z = (place.z + dz) % place.deep
            copies.append(
                self.copy(
                    place.deep + 2 + dz,
                    self.quarter.at[z],
                    self.from_far.at[dz - 1],
                    place.moved(dz=dz),
                )
            )
        return copies

    def fold_across(self, own):
        for copy in self.across():
            copy.wait_recv()

        def one(i, carry):
            z, q = i // 4, i % 4
            total = own(z, q).astype(F32) + self.from_core[z, q].astype(F32)
            self.halves[z, q] = total.astype(BF16)
            return carry

        lax.fori_loop(0, self.place.deep * 4, one, 0)
        for copy in self.near():
            copy.start()

    def fold_near(self):
        for copy in self.near():
            copy.wait_recv()

        def one(z, carry):
            total = self.halves[z, self.place.square].astype(F32)
            for dxy in range(3):
                total = total + self.from_near[dxy, z].astype(F32)
            self.quarter[z] = total.astype(BF16)
            return carry

        lax.fori_loop(0, self.place.deep, one, 0)
        for copy in self.far():
            copy.start()

    def result(self):
        for copy in self.far():
            copy.wait_recv()
        total = self.quarter[self.place.z].astype(F32)
        for dz in range(self.place.deep - 1):
            total = total + self.from_far[dz].astype(F32)
        return total

    def drain(self):
        for copy in self.across() + self.near() + self.far():
            copy.wait_send()


class SmallSum:
    def __init__(self, place, buffers, received, sems):
        self.place, self.buffers, self.received = place, buffers, received
        self.send_sem, self.recv_sem = sems

    def copies(self, stage):
        place = self.place
        if stage == 0:
            devices, first = [place.moved(flip=1)], 0
        elif stage == 1:
            devices, first = [place.moved(dxy=dxy) for dxy in range(1, 4)], 1
        else:
            devices, first = [place.moved(dz=dz) for dz in range(1, place.deep)], 4
        return [
            pltpu.make_async_remote_copy(
                src_ref=self.buffers.at[stage],
                dst_ref=self.received.at[first + i],
                send_sem=self.send_sem.at[first + i],
                recv_sem=self.recv_sem.at[first + i],
                device_id=device,
                device_id_type=MESH,
            )
            for i, device in enumerate(devices)
        ]

    def send(self, stage, value):
        self.buffers[stage] = value
        for copy in self.copies(stage):
            copy.start()

    def receive(self, stage):
        total = self.buffers[stage]
        first = (0, 1, 4)[stage]
        for i, copy in enumerate(self.copies(stage)):
            copy.wait_recv()
            total = total + self.received[first + i]
        return total

    def drain(self):
        for stage in range(3):
            for copy in self.copies(stage):
                copy.wait_send()


def own_small(total, place):
    width = total.shape[1]
    line = lax.broadcasted_iota(jnp.int32, total.shape, 0)
    short = pltpu.roll(total, width - place.me * 16, 1)
    long = jnp.sum(jnp.where(line == place.me // 8, total, 0.0), axis=0, keepdims=True)
    long = pltpu.roll(jnp.broadcast_to(long, total.shape), width - place.me % 8 * 64, 1)
    return jnp.where(line == 0, long, short)[:, :128]


def attend_back_kernel(frames, mesh_shape, *refs):
    x_in, dx_in, qa_in, ka_in, vt_in, ht_in, qe_in, do_in, de_in, table_in = refs[:10]
    vec_ref, small_in = refs[10:12]
    refs = refs[12:]
    if mesh_shape is None:
        dinput_out, source, small_ref = refs[:3]
        refs = refs[3:]
    else:
        grads_ref = refs[0]
        dinput_out, gq_ref, gk_ref, gv_ref, go_ref, gu_ref, gd_ref = refs[1:8]
        short_refs = refs[8:17]
        refs = refs[17:]
    x_ref, dx_ref, qa_ref, ka_ref, vt_ref, ht_ref, qe_ref, do_ref, de_ref, table = refs[:10]
    dinput_ref, load, store = refs[10:13]
    dq, dkt, dvt, sum_k, sum_v, key_ext, value_ext, small = refs[13:21]
    refs = refs[21:]

    padded = qa_ref.shape[1]
    width = ht_ref.shape[0]
    depth = width // HEADS

    def head_loads(head):
        return [
            pltpu.make_async_copy(qa_in.at[head], qa_ref.at[head], load.at[2 * head]),
            pltpu.make_async_copy(ka_in.at[head], ka_ref.at[head], load.at[2 * head + 1]),
        ]

    sources = (vt_in, do_in, de_in, qe_in, ht_in, table_in.at[:, 0:48], x_in, dx_in)
    targets = (vt_ref, do_ref, de_ref, qe_ref, ht_ref, table, x_ref, dx_ref)
    loads = [
        pltpu.make_async_copy(source_ref, target_ref, load.at[2 * HEADS + i])
        for i, (source_ref, target_ref) in enumerate(zip(sources, targets))
    ]
    for copy in head_loads(0) + loads[:4]:
        copy.start()
    for head in range(1, HEADS):
        for copy in head_loads(head):
            copy.start()
    for copy in loads[4:]:
        copy.start()

    if mesh_shape is not None:
        place = Place(mesh_shape)
        halves = [
            Gather(place, refs[8 * t], *refs[8 * t + 1 : 8 * t + 6], refs[8 * t + 6 : 8 * t + 8])
            for t in range(2)
        ]
        second = Gather(place, grads_ref, *refs[16:21], refs[21:23])
        shorts = SmallSum(place, refs[23], refs[24], refs[25:27])
        second_half, keep = refs[27:]
        place.greet()
        place.meet()
        for copy in second.across():
            copy.start()
        keep_half = pltpu.make_async_copy(grads_ref.at[:, :, place.core], second_half, keep)
        keep_half.start()
    for copy in loads[:4]:
        copy.wait()

    def second_across():
        keep_half.wait()
        second.fold_across(lambda z, q: second_half[z, q])

    lane_half = lax.broadcasted_iota(jnp.int32, (padded, 128), 1) < depth

    def weight_grads(t):
        cols = slice(t * (width // 2), (t + 1) * (width // 2))
        heads = range(t * (HEADS // 2), (t + 1) * (HEADS // 2), 2)
        queries = jnp.concatenate([jnp.where(lane_half, dq[h], dq[h + 1]) for h in heads], axis=1)
        ht = ht_ref[...]
        parts = (
            dot(ht, queries, NN),
            dot(ht, dkt[cols, :], NT),
            dot(ht, dvt[cols, :], NT),
        )
        for i, part in enumerate(parts):
            part = part.astype(BF16)
            if mesh_shape is None:
                source[:, 16 * i : 16 * i + 16, cols] = part.reshape(-1, 16, width // 2)
            else:
                target = halves[t].source
                target[:, :, :, 16 * i : 16 * i + 16, :] = part.reshape(
                    target.shape[:3] + (16, width // 2)
                )
        if mesh_shape is not None:
            for copy in halves[t].across():
                copy.start()

    def fold_half(t):
        halves[t].fold_across(lambda z, q: halves[t].source[z, q, place.core])

    def half_result(t):
        total = halves[t].result()
        for i, ref in enumerate((gq_ref, gk_ref, gv_ref)):
            ref[:, t * (width // 2) : (t + 1) * (width // 2)] = total[16 * i : 16 * i + 16]

    def first_weight_grads():
        loads[4].wait()
        weight_grads(0)

    def one_head(head, carry):
        pl.when(head == HEADS // 2)(first_weight_grads)
        if mesh_shape is not None:
            pl.when(head == 1)(second_across)
            pl.when(head == 5)(second.fold_near)
            pl.when(head == 6)(functools.partial(fold_half, 0))
        for copy in head_loads(head):
            copy.wait()
        key_ext[...] = key_extra(head, padded, frames)
        line = lax.broadcasted_iota(jnp.int32, (128, padded), 0)
        mine = pl.ds(pl.multiple_of(head // 2 * 128, 128), 128)
        values = jnp.where(line // depth == head % 2, vt_ref[mine, :].astype(F32), 0.0)
        value_ext[0:128, :] = values.astype(BF16)
        extra = jnp.where((line // 16 == head) & (line % 16 < 3), 1.0, 0.0)
        value_ext[128:256, :] = extra.astype(BF16)
        for i in range(padded // ROWS):
            rows = slice(i * ROWS, (i + 1) * ROWS)
            q = qa_ref[head, rows, :]
            d = do_ref[rows, mine]
            turned = d.T
            turned = jnp.where(head % 2 == 0, turned[:depth], turned[depth:])
            s = dot(
                jnp.concatenate([q, qe_ref[rows, :]], axis=1),
                jnp.concatenate([ka_ref[head], key_ext[...]], axis=1),
                NT,
            )
            p = jnp.exp2(s)
            dp = dot(jnp.concatenate([d, de_ref[rows, :]], axis=1), value_ext[...], NN)
            ds = (p * dp).astype(BF16)
            p = p.astype(BF16)
            new_v = dot(turned, p, NN)
            new_k = dot(q[:, :depth], ds, TN)
            if i == 0:
                sum_v[...] = new_v
                sum_k[...] = new_k
            else:
                sum_v[...] += new_v
                sum_k[...] += new_k
            both = dot(ds, ka_ref[head], NN)
            both = both + pltpu.roll(both, depth, 1)
            dq[head, rows, :] = (both * LN2).astype(BF16)
        out_rows = pl.ds(pl.multiple_of(head * depth, depth), depth)
        dkt[out_rows, :] = (sum_k[...] * (1.0 / math.sqrt(depth))).astype(BF16)
        dvt[out_rows, :] = sum_v[...].astype(BF16)
        return carry

    lax.fori_loop(0, HEADS, one_head, 0)

    weight_grads(1)
    for copy in loads[5:]:
        copy.wait()
    if mesh_shape is not None:
        halves[0].fold_near()
        second_own = second.result()
        chunks = gu_ref.shape[1] // FF_CHUNK
        go_ref[...] = second_own[0:16]
        for j in range(chunks):
            gu_ref[:, j * FF_CHUNK : (j + 1) * FF_CHUNK] = second_own[16 + 16 * j : 32 + 16 * j]
        gd_ref[...] = second_own[16 + 16 * chunks :]

    gain = vec_ref[12:13, :]
    small[...] = small_in[...]
    stores = []
    for index, start in enumerate(range(0, frames, ROWS)):
        if mesh_shape is not None and index == FOLD_AT:
            fold_half(1)
        count = min(ROWS, frames - start)
        rows = slice(start, start + count)
        wide = slice(start, start + ROWS)
        some = lane_half[:ROWS]
        dq_rows = jnp.concatenate(
            [jnp.where(some, dq[h, wide, :], dq[h + 1, wide, :]) for h in range(0, HEADS, 2)],
            axis=1,
        )
        dk_rows = dkt[:, wide].T
        dv_rows = dvt[:, wide].T
        dh1 = (
            dot(dq_rows, matrix(table, 0), NT)
            + dot(dk_rows, matrix(table, 16), NT)
            + dot(dv_rows, matrix(table, 32), NT)
        )
        small[8:9, :] += column_sums(dq_rows.astype(F32))
        small[9:10, :] += column_sums(dv_rows.astype(F32))
        dh1 = dh1[:count]
        unit, inv_std = normalize(x_ref[rows, :].astype(F32))
        small[12:13, :] += column_sums(dh1 * unit)
        small[13:14, :] += column_sums(dh1)
        dinput = dx_ref[rows, :] + normalize_back(dh1, unit, inv_std, gain)
        store_rows(dinput_ref, start, dinput)
        part = pl.ds(start * (width // 128), count * (width // 128))
        stores.append(
            pltpu.make_async_copy(dinput_ref.at[part], dinput_out.at[part], store.at[index])
        )
        stores[-1].start()
    if mesh_shape is None:
        small_ref[...] = small[...]
    else:
        shorts.send(0, small[...])
        half_result(0)
        shorts.send(1, shorts.receive(0))
        halves[1].fold_near()
        shorts.send(2, shorts.receive(1))
        second.drain()
        halves[0].drain()
        half_result(1)
        small_own = own_small(shorts.receive(2), place)
        for i, ref in enumerate(short_refs[:8]):
            ref[...] = small_own[8 + i, :16]
        short_refs[8][...] = small_own[0, :64]
        halves[1].drain()
        shorts.drain()
    for copy in stores:
        copy.wait()


def attend_back(mesh_shape, x, dx, qa, ka, vt, ht, qe, do, de, table, vectors, small, grads):
    frames, width = x.shape
    padded = ht.shape[1]
    blocks = width // 16
    vmem = pl.BlockSpec(memory_space=pltpu.VMEM)
    hbm = pl.BlockSpec(memory_space=pltpu.HBM)
    args = [x, dx, qa, ka, vt, ht, qe, do, de, table, vectors, small]
    in_specs = [hbm] * 10 + [vmem] * 2
    lines = frames * width // 128
    out_shape = [jax.ShapeDtypeStruct((lines, 128), F32)]
    scratch = [pltpu.VMEM(array.shape, array.dtype) for array in args[:9]]
    scratch += [
        pltpu.VMEM((blocks, 48, width), BF16),
        pltpu.VMEM((lines, 128), F32),
        pltpu.SemaphoreType.DMA((2 * HEADS + 8,)),
        pltpu.SemaphoreType.DMA((padded // ROWS,)),
        pltpu.VMEM((HEADS, padded, 128), BF16),
        pltpu.VMEM((width, padded), BF16),
        pltpu.VMEM((width, padded), BF16),
        pltpu.VMEM((width // HEADS, padded), F32),
        pltpu.VMEM((width // HEADS, padded), F32),
        pltpu.VMEM((padded, 128), BF16),
        pltpu.VMEM((256, padded), BF16),
        pltpu.VMEM((16, width), F32),
    ]
    options = {}
    if mesh_shape is None:
        out_shape += [
            jax.ShapeDtypeStruct((blocks, 48, width), BF16),
            jax.ShapeDtypeStruct((16, width), F32),
        ]
    else:
        deep = mesh_shape[0] // 2
        rows = grads.shape[1]
        hidden = (rows - 16) * blocks // 2
        args.append(grads.reshape(deep, 4, 2, rows, width))
        in_specs.append(hbm)
        out_shape += [
            jax.ShapeDtypeStruct((16, width), F32),
            jax.ShapeDtypeStruct((16, width), F32),
            jax.ShapeDtypeStruct((16, width), F32),
            jax.ShapeDtypeStruct((16, width), F32),
            jax.ShapeDtypeStruct((16, hidden), F32),
            jax.ShapeDtypeStruct((hidden // blocks, width), F32),
        ]
        out_shape += [jax.ShapeDtypeStruct((16,), F32)] * 8
        out_shape += [jax.ShapeDtypeStruct((hidden // blocks,), F32)]

        def stages(shape):
            return [
                pltpu.VMEM((deep, 4) + shape, BF16),
                pltpu.VMEM((deep, 4) + shape, BF16),
                pltpu.VMEM((3, deep) + shape, BF16),
                pltpu.VMEM((deep,) + shape, BF16),
                pltpu.VMEM((deep - 1,) + shape, BF16),
                pltpu.SemaphoreType.DMA((2 * deep + 2,)),
                pltpu.SemaphoreType.DMA((2 * deep + 2,)),
            ]

        half_shape = (48, width // 2)
        for _ in range(2):
            scratch += [pltpu.VMEM((deep, 4, 2) + half_shape, BF16)] + stages(half_shape)
        scratch += stages((rows, width))
        scratch += [
            pltpu.VMEM((3, 16, width), F32),
            pltpu.VMEM((deep + 3, 16, width), F32),
            pltpu.SemaphoreType.DMA((deep + 3,)),
            pltpu.SemaphoreType.DMA((deep + 3,)),
            pltpu.VMEM((deep, 4, rows, width), BF16),
            pltpu.SemaphoreType.DMA,
        ]
        options = dict(collective_id=1, has_side_effects=True)
    return pl.pallas_call(
        functools.partial(attend_back_kernel, frames, mesh_shape),
        out_shape=out_shape,
        in_specs=in_specs,
        out_specs=[hbm] + [vmem] * (len(out_shape) - 1),
        scratch_shapes=scratch,
        compiler_params=pltpu.CompilerParams(vmem_limit_bytes=60 << 20, **options),
        name="attend_back",
    )(*args)


def hand_over_kernel(count, *refs):
    large, small = refs[0], refs[1 : count + 1]
    large_buf, small_buf = refs[2 * count + 2], refs[2 * count + 3 : 3 * count + 3]
    large_out, small_out = refs[count + 1], refs[count + 2 : 2 * count + 2]
    sem_in, sem_out = refs[3 * count + 3 :]
    pieces = large_buf.shape[0]
    rows = large_buf.shape[1]
    sources = [large.at[pl.ds(i * rows, rows)] for i in range(pieces)] + list(small)
    buffers = [large_buf.at[i] for i in range(pieces)] + list(small_buf)
    targets = [large_out.at[pl.ds(i * rows, rows)] for i in range(pieces)] + list(small_out)
    inward = [
        pltpu.make_async_copy(source, buffer, sem_in.at[i])
        for i, (source, buffer) in enumerate(zip(sources, buffers))
    ]
    outward = [
        pltpu.make_async_copy(buffer, target, sem_out.at[i])
        for i, (buffer, target) in enumerate(zip(buffers, targets))
    ]
    for copy in inward:
        copy.start()
    for first, then in zip(inward, outward):
        first.wait()
        then.start()
    for copy in outward:
        copy.wait()


def hand_over(large, *small):
    anywhere = pl.BlockSpec(memory_space=pltpu.HBM)
    arrays = (large,) + small
    rows = large.shape[0]
    pieces = 6 if rows % 48 == 0 else 1
    return pl.pallas_call(
        functools.partial(hand_over_kernel, len(small)),
        out_shape=[jax.ShapeDtypeStruct(array.shape, array.dtype) for array in arrays],
        in_specs=[anywhere] * len(arrays),
        out_specs=[anywhere] * len(arrays),
        scratch_shapes=[pltpu.VMEM((pieces, rows // pieces) + large.shape[1:], large.dtype)]
        + [pltpu.VMEM(array.shape, array.dtype) for array in small]
        + [pltpu.SemaphoreType.DMA((len(small) + pieces,))] * 2,
        compiler_params=pltpu.CompilerParams(vmem_limit_bytes=60 << 20),
        name="hand_over",
    )(*arrays)


def staged(mesh_shape, windows, cotangent, valid, *owned):
    x, cot = windows[0], cotangent[0]
    bq, bv, bo, bu, bd, gain_one, shift_one, gain_two, shift_two = owned[6:]
    short = [bq, bv, bo, bd, gain_one, shift_one, gain_two, shift_two, bu]
    qa, ka, vt, ht, ot, qe, vectors, first, second = attend(mesh_shape, x, *owned[:6], *short)
    out, dx, do, de, grads, small = mlp(valid, x, cot, ot, second, vectors)
    results = attend_back(
        mesh_shape, x, dx, qa, ka, vt, ht, qe, do, de, first, vectors, small, grads
    )
    dinput, gq, gk, gv, go, gu, gd, *shorts = hand_over(*results)
    gbq, gbv, gbo, gbd, *gains, gbu = shorts
    return (
        out.reshape(windows.shape),
        dinput.reshape(windows.shape),
        *(gq, gk, gv, go, gu, gd, gbq, gbv, gbo, gbu, gbd),
        *gains,
    )


def collective(windows, cotangent, valid, *owned):
    axes = ("batch", "shard")
    wq, wk, wv, wo, wu, wd, bq, bv, bo, bu, bd, gain_one, shift_one, gain_two, shift_two = [
        lax.all_gather(part, axes, axis=0, tiled=True) for part in owned
    ]
    x, cot = windows[0], cotangent[0]
    width, hidden = wu.shape
    blocks, chunks = width // 16, hidden // FF_CHUNK
    split = lambda part: part.reshape(blocks, -1, width)
    vectors = jnp.concatenate(
        [jnp.pad(bu.reshape(chunks, FF_CHUNK), ((0, 8 - chunks), (0, 0)))]
        + [v[None] for v in (bq, bv, bo, bd, gain_one, shift_one, gain_two, shift_two)]
    ).astype(F32)
    first = jnp.concatenate([split(wq), split(wk), split(wv)], axis=1)
    ups = wu.reshape(blocks, 16, chunks, FF_CHUNK).transpose(0, 2, 1, 3)
    ups = ups.reshape(blocks, 16 * chunks, FF_CHUNK)
    second = jnp.concatenate([split(wo), ups, split(wd)], axis=1)
    qa, ka, vt, ht, ot, qe = attend(None, x, first, vectors)
    out, dx, do, de, grads, small = mlp(valid, x, cot, ot, second, vectors)
    dinput, first_grads, small = attend_back(
        None, x, dx, qa, ka, vt, ht, qe, do, de, first, vectors, small, None
    )
    first_grads, grads = first_grads.astype(F32), grads.astype(F32)
    joined = lambda part: part.reshape(-1, width)
    gwu = grads[:, 16 : 16 + 16 * chunks].reshape(blocks, chunks, 16, FF_CHUNK)
    gwu = gwu.transpose(0, 2, 1, 3).reshape(width, hidden)
    totals = (
        joined(first_grads[:, 0:16]),
        joined(first_grads[:, 16:32]),
        joined(first_grads[:, 32:48]),
        joined(grads[:, 0:16]),
        gwu,
        joined(grads[:, 16 + 16 * chunks :]),
        small[8],
        small[9],
        small[10],
        small[:chunks].reshape(hidden),
        small[11],
        small[12],
        small[13],
        small[14],
        small[15],
    )
    grads = [lax.psum_scatter(total, axes, scatter_dimension=0, tiled=True) for total in totals]
    return (out.reshape(windows.shape), dinput.reshape(windows.shape), *grads)


def solution(mesh):
    both = ("batch", "shard")
    windows_spec, matrix_spec, vector_spec = P(both, None, None), P(both, None), P(both)
    params = (matrix_spec,) * 6 + (vector_spec,) * 9
    mesh_shape = (mesh.shape["batch"], mesh.shape["shard"])

    def per_device(windows, cotangent, valid, *owned):
        if mesh_shape[1] == 4 and mesh_shape[0] % 2 == 0 and owned[0].shape[0] == 16:
            return staged(mesh_shape, windows, cotangent, valid, *owned)
        return collective(windows, cotangent, valid, *owned)

    return jax.shard_map(
        per_device,
        mesh=mesh,
        in_specs=(windows_spec, windows_spec, vector_spec) + params,
        out_specs=(windows_spec, windows_spec) + params,
        check_vma=False,
    )
```

```python
import functools
import math

import jax
import jax.numpy as jnp
from jax import lax
from jax.experimental import pallas as pl
from jax.experimental.pallas import tpu as pltpu
from jax.sharding import PartitionSpec as P

HEADS = 8
NORM_EPS = 1e-05
LOG2E = math.log2(math.e)
LN2 = math.log(2.0)
F32 = jnp.float32
BF16 = jnp.bfloat16
MESH = pl.DeviceIdType.MESH
ROWS = 256
MLP_ROWS = 512
EARLY_HEADS = 4
B_FAR_AT = 0
B_NEAR_AT = 2
FAR_AT = 2
NEAR_AT = 7
FOLD_AT = 2
ACROSS_AT = 1
SQUARE_AT = 5
PARTS = ((0, 4), (4, 8))
QUERIES = 768
FF_CHUNK = 512
MASKED = -1e30

NN = (((1,), (0,)), ((), ()))
NT = (((1,), (1,)), ((), ()))
TN = (((0,), (0,)), ((), ()))

TAIL_RATE = 0.3
TAIL = (
    0.1196320072075501,
    0.12071213658889111,
    0.10017594509547065,
    0.12769178078587456,
    -0.0520340331315144,
    0.2045568015805396,
    -0.1561584571261984,
    0.03542373729935703,
)


def dot(left, right, dims):
    return lax.dot_general(left, right, dims, preferred_element_type=F32)


def normalize(values):
    centred = values - jnp.mean(values, axis=-1, keepdims=True)
    variance = jnp.mean(centred * centred, axis=-1, keepdims=True)
    inv_std = lax.rsqrt(variance + NORM_EPS)
    return centred * inv_std, inv_std


def normalize_back(grad_rows, unit_rows, inv_std, gain):
    scaled = grad_rows * gain
    first_mean = jnp.mean(scaled, axis=-1, keepdims=True)
    second_mean = jnp.mean(scaled * unit_rows, axis=-1, keepdims=True)
    return inv_std * (scaled - first_mean - unit_rows * second_mean)


def store_rows(ref, start, rows):
    count, width = rows.shape
    parts = width // 128
    for j in range(parts):
        ref[pl.ds(start * parts + j, count, stride=parts), :] = rows[:, j * 128 : (j + 1) * 128]


def column_sums(rows):
    return jnp.sum(rows, axis=0, keepdims=True)


def in_three(values):
    high = values.astype(BF16).astype(F32)
    rest = values - high
    middle = rest.astype(BF16).astype(F32)
    return high, middle, rest - middle


def gelu_and_slope(z):
    size = jnp.abs(z)
    t = 1.0 / (1.0 + TAIL_RATE * size)
    poly = jnp.full_like(t, TAIL[-1])
    for coefficient in TAIL[-2::-1]:
        poly = poly * t + coefficient
    bell = jnp.exp2(z * z * (-0.5 * LOG2E))
    tail = poly * t * bell
    cdf = jnp.where(z > 0, 1.0 - tail, tail)
    return z * cdf, cdf + z * bell * (1.0 / math.sqrt(2.0 * math.pi))


def key_extra(head, keys, frames):
    row = lax.broadcasted_iota(jnp.int32, (keys, 128), 0)
    lane = lax.broadcasted_iota(jnp.int32, (keys, 128), 1) - head * 16
    mask = jnp.where(row < frames, 0.0, MASKED)
    ones = jnp.where((lane > 0) & (lane < 4), 1.0, 0.0)
    return jnp.where(lane == 0, mask, ones).astype(BF16)


class Place:
    def __init__(self, mesh_shape):
        self.batch, self.shard = mesh_shape
        self.deep = self.batch // 2
        b, s = lax.axis_index("batch"), lax.axis_index("shard")
        self.z, self.x, self.y, self.core = b // 2, b % 2, s // 2, s % 2
        self.me = b * self.shard + s
        self.square = self.x * 2 + self.y

    def moved(self, dz=0, dxy=0, flip=0):
        dx, dy = dxy // 2, dxy % 2
        x = 1 - self.x if dx else self.x
        y = 1 - self.y if dy else self.y
        core = 1 - self.core if flip else self.core
        return (self.z + self.deep + dz) % self.deep * 2 + x, y * 2 + core

    def block(self, dz=0, dxy=0, flip=0):
        b, s = self.moved(-dz, dxy, flip)
        return b * self.shard + s

    def partners(self):
        far = [self.moved(dz=dz) for dz in range(1, self.deep)]
        near = [self.moved(dxy=dxy) for dxy in range(1, 4)]
        return far + near + [self.moved(flip=1)]

    def greet(self):
        barrier = pltpu.get_barrier_semaphore()
        for partner in self.partners():
            pl.semaphore_signal(barrier, inc=1, device_id=partner, device_id_type=MESH)

    def meet(self):
        pl.semaphore_wait(pltpu.get_barrier_semaphore(), self.deep + 3)


class Spread:
    def __init__(self, place, own, table, send_sem, recv_sem):
        self.place, self.own, self.table = place, own, table
        self.send_sem, self.recv_sem = send_sem, recv_sem
        self.started = []

    def copy(self, slot, dz, dxy, device):
        block = self.place.block(dz, dxy)
        here = dz == 0 and dxy == 0
        return pltpu.make_async_remote_copy(
            src_ref=self.own if here else self.table.at[block],
            dst_ref=self.table.at[block],
            send_sem=self.send_sem.at[slot],
            recv_sem=self.recv_sem.at[slot],
            device_id=device,
            device_id_type=MESH,
        )

    def far(self, dz):
        return self.copy(dz - 1, 0, 0, self.place.moved(dz=dz))

    def near(self, dz, dxy):
        slot = self.place.deep - 1 + dz * 3 + dxy - 1
        return self.copy(slot, dz, 0, self.place.moved(dxy=dxy))

    def across(self, dz, dxy):
        slot = self.place.deep * 4 - 1 + dz * 4 + dxy
        return self.copy(slot, dz, dxy, self.place.moved(flip=1))

    def launch(self, copy):
        copy.start()
        self.started.append(copy)

    def begin_far(self):
        for dz in range(1, self.place.deep):
            self.launch(self.far(dz))

    def begin_near(self):
        for dxy in range(1, 4):
            self.launch(self.near(0, dxy))
        self.launch(self.across(0, 0))

    def relay_far(self):
        for dz in range(1, self.place.deep):
            self.far(dz).wait_recv()
            for dxy in range(1, 4):
                self.launch(self.near(dz, dxy))
            self.launch(self.across(dz, 0))

    def relay_near(self, low, high):
        for dz in range(low, high):
            for dxy in range(1, 4):
                self.near(dz, dxy).wait_recv()
                self.launch(self.across(dz, dxy))

    def arrive(self):
        for dz in range(self.place.deep):
            for dxy in range(4):
                self.across(dz, dxy).wait_recv()

    def drain(self):
        deep = self.place.deep
        for dz in range(1, deep):
            self.far(dz).wait_send()
        for dz in range(deep):
            for dxy in range(1, 4):
                self.near(dz, dxy).wait_send()
        for dz in range(deep):
            for dxy in range(4):
                self.across(dz, dxy).wait_send()


def small_tile(vectors, long):
    wide = lambda v: jnp.concatenate([v, jnp.zeros((1, 128 - v.shape[1]), F32)], axis=1)
    long = long.astype(F32).reshape(1, -1)
    lines = [wide(v.astype(F32).reshape(1, -1)) for v in vectors]
    lines += [wide(long[:, 16 * c : 16 * c + 16]) for c in range(4)]
    lines.append(jnp.zeros((128 - len(lines), 128), F32))
    return jnp.concatenate(lines, axis=0).T[:16].astype(BF16)


def small_lines(tiles):
    width = 16 * tiles.shape[0]
    columns = tiles.reshape(width, 128).astype(F32).T
    quarters = width // 128
    rows = [
        jnp.concatenate(
            [columns[8 + c : 9 + c, 128 * j : 128 * j + 128] for c in range(4)], axis=1
        )
        for j in range(quarters)
    ]
    rows.append(jnp.zeros((8 - quarters, width), F32))
    source = lax.broadcasted_iota(jnp.int32, (width, width), 0)
    target = lax.broadcasted_iota(jnp.int32, (width, width), 1)
    goal = source // 16 % 8 * 64 + source // 128 * 16 + source % 16
    moved = jnp.where(goal == target, 1.0, 0.0).astype(BF16)
    long = dot(jnp.concatenate(rows, axis=0).astype(BF16), moved, NN)
    return jnp.concatenate([long, columns[:8]], axis=0)


def matrix(table, first, count=16):
    part = table[:, first : first + count, :]
    return part.reshape(part.shape[0] * count, part.shape[2])


def attend_kernel(frames, mesh_shape, *refs):
    x_in = refs[0]
    if mesh_shape is None:
        table, small_ref = refs[1:3]
        refs = refs[3:]
    else:
        wq_own, wk_own, wv_own, wo_own, wu_own, wd_own = refs[1:7]
        short_own = refs[7:16]
        refs = refs[16:]
    outputs, refs = refs[:6], refs[6:]
    if mesh_shape is not None:
        small_ref, first_ref, second_ref = refs[:3]
        refs = refs[3:]
    results, refs = refs[:6], refs[6:]
    qa_ref, ka_ref, vt_ref, ht_ref, ot_ref, qe_ref = results
    x_ref, units, rows_low, scores, peaks, key_ext, log_rows, load, store = refs[:9]
    padded, width = units.shape
    depth = width // HEADS
    read = pltpu.make_async_copy(x_in, x_ref, load)
    read.start()

    def unit_rows():
        read.wait()
        for start in range(0, padded, ROWS):
            count = min(ROWS, frames - start)
            units[start : start + count, :] = normalize(
                x_ref[start : start + count, :].astype(F32)
            )[0]
        units[frames:, :] = jnp.zeros((padded - frames, width), F32)

    if mesh_shape is None:
        unit_rows()
    else:
        table_a, table_b, own, *sems, keep = refs[9:]
        place = Place(mesh_shape)
        place.greet()
        part_a = Spread(place, table_a.at[place.me], table_a, *sems[0:2])
        part_b = Spread(place, table_b.at[place.me], table_b, *sems[2:4])
        second = Spread(place, own, second_ref, *sems[4:6])
        early = EARLY_HEADS * depth
        if early > 128:
            table_a[place.me, 48:64, 128:] = jnp.zeros((16, early - 128), BF16)
        for i, weight_own in enumerate((wq_own, wk_own, wv_own)):
            table_a[place.me, 16 * i : 16 * i + 16, :] = weight_own[:, :early]
            table_b[place.me, 16 * i : 16 * i + 16, :] = weight_own[:, early:]
        table_a[place.me, 48:64, 0:128] = small_tile(
            [ref[...] for ref in short_own[:8]], short_own[8][...]
        )
        place.meet()
        part_a.begin_far()
        part_a.begin_near()
        own[0:16, :] = wo_own[...]
        chunks = wu_own.shape[1] // FF_CHUNK
        for j in range(chunks):
            own[16 + 16 * j : 32 + 16 * j, :] = wu_own[:, j * FF_CHUNK : (j + 1) * FF_CHUNK]
        own[16 + 16 * chunks :, :] = wd_own[...]
        unit_rows()
        part_a.relay_far()
        part_b.begin_far()
        part_a.relay_near(0, place.deep)
        part_b.begin_near()
        second.begin_far()
        second.begin_near()
        keep_own = pltpu.make_async_copy(own, second_ref.at[place.me], keep.at[0])
        keep_own.start()
        part_a.arrive()
        keep_a = pltpu.make_async_copy(
            table_a.at[:, 0:48], first_ref.at[:, :, pl.ds(0, early)], keep.at[1]
        )
        keep_a.start()
        keep_b = pltpu.make_async_copy(
            table_b, first_ref.at[:, :, pl.ds(early, width - early)], keep.at[2]
        )
        small_ref[...] = small_lines(table_a[:, 48:64, 0:128])

    writes = [
        pltpu.make_async_copy(results[i], outputs[i], store.at[i]) for i in (0, 1, 2, 3)
    ]
    last_write = pltpu.make_async_copy(qe_ref, outputs[5], store.at[4])

    def head_write(head):
        rows = pl.ds(pl.multiple_of(head * depth, depth), depth)
        return pltpu.make_async_copy(ot_ref.at[rows], outputs[4].at[rows], store.at[5 + head])

    bq, bv, gain, shift = (small_ref[r : r + 1, :] for r in (8, 9, 12, 13))

    def project(heads, i, carry):
        low, high = heads
        lanes = slice(low * depth, high * depth)

        def weight(which):
            if mesh_shape is None:
                return matrix(table[:, :, lanes], 16 * which)
            return matrix(table_a if low == 0 else table_b, 16 * which)

        rows = pl.ds(pl.multiple_of(i * ROWS, ROWS), ROWS)
        if low == 0:
            h1 = (units[rows, :] * gain + shift).astype(BF16)
            rows_low[rows, :] = h1
            ht_ref[:, rows] = h1.T
        else:
            h1 = rows_low[rows, :]
        q = (dot(h1, weight(0), NN) + bq[:, lanes]).astype(BF16)
        k = dot(h1, weight(1), NN).astype(BF16).astype(F32)
        k = k * (LOG2E / math.sqrt(depth))
        v = (dot(h1, weight(2), NN) + bv[:, lanes]).astype(BF16)
        k_high = k.astype(BF16)
        k_low = (k - k_high.astype(F32)).astype(BF16)
        vt_ref[lanes, rows] = v.T
        for h in range(low, high):
            cols = slice((h - low) * depth, (h - low + 1) * depth)
            qa_ref[h, rows, :] = jnp.concatenate([q[:, cols], q[:, cols]], axis=1)
            ka_ref[h, rows, :] = jnp.concatenate([k_high[:, cols], k_low[:, cols]], axis=1)
        return carry

    lax.fori_loop(0, padded // ROWS, functools.partial(project, (0, EARLY_HEADS)), 0)

    def project_rest():
        if mesh_shape is not None:
            part_b.arrive()
            keep_b.start()
        lax.fori_loop(0, padded // ROWS, functools.partial(project, (EARLY_HEADS, HEADS)), 0)
        for copy in writes:
            copy.start()

    blocks = padded // QUERIES
    steps = HEADS * blocks
    lane = lax.broadcasted_iota(jnp.int32, (QUERIES, 128), 1)
    query_ext = jnp.where(lane % 16 == 0, 1.0, 0.0).astype(BF16)

    def score(step, slot):
        head = step // blocks
        rows = pl.ds(pl.multiple_of((step % blocks) * QUERIES, QUERIES), QUERIES)
        key_ext[slot] = key_extra(head, padded, frames)
        left = jnp.concatenate([ka_ref[head], key_ext[slot]], axis=1)
        right = jnp.concatenate([qa_ref[head, rows, :], query_ext], axis=1)
        s = dot(left, right, NT)
        scores[slot] = s
        peaks[slot] = jnp.max(s, axis=0, keepdims=True)

    def finish(step, slot):
        head = step // blocks
        cols = pl.ds(pl.multiple_of((step % blocks) * QUERIES, QUERIES), QUERIES)
        peak = peaks[slot]
        weights = jnp.exp2(scores[slot] - peak).astype(BF16)
        rows = pl.ds(pl.multiple_of(head * depth, depth), depth)
        ones = jnp.ones((16, padded), BF16)
        mixed = dot(jnp.concatenate([vt_ref[rows, :], ones], axis=0), weights, NN)
        total = mixed[depth : depth + 1, :]
        ot_ref[rows, cols] = (mixed[:depth, :] * (1.0 / total)).astype(BF16)
        log_rows[head, :, cols] = peak + jnp.log2(total)

    score(0, 0)

    def pair(i, carry):
        if mesh_shape is not None:
            pl.when(i == B_FAR_AT)(part_b.relay_far)
            pl.when(i == B_NEAR_AT)(functools.partial(part_b.relay_near, 0, place.deep))
            pl.when(i == FAR_AT)(second.relay_far)
            pl.when(i == NEAR_AT)(functools.partial(second.relay_near, 0, 2))
        pl.when(i == EARLY_HEADS - 1)(project_rest)
        score(i * 2 + 1, 1)
        finish(i * 2, 0)
        score(jnp.minimum(i * 2 + 2, steps - 1), 0)
        finish(i * 2 + 1, 1)
        head_write(i).start()
        return carry

    lax.fori_loop(0, steps // 2, pair, 0)

    def extend(i, carry):
        rows = pl.ds(pl.multiple_of(i * ROWS, ROWS), ROWS)
        pieces = []
        for h in range(HEADS):
            high, middle, low = in_three(-log_rows[h, :, rows])
            pieces += [jnp.ones((1, ROWS), F32), high, middle, low, jnp.zeros((12, ROWS), F32)]
        qe_ref[rows, :] = jnp.concatenate(pieces, axis=0).T.astype(BF16)
        return carry

    if mesh_shape is not None:
        second.relay_near(2, place.deep)
    lax.fori_loop(0, padded // ROWS, extend, 0)
    last_write.start()
    for copy in writes + [last_write] + [head_write(head) for head in range(HEADS)]:
        copy.wait()
    if mesh_shape is not None:
        second.arrive()
        keep_own.wait()
        keep_a.wait()
        keep_b.wait()
        part_a.drain()
        part_b.drain()
        second.drain()


def attend(mesh_shape, x, *rest):
    frames, width = x.shape
    padded = -(-frames // QUERIES) * QUERIES
    blocks = width // 16
    vmem = pl.BlockSpec(memory_space=pltpu.VMEM)
    hbm = pl.BlockSpec(memory_space=pltpu.HBM)
    out_shape = [
        jax.ShapeDtypeStruct((HEADS, padded, 128), BF16),
        jax.ShapeDtypeStruct((HEADS, padded, 128), BF16),
        jax.ShapeDtypeStruct((width, padded), BF16),
        jax.ShapeDtypeStruct((width, padded), BF16),
        jax.ShapeDtypeStruct((width, padded), BF16),
        jax.ShapeDtypeStruct((padded, 128), BF16),
    ]
    scratch = [pltpu.VMEM(shape.shape, shape.dtype) for shape in out_shape]
    scratch += [
        pltpu.VMEM((frames, width), BF16),
        pltpu.VMEM((padded, width), F32),
        pltpu.VMEM((padded, width), BF16),
        pltpu.VMEM((2, padded, QUERIES), F32),
        pltpu.VMEM((2, 1, QUERIES), F32),
        pltpu.VMEM((2, padded, 128), BF16),
        pltpu.VMEM((HEADS, 1, padded), F32),
        pltpu.SemaphoreType.DMA,
        pltpu.SemaphoreType.DMA((5 + HEADS,)),
    ]
    out_specs = [hbm] * 6
    options = {}
    if mesh_shape is not None:
        early = EARLY_HEADS * (width // HEADS)
        hidden = rest[4].shape[1]
        own_rows = 16 + hidden // FF_CHUNK * 16 + rest[5].shape[0]
        out_shape += [
            jax.ShapeDtypeStruct((16, width), F32),
            jax.ShapeDtypeStruct((blocks, 48, width), BF16),
            jax.ShapeDtypeStruct((blocks, own_rows, width), BF16),
        ]
        out_specs += [vmem, hbm, hbm]
        scratch += [
            pltpu.VMEM((blocks, 64, early), BF16),
            pltpu.VMEM((blocks, 48, width - early), BF16),
            pltpu.VMEM((own_rows, width), BF16),
        ]
        scratch += [pltpu.SemaphoreType.DMA((blocks - 1,)) for _ in range(6)]
        scratch += [pltpu.SemaphoreType.DMA((3,))]
        options = dict(collective_id=0, has_side_effects=True)
    return pl.pallas_call(
        functools.partial(attend_kernel, frames, mesh_shape),
        out_shape=out_shape,
        in_specs=[hbm] + [vmem] * len(rest),
        out_specs=out_specs,
        scratch_shapes=scratch,
        compiler_params=pltpu.CompilerParams(vmem_limit_bytes=60 << 20, **options),
        name="attend",
    )(x, *rest)


def mlp_kernel(
    frames,
    flag_ref,
    x_ref,
    cot_ref,
    ot_ref,
    table_in,
    vec_ref,
    out_ref,
    dx_ref,
    do_ref,
    de_ref,
    grads_out,
    small_ref,
    gwo,
    gwu,
    gwd,
    table,
    grads_ref,
    load,
    store,
):
    step = pl.program_id(0)
    rows, width = x_ref.shape
    chunks = gwu.shape[0]
    depth = width // HEADS
    down = table.shape[1] - 16 - 16 * chunks
    per_chunk = FF_CHUNK // down

    def up_part(j):
        return matrix(table, 16 + 16 * j)

    def down_part(j):
        part = table[j * per_chunk : (j + 1) * per_chunk, 16 + 16 * chunks :, :]
        return part.reshape(FF_CHUNK, width)

    bounds = (0, 16, 16 + 16 * chunks, table.shape[1])
    loads = [
        pltpu.make_async_copy(table_in.at[:, low:high], table.at[:, low:high], load.at[i])
        for i, (low, high) in enumerate(zip(bounds, bounds[1:]))
    ]

    @pl.when(step == 0)
    def _():
        for copy in loads:
            copy.start()
        small_ref[...] = jnp.zeros_like(small_ref)
        loads[0].wait()

    def kept(ref, *index):
        return jnp.where(step == 0, 0.0, ref[index] if index else ref[...])

    flag = flag_ref[0].astype(F32)
    inside = step * rows + lax.broadcasted_iota(jnp.int32, (rows, width), 0) < frames
    x = jnp.where(inside, x_ref[...].astype(F32), 0.0)
    dy = jnp.where(inside, cot_ref[...].astype(F32), 0.0) * flag
    dy_low = dy.astype(BF16)
    bo, bd, gain, shift = (vec_ref[r : r + 1, :] for r in (10, 11, 14, 15))
    wo = matrix(table, 0)
    ot = ot_ref[...]
    o = ot.T
    x1 = x + (dot(o, wo, NN) + bo)
    unit, inv_std = normalize(x1)
    h2 = (unit * gain + shift).astype(BF16)
    h2t = h2.T

    @pl.when(step == 0)
    def _():
        loads[1].wait()
        loads[2].wait()

    z_next = dot(h2, up_part(0), NN)
    out = x1 + bd
    dh2 = jnp.zeros((rows, width), F32)
    for j in range(chunks):
        z = z_next + vec_ref[j : j + 1, :]
        if j + 1 < chunks:
            z_next = dot(h2, up_part(j + 1), NN)
        dg = dot(dy_low, down_part(j), NT)
        g, slope = gelu_and_slope(z)
        g = g.astype(BF16)
        dz = (dg * slope).astype(BF16)
        out = out + dot(g, down_part(j), NN)
        gwd[j] = kept(gwd, j) + dot(g, dy_low, TN)
        gwu[j] = kept(gwu, j) + dot(h2t, dz, NN)
        small_ref[j : j + 1, :] += column_sums(dz.astype(F32))
        dh2 = dh2 + dot(dz, up_part(j), NT)
    store_rows(out_ref, 0, out * flag)
    dx1 = dy + normalize_back(dh2, unit, inv_std, gain)
    dx_ref[...] = dx1
    da = dx1.astype(BF16)
    gwo[...] = kept(gwo) + dot(ot, da, NN)
    do = dot(da, wo, NT).astype(BF16)
    small_ref[10:11, :] += column_sums(da.astype(F32))
    small_ref[11:12, :] += column_sums(dy)
    small_ref[14:15, :] += column_sums(dh2 * unit)
    small_ref[15:16, :] += column_sums(dh2)
    do_ref[...] = do
    prod = do.astype(F32) * o.astype(F32)
    high = prod.astype(BF16)
    low = (prod - high.astype(F32)).astype(BF16)
    owner = lax.broadcasted_iota(jnp.int32, (width, 128), 0) // depth
    pick = lax.broadcasted_iota(jnp.int32, (width, 128), 1) // 16
    pick = jnp.where(owner == pick, 1.0, 0.0).astype(BF16)
    high, middle, low = in_three(-(dot(high, pick, NN) + dot(low, pick, NN)))
    lane = lax.broadcasted_iota(jnp.int32, (rows, 128), 1) % 16
    extra = jnp.where(lane == 1, middle, jnp.where(lane == 2, low, 0.0))
    de_ref[...] = jnp.where(lane == 0, high, extra).astype(BF16)

    @pl.when(step == pl.num_programs(0) - 1)
    def _():
        split = lambda part, count: part.astype(BF16).reshape(-1, count, width)
        copies = []

        def send(*index):
            copies.append(
                pltpu.make_async_copy(
                    grads_ref.at[index], grads_out.at[index], store.at[len(copies)]
                )
            )
            copies[-1].start()

        for j in range(chunks):
            rows_up = slice(16 + 16 * j, 32 + 16 * j)
            grads_ref[:, rows_up, :] = split(gwu[j], 16)
            send(slice(None), rows_up)
            blocks_down = slice(j * per_chunk, (j + 1) * per_chunk)
            rows_down = slice(16 + 16 * chunks, table.shape[1])
            grads_ref[blocks_down, rows_down, :] = split(gwd[j], down)
            send(blocks_down, rows_down)
        grads_ref[:, 0:16, :] = split(gwo[...], 16)
        send(slice(None), slice(0, 16))
        for copy in copies:
            copy.wait()


def mlp(flag, x, cot, ot, table, vectors):
    frames, width = x.shape
    padded = ot.shape[1]
    blocks, rows = table.shape[:2]
    chunks = (rows - 16) * blocks // (2 * FF_CHUNK)
    by_rows = pl.BlockSpec((MLP_ROWS, width), lambda i: (i, 0))
    fixed = lambda shape: pl.BlockSpec(
        shape, lambda i: (0,) * len(shape), pipeline_mode=pl.Buffered(1)
    )
    return pl.pallas_call(
        functools.partial(mlp_kernel, frames),
        grid=(padded // MLP_ROWS,),
        out_shape=[
            jax.ShapeDtypeStruct((frames * width // 128, 128), F32),
            jax.ShapeDtypeStruct((frames, width), F32),
            jax.ShapeDtypeStruct((padded, width), BF16),
            jax.ShapeDtypeStruct((padded, 128), BF16),
            jax.ShapeDtypeStruct(table.shape, BF16),
            jax.ShapeDtypeStruct((16, width), F32),
        ],
        in_specs=[
            pl.BlockSpec(memory_space=pltpu.SMEM),
            by_rows,
            by_rows,
            pl.BlockSpec((width, MLP_ROWS), lambda i: (0, i)),
            pl.BlockSpec(memory_space=pltpu.HBM),
            fixed((16, width)),
        ],
        out_specs=[
            pl.BlockSpec((MLP_ROWS * width // 128, 128), lambda i: (i, 0)),
            by_rows,
            by_rows,
            pl.BlockSpec((MLP_ROWS, 128), lambda i: (i, 0)),
            pl.BlockSpec(memory_space=pltpu.HBM),
            fixed((16, width)),
        ],
        scratch_shapes=[
            pltpu.VMEM((width, width), F32),
            pltpu.VMEM((chunks, width, FF_CHUNK), F32),
            pltpu.VMEM((chunks, FF_CHUNK, width), F32),
            pltpu.VMEM(table.shape, BF16),
            pltpu.VMEM(table.shape, BF16),
            pltpu.SemaphoreType.DMA((3,)),
            pltpu.SemaphoreType.DMA((2 * chunks + 1,)),
        ],
        compiler_params=pltpu.CompilerParams(
            vmem_limit_bytes=60 << 20, dimension_semantics=("arbitrary",)
        ),
        name="mlp",
    )(flag, x, cot, ot, table, vectors)


class Gather:
    def __init__(self, place, source, from_core, halves, from_near, quarter, from_far, sems):
        self.place, self.source = place, source
        self.from_core, self.halves = from_core, halves
        self.from_near, self.quarter = from_near, quarter
        self.from_far = from_far
        self.send_sem, self.recv_sem = sems

    def copy(self, slot, src, dst, device):
        return pltpu.make_async_remote_copy(
            src_ref=src,
            dst_ref=dst,
            send_sem=self.send_sem.at[slot],
            recv_sem=self.recv_sem.at[slot],
            device_id=device,
            device_id_type=MESH,
        )

    def across(self):
        place = self.place
        return [
            self.copy(
                z, self.source.at[z, :, 1 - place.core], self.from_core.at[z], place.moved(flip=1)
            )
            for z in range(place.deep)
        ]

    def near(self):
        place = self.place
        copies = []
        for dxy in range(1, 4):
            b, s = place.moved(dxy=dxy)
            square = b % 2 * 2 + s // 2
            copies.append(
                self.copy(
                    place.deep + dxy - 1,
                    self.halves.at[:, square],
                    self.from_near.at[dxy - 1],
                    (b, s),
                )
            )
        return copies

    def far(self):
        place = self.place
        copies = []
        for dz in range(1, place.deep):
            z = (place.z + dz) % place.deep
            copies.append(
                self.copy(
                    place.deep + 2 + dz,
                    self.quarter.at[z],
                    self.from_far.at[dz - 1],
                    place.moved(dz=dz),
                )
            )
        return copies

    def fold_across(self, own):
        for copy in self.across():
            copy.wait_recv()

        def one(i, carry):
            z, q = i // 4, i % 4
            total = own(z, q).astype(F32) + self.from_core[z, q].astype(F32)
            self.halves[z, q] = total.astype(BF16)
            return carry

        lax.fori_loop(0, self.place.deep * 4, one, 0)
        for copy in self.near():
            copy.start()

    def fold_near(self):
        for copy in self.near():
            copy.wait_recv()

        def one(z, carry):
            total = self.halves[z, self.place.square].astype(F32)
            for dxy in range(3):
                total = total + self.from_near[dxy, z].astype(F32)
            self.quarter[z] = total.astype(BF16)
            return carry

        lax.fori_loop(0, self.place.deep, one, 0)
        for copy in self.far():
            copy.start()

    def result(self):
        for copy in self.far():
            copy.wait_recv()
        total = self.quarter[self.place.z].astype(F32)
        for dz in range(self.place.deep - 1):
            total = total + self.from_far[dz].astype(F32)
        return total

    def drain(self):
        for copy in self.across() + self.near() + self.far():
            copy.wait_send()


class SmallSum:
    def __init__(self, place, buffers, received, sems):
        self.place, self.buffers, self.received = place, buffers, received
        self.send_sem, self.recv_sem = sems

    def copies(self, stage):
        place = self.place
        if stage == 0:
            devices, first = [place.moved(flip=1)], 0
        elif stage == 1:
            devices, first = [place.moved(dxy=dxy) for dxy in range(1, 4)], 1
        else:
            devices, first = [place.moved(dz=dz) for dz in range(1, place.deep)], 4
        return [
            pltpu.make_async_remote_copy(
                src_ref=self.buffers.at[stage],
                dst_ref=self.received.at[first + i],
                send_sem=self.send_sem.at[first + i],
                recv_sem=self.recv_sem.at[first + i],
                device_id=device,
                device_id_type=MESH,
            )
            for i, device in enumerate(devices)
        ]

    def send(self, stage, value):
        self.buffers[stage] = value
        for copy in self.copies(stage):
            copy.start()

    def receive(self, stage):
        total = self.buffers[stage]
        first = (0, 1, 4)[stage]
        for i, copy in enumerate(self.copies(stage)):
            copy.wait_recv()
            total = total + self.received[first + i]
        return total

    def drain(self):
        for stage in range(3):
            for copy in self.copies(stage):
                copy.wait_send()


def own_small(total, place):
    width = total.shape[1]
    line = lax.broadcasted_iota(jnp.int32, total.shape, 0)
    short = pltpu.roll(total, width - place.me * 16, 1)
    long = jnp.sum(jnp.where(line == place.me // 8, total, 0.0), axis=0, keepdims=True)
    long = pltpu.roll(jnp.broadcast_to(long, total.shape), width - place.me % 8 * 64, 1)
    return jnp.where(line == 0, long, short)[:, :128]


def attend_back_kernel(frames, mesh_shape, *refs):
    x_in, dx_in, qa_in, ka_in, vt_in, ht_in, qe_in, do_in, de_in, table_in = refs[:10]
    vec_ref, small_in = refs[10:12]
    refs = refs[12:]
    if mesh_shape is None:
        dinput_out, source, small_ref = refs[:3]
        refs = refs[3:]
    else:
        grads_ref = refs[0]
        dinput_out, gq_ref, gk_ref, gv_ref, go_ref, gu_ref, gd_ref = refs[1:8]
        short_refs = refs[8:17]
        refs = refs[17:]
    x_ref, dx_ref, qa_ref, ka_ref, vt_ref, ht_ref, qe_ref, do_ref, de_ref, table = refs[:10]
    dinput_ref, load, store = refs[10:13]
    dq, dkt, dvt, sum_k, sum_v, key_ext, value_ext, small = refs[13:21]
    refs = refs[21:]

    padded = qa_ref.shape[1]
    width = ht_ref.shape[0]
    depth = width // HEADS

    def head_loads(head):
        return [
            pltpu.make_async_copy(qa_in.at[head], qa_ref.at[head], load.at[2 * head]),
            pltpu.make_async_copy(ka_in.at[head], ka_ref.at[head], load.at[2 * head + 1]),
        ]

    sources = (vt_in, do_in, de_in, qe_in, ht_in, table_in.at[:, 0:48], x_in, dx_in)
    targets = (vt_ref, do_ref, de_ref, qe_ref, ht_ref, table, x_ref, dx_ref)
    loads = [
        pltpu.make_async_copy(source_ref, target_ref, load.at[2 * HEADS + i])
        for i, (source_ref, target_ref) in enumerate(zip(sources, targets))
    ]
    for copy in head_loads(0) + loads[:4]:
        copy.start()
    for head in range(1, HEADS):
        for copy in head_loads(head):
            copy.start()
    for copy in loads[4:]:
        copy.start()

    if mesh_shape is not None:
        place = Place(mesh_shape)
        place.greet()
        parts = []
        for _ in PARTS:
            parts.append(Gather(place, refs[0], *refs[1:6], refs[6:8]))
            refs = refs[8:]
        second = Gather(place, grads_ref, *refs[:5], refs[5:7])
        shorts = SmallSum(place, refs[7], refs[8], refs[9:11])
        second_half, keep = refs[11:]
        keep_half = pltpu.make_async_copy(grads_ref.at[:, :, place.core], second_half, keep)
        place.meet()
        for copy in second.across():
            copy.start()
        keep_half.start()
    for copy in loads[:4]:
        copy.wait()

    def second_across():
        keep_half.wait()
        second.fold_across(lambda z, q: second_half[z, q])

    lane_half = lax.broadcasted_iota(jnp.int32, (padded, 128), 1) < depth

    def weight_grads(t):
        low, high = PARTS[t]
        cols = slice(low * depth, high * depth)
        wide = (high - low) * depth
        queries = jnp.concatenate(
            [jnp.where(lane_half, dq[h], dq[h + 1]) for h in range(low, high, 2)], axis=1
        )
        ht = ht_ref[...]
        grads = (
            dot(ht, queries, NN),
            dot(ht, dkt[cols, :], NT),
            dot(ht, dvt[cols, :], NT),
        )
        for i, grad in enumerate(grads):
            grad = grad.astype(BF16)
            if mesh_shape is None:
                source[:, 16 * i : 16 * i + 16, cols] = grad.reshape(-1, 16, wide)
            else:
                target = parts[t].source
                target[:, :, :, 16 * i : 16 * i + 16, :] = grad.reshape(
                    target.shape[:3] + (16, wide)
                )
        if mesh_shape is not None:
            for copy in parts[t].across():
                copy.start()

    def fold_part(t):
        parts[t].fold_across(lambda z, q: parts[t].source[z, q, place.core])

    def part_result(t):
        total = parts[t].result()
        for i, ref in enumerate((gq_ref, gk_ref, gv_ref)):
            ref[:, PARTS[t][0] * depth : PARTS[t][1] * depth] = total[16 * i : 16 * i + 16]

    def early_weight_grads(t):
        if t == 0:
            loads[4].wait()
        weight_grads(t)

    last = len(PARTS) - 1

    def one_head(head, carry):
        for t in range(last):
            pl.when(head == PARTS[t][1])(functools.partial(early_weight_grads, t))
            if mesh_shape is not None and PARTS[t][1] + 1 < HEADS:
                pl.when(head == PARTS[t][1] + 1)(functools.partial(fold_part, t))
        if mesh_shape is not None:
            pl.when(head == ACROSS_AT)(second_across)
            pl.when(head == SQUARE_AT)(second.fold_near)
        for copy in head_loads(head):
            copy.wait()
        key_ext[...] = key_extra(head, padded, frames)
        line = lax.broadcasted_iota(jnp.int32, (128, padded), 0)
        mine = pl.ds(pl.multiple_of(head // 2 * 128, 128), 128)
        values = jnp.where(line // depth == head % 2, vt_ref[mine, :].astype(F32), 0.0)
        value_ext[0:128, :] = values.astype(BF16)
        extra = jnp.where((line // 16 == head) & (line % 16 < 3), 1.0, 0.0)
        value_ext[128:256, :] = extra.astype(BF16)
        for i in range(padded // ROWS):
            rows = slice(i * ROWS, (i + 1) * ROWS)
            q = qa_ref[head, rows, :]
            d = do_ref[rows, mine]
            turned = d.T
            turned = jnp.where(head % 2 == 0, turned[:depth], turned[depth:])
            s = dot(
                jnp.concatenate([q, qe_ref[rows, :]], axis=1),
                jnp.concatenate([ka_ref[head], key_ext[...]], axis=1),
                NT,
            )
            p = jnp.exp2(s)
            dp = dot(jnp.concatenate([d, de_ref[rows, :]], axis=1), value_ext[...], NN)
            ds = (p * dp).astype(BF16)
            p = p.astype(BF16)
            new_v = dot(turned, p, NN)
            new_k = dot(q[:, :depth], ds, TN)
            if i == 0:
                sum_v[...] = new_v
                sum_k[...] = new_k
            else:
                sum_v[...] += new_v
                sum_k[...] += new_k
            both = dot(ds, ka_ref[head], NN)
            both = both + pltpu.roll(both, depth, 1)
            dq[head, rows, :] = (both * LN2).astype(BF16)
        out_rows = pl.ds(pl.multiple_of(head * depth, depth), depth)
        dkt[out_rows, :] = (sum_k[...] * (1.0 / math.sqrt(depth))).astype(BF16)
        dvt[out_rows, :] = sum_v[...].astype(BF16)
        return carry

    lax.fori_loop(0, HEADS, one_head, 0)

    weight_grads(last)
    for copy in loads[5:]:
        copy.wait()
    if mesh_shape is not None:
        for t in range(last):
            if PARTS[t][1] + 1 >= HEADS:
                fold_part(t)
            else:
                parts[t].fold_near()
        second_own = second.result()
        chunks = gu_ref.shape[1] // FF_CHUNK
        go_ref[...] = second_own[0:16]
        for j in range(chunks):
            gu_ref[:, j * FF_CHUNK : (j + 1) * FF_CHUNK] = second_own[16 + 16 * j : 32 + 16 * j]
        gd_ref[...] = second_own[16 + 16 * chunks :]

    gain = vec_ref[12:13, :]
    small[...] = small_in[...]
    stores = []
    for index, start in enumerate(range(0, frames, ROWS)):
        if mesh_shape is not None and index == FOLD_AT:
            fold_part(last)
            for t in range(last):
                if PARTS[t][1] + 1 >= HEADS:
                    parts[t].fold_near()
        count = min(ROWS, frames - start)
        rows = slice(start, start + count)
        wide = slice(start, start + ROWS)
        some = lane_half[:ROWS]
        dq_rows = jnp.concatenate(
            [jnp.where(some, dq[h, wide, :], dq[h + 1, wide, :]) for h in range(0, HEADS, 2)],
            axis=1,
        )
        dk_rows = dkt[:, wide].T
        dv_rows = dvt[:, wide].T
        dh1 = (
            dot(dq_rows, matrix(table, 0), NT)
            + dot(dk_rows, matrix(table, 16), NT)
            + dot(dv_rows, matrix(table, 32), NT)
        )
        small[8:9, :] += column_sums(dq_rows.astype(F32))
        small[9:10, :] += column_sums(dv_rows.astype(F32))
        dh1 = dh1[:count]
        unit, inv_std = normalize(x_ref[rows, :].astype(F32))
        small[12:13, :] += column_sums(dh1 * unit)
        small[13:14, :] += column_sums(dh1)
        dinput = dx_ref[rows, :] + normalize_back(dh1, unit, inv_std, gain)
        store_rows(dinput_ref, start, dinput)
        part = pl.ds(start * (width // 128), count * (width // 128))
        stores.append(
            pltpu.make_async_copy(dinput_ref.at[part], dinput_out.at[part], store.at[index])
        )
        stores[-1].start()
    if mesh_shape is None:
        small_ref[...] = small[...]
    else:
        shorts.send(0, small[...])
        for t in range(last):
            part_result(t)
        shorts.send(1, shorts.receive(0))
        parts[last].fold_near()
        shorts.send(2, shorts.receive(1))
        second.drain()
        for t in range(last):
            parts[t].drain()
        part_result(last)
        small_own = own_small(shorts.receive(2), place)
        for i, ref in enumerate(short_refs[:8]):
            ref[...] = small_own[8 + i, :16]
        short_refs[8][...] = small_own[0, :64]
        parts[last].drain()
        shorts.drain()
    for copy in stores:
        copy.wait()


def attend_back(mesh_shape, x, dx, qa, ka, vt, ht, qe, do, de, table, vectors, small, grads):
    frames, width = x.shape
    padded = ht.shape[1]
    blocks = width // 16
    vmem = pl.BlockSpec(memory_space=pltpu.VMEM)
    hbm = pl.BlockSpec(memory_space=pltpu.HBM)
    args = [x, dx, qa, ka, vt, ht, qe, do, de, table, vectors, small]
    in_specs = [hbm] * 10 + [vmem] * 2
    lines = frames * width // 128
    out_shape = [jax.ShapeDtypeStruct((lines, 128), F32)]
    scratch = [pltpu.VMEM(array.shape, array.dtype) for array in args[:9]]
    scratch += [
        pltpu.VMEM((blocks, 48, width), BF16),
        pltpu.VMEM((lines, 128), F32),
        pltpu.SemaphoreType.DMA((2 * HEADS + 8,)),
        pltpu.SemaphoreType.DMA((padded // ROWS,)),
        pltpu.VMEM((HEADS, padded, 128), BF16),
        pltpu.VMEM((width, padded), BF16),
        pltpu.VMEM((width, padded), BF16),
        pltpu.VMEM((width // HEADS, padded), F32),
        pltpu.VMEM((width // HEADS, padded), F32),
        pltpu.VMEM((padded, 128), BF16),
        pltpu.VMEM((256, padded), BF16),
        pltpu.VMEM((16, width), F32),
    ]
    options = {}
    if mesh_shape is None:
        out_shape += [
            jax.ShapeDtypeStruct((blocks, 48, width), BF16),
            jax.ShapeDtypeStruct((16, width), F32),
        ]
    else:
        deep = mesh_shape[0] // 2
        rows = grads.shape[1]
        hidden = (rows - 16) * blocks // 2
        args.append(grads.reshape(deep, 4, 2, rows, width))
        in_specs.append(hbm)
        out_shape += [
            jax.ShapeDtypeStruct((16, width), F32),
            jax.ShapeDtypeStruct((16, width), F32),
            jax.ShapeDtypeStruct((16, width), F32),
            jax.ShapeDtypeStruct((16, width), F32),
            jax.ShapeDtypeStruct((16, hidden), F32),
            jax.ShapeDtypeStruct((hidden // blocks, width), F32),
        ]
        out_shape += [jax.ShapeDtypeStruct((16,), F32)] * 8
        out_shape += [jax.ShapeDtypeStruct((hidden // blocks,), F32)]

        def stages(shape):
            return [
                pltpu.VMEM((deep, 4) + shape, BF16),
                pltpu.VMEM((deep, 4) + shape, BF16),
                pltpu.VMEM((3, deep) + shape, BF16),
                pltpu.VMEM((deep,) + shape, BF16),
                pltpu.VMEM((deep - 1,) + shape, BF16),
                pltpu.SemaphoreType.DMA((2 * deep + 2,)),
                pltpu.SemaphoreType.DMA((2 * deep + 2,)),
            ]

        for low, high in PARTS:
            shape = (48, (high - low) * (width // HEADS))
            scratch += [pltpu.VMEM((deep, 4, 2) + shape, BF16)] + stages(shape)
        scratch += stages((rows, width))
        scratch += [
            pltpu.VMEM((3, 16, width), F32),
            pltpu.VMEM((deep + 3, 16, width), F32),
            pltpu.SemaphoreType.DMA((deep + 3,)),
            pltpu.SemaphoreType.DMA((deep + 3,)),
            pltpu.VMEM((deep, 4, rows, width), BF16),
            pltpu.SemaphoreType.DMA,
        ]
        options = dict(collective_id=1, has_side_effects=True)
    return pl.pallas_call(
        functools.partial(attend_back_kernel, frames, mesh_shape),
        out_shape=out_shape,
        in_specs=in_specs,
        out_specs=[hbm] + [vmem] * (len(out_shape) - 1),
        scratch_shapes=scratch,
        compiler_params=pltpu.CompilerParams(vmem_limit_bytes=60 << 20, **options),
        name="attend_back",
    )(*args)


def hand_over_kernel(count, *refs):
    large, small = refs[0], refs[1 : count + 1]
    large_buf, small_buf = refs[2 * count + 2], refs[2 * count + 3 : 3 * count + 3]
    large_out, small_out = refs[count + 1], refs[count + 2 : 2 * count + 2]
    sem_in, sem_out = refs[3 * count + 3 :]
    pieces = large_buf.shape[0]
    rows = large_buf.shape[1]
    sources = [large.at[pl.ds(i * rows, rows)] for i in range(pieces)] + list(small)
    buffers = [large_buf.at[i] for i in range(pieces)] + list(small_buf)
    targets = [large_out.at[pl.ds(i * rows, rows)] for i in range(pieces)] + list(small_out)
    inward = [
        pltpu.make_async_copy(source, buffer, sem_in.at[i])
        for i, (source, buffer) in enumerate(zip(sources, buffers))
    ]
    outward = [
        pltpu.make_async_copy(buffer, target, sem_out.at[i])
        for i, (buffer, target) in enumerate(zip(buffers, targets))
    ]
    for copy in inward:
        copy.start()
    for first, then in zip(inward, outward):
        first.wait()
        then.start()
    for copy in outward:
        copy.wait()


def hand_over(large, *small):
    anywhere = pl.BlockSpec(memory_space=pltpu.HBM)
    arrays = (large,) + small
    rows = large.shape[0]
    pieces = 6 if rows % 48 == 0 else 1
    return pl.pallas_call(
        functools.partial(hand_over_kernel, len(small)),
        out_shape=[jax.ShapeDtypeStruct(array.shape, array.dtype) for array in arrays],
        in_specs=[anywhere] * len(arrays),
        out_specs=[anywhere] * len(arrays),
        scratch_shapes=[pltpu.VMEM((pieces, rows // pieces) + large.shape[1:], large.dtype)]
        + [pltpu.VMEM(array.shape, array.dtype) for array in small]
        + [pltpu.SemaphoreType.DMA((len(small) + pieces,))] * 2,
        compiler_params=pltpu.CompilerParams(vmem_limit_bytes=60 << 20),
        name="hand_over",
    )(*arrays)


def staged(mesh_shape, windows, cotangent, valid, *owned):
    x, cot = windows[0], cotangent[0]
    bq, bv, bo, bu, bd, gain_one, shift_one, gain_two, shift_two = owned[6:]
    short = [bq, bv, bo, bd, gain_one, shift_one, gain_two, shift_two, bu]
    qa, ka, vt, ht, ot, qe, vectors, first, second = attend(mesh_shape, x, *owned[:6], *short)
    out, dx, do, de, grads, small = mlp(valid, x, cot, ot, second, vectors)
    results = attend_back(
        mesh_shape, x, dx, qa, ka, vt, ht, qe, do, de, first, vectors, small, grads
    )
    dinput, gq, gk, gv, go, gu, gd, *shorts = hand_over(*results)
    gbq, gbv, gbo, gbd, *gains, gbu = shorts
    return (
        out.reshape(windows.shape),
        dinput.reshape(windows.shape),
        *(gq, gk, gv, go, gu, gd, gbq, gbv, gbo, gbu, gbd),
        *gains,
    )


def collective(windows, cotangent, valid, *owned):
    axes = ("batch", "shard")
    wq, wk, wv, wo, wu, wd, bq, bv, bo, bu, bd, gain_one, shift_one, gain_two, shift_two = [
        lax.all_gather(part, axes, axis=0, tiled=True) for part in owned
    ]
    x, cot = windows[0], cotangent[0]
    width, hidden = wu.shape
    blocks, chunks = width // 16, hidden // FF_CHUNK
    split = lambda part: part.reshape(blocks, -1, width)
    vectors = jnp.concatenate(
        [jnp.pad(bu.reshape(chunks, FF_CHUNK), ((0, 8 - chunks), (0, 0)))]
        + [v[None] for v in (bq, bv, bo, bd, gain_one, shift_one, gain_two, shift_two)]
    ).astype(F32)
    first = jnp.concatenate([split(wq), split(wk), split(wv)], axis=1)
    ups = wu.reshape(blocks, 16, chunks, FF_CHUNK).transpose(0, 2, 1, 3)
    ups = ups.reshape(blocks, 16 * chunks, FF_CHUNK)
    second = jnp.concatenate([split(wo), ups, split(wd)], axis=1)
    qa, ka, vt, ht, ot, qe = attend(None, x, first, vectors)
    out, dx, do, de, grads, small = mlp(valid, x, cot, ot, second, vectors)
    dinput, first_grads, small = attend_back(
        None, x, dx, qa, ka, vt, ht, qe, do, de, first, vectors, small, None
    )
    first_grads, grads = first_grads.astype(F32), grads.astype(F32)
    joined = lambda part: part.reshape(-1, width)
    gwu = grads[:, 16 : 16 + 16 * chunks].reshape(blocks, chunks, 16, FF_CHUNK)
    gwu = gwu.transpose(0, 2, 1, 3).reshape(width, hidden)
    totals = (
        joined(first_grads[:, 0:16]),
        joined(first_grads[:, 16:32]),
        joined(first_grads[:, 32:48]),
        joined(grads[:, 0:16]),
        gwu,
        joined(grads[:, 16 + 16 * chunks :]),
        small[8],
        small[9],
        small[10],
        small[:chunks].reshape(hidden),
        small[11],
        small[12],
        small[13],
        small[14],
        small[15],
    )
    grads = [lax.psum_scatter(total, axes, scatter_dimension=0, tiled=True) for total in totals]
    return (out.reshape(windows.shape), dinput.reshape(windows.shape), *grads)


def solution(mesh):
    both = ("batch", "shard")
    windows_spec, matrix_spec, vector_spec = P(both, None, None), P(both, None), P(both)
    params = (matrix_spec,) * 6 + (vector_spec,) * 9
    mesh_shape = (mesh.shape["batch"], mesh.shape["shard"])

    def per_device(windows, cotangent, valid, *owned):
        if mesh_shape[1] == 4 and mesh_shape[0] % 2 == 0 and owned[0].shape[0] == 16:
            return staged(mesh_shape, windows, cotangent, valid, *owned)
        return collective(windows, cotangent, valid, *owned)

    return jax.shard_map(
        per_device,
        mesh=mesh,
        in_specs=(windows_spec, windows_spec, vector_spec) + params,
        out_specs=(windows_spec, windows_spec) + params,
        check_vma=False,
    )
```

```python
import functools
import math

import jax
import jax.numpy as jnp
from jax import lax
from jax.experimental import pallas as pl
from jax.experimental.pallas import tpu as pltpu
from jax.sharding import PartitionSpec as P

HEADS = 8
NORM_EPS = 1e-05
LOG2E = math.log2(math.e)
LN2 = math.log(2.0)
F32 = jnp.float32
BF16 = jnp.bfloat16
MESH = pl.DeviceIdType.MESH
ROWS = 256
MLP_ROWS = 512
PROJECT_ROWS = 768
EARLY_HEADS = 4
B_FAR_AT = 0
B_NEAR_AT = 2
FAR_AT = 2
NEAR_AT = 5
CORNER_AT = 7
FOLD_AT = 2
ACROSS_AT = 1
SQUARE_AT = 5
PARTS = ((0, 4), (4, 8))
QUERIES = 768
FF_CHUNK = 512
MASKED = -1e30

NN = (((1,), (0,)), ((), ()))
NT = (((1,), (1,)), ((), ()))
TN = (((0,), (0,)), ((), ()))

TAIL_RATE = 0.3
TAIL = (
    0.1196320072075501,
    0.12071213658889111,
    0.10017594509547065,
    0.12769178078587456,
    -0.0520340331315144,
    0.2045568015805396,
    -0.1561584571261984,
    0.03542373729935703,
)


def dot(left, right, dims):
    return lax.dot_general(left, right, dims, preferred_element_type=F32)


def normalize(values):
    centred = values - jnp.mean(values, axis=-1, keepdims=True)
    variance = jnp.mean(centred * centred, axis=-1, keepdims=True)
    inv_std = lax.rsqrt(variance + NORM_EPS)
    return centred * inv_std, inv_std


def normalize_back(grad_rows, unit_rows, inv_std, gain):
    scaled = grad_rows * gain
    first_mean = jnp.mean(scaled, axis=-1, keepdims=True)
    second_mean = jnp.mean(scaled * unit_rows, axis=-1, keepdims=True)
    return inv_std * (scaled - first_mean - unit_rows * second_mean)


def store_rows(ref, start, rows):
    count, width = rows.shape
    parts = width // 128
    for j in range(parts):
        ref[pl.ds(start * parts + j, count, stride=parts), :] = rows[:, j * 128 : (j + 1) * 128]


def column_sums(rows):
    return jnp.sum(rows, axis=0, keepdims=True)


def in_three(values):
    high = values.astype(BF16).astype(F32)
    rest = values - high
    middle = rest.astype(BF16).astype(F32)
    return high, middle, rest - middle


def gelu_and_slope(z):
    size = jnp.abs(z)
    t = 1.0 / (1.0 + TAIL_RATE * size)
    poly = jnp.full_like(t, TAIL[-1])
    for coefficient in TAIL[-2::-1]:
        poly = poly * t + coefficient
    bell = jnp.exp2(z * z * (-0.5 * LOG2E))
    tail = poly * t * bell
    cdf = jnp.where(z > 0, 1.0 - tail, tail)
    return z * cdf, cdf + z * bell * (1.0 / math.sqrt(2.0 * math.pi))


def key_extra(head, keys, frames):
    row = lax.broadcasted_iota(jnp.int32, (keys, 128), 0)
    lane = lax.broadcasted_iota(jnp.int32, (keys, 128), 1) - head * 16
    mask = jnp.where(row < frames, 0.0, MASKED)
    ones = jnp.where((lane > 0) & (lane < 4), 1.0, 0.0)
    return jnp.where(lane == 0, mask, ones).astype(BF16)


class Place:
    def __init__(self, mesh_shape):
        self.batch, self.shard = mesh_shape
        self.deep = self.batch // 2
        b, s = lax.axis_index("batch"), lax.axis_index("shard")
        self.z, self.x, self.y, self.core = b // 2, b % 2, s // 2, s % 2
        self.me = b * self.shard + s
        self.square = self.x * 2 + self.y

    def moved(self, dz=0, dxy=0, flip=0):
        dx, dy = dxy // 2, dxy % 2
        x = 1 - self.x if dx else self.x
        y = 1 - self.y if dy else self.y
        core = 1 - self.core if flip else self.core
        return (self.z + self.deep + dz) % self.deep * 2 + x, y * 2 + core

    def block(self, dz=0, dxy=0, flip=0):
        b, s = self.moved(-dz, dxy, flip)
        return b * self.shard + s

    def partners(self):
        far = [self.moved(dz=dz) for dz in range(1, self.deep)]
        near = [self.moved(dxy=dxy) for dxy in range(1, 4)]
        return far + near + [self.moved(flip=1)]

    def greet(self):
        barrier = pltpu.get_barrier_semaphore()
        for partner in self.partners():
            pl.semaphore_signal(barrier, inc=1, device_id=partner, device_id_type=MESH)

    def meet(self):
        pl.semaphore_wait(pltpu.get_barrier_semaphore(), self.deep + 3)


class Spread:
    def __init__(self, place, own, table, send_sem, recv_sem, relayed=False):
        self.place, self.own, self.table = place, own, table
        self.direct = range(1, 3) if relayed else range(1, 4)
        self.send_sem, self.recv_sem = send_sem, recv_sem
        self.started = []

    def copy(self, slot, dz, dxy, device):
        block = self.place.block(dz, dxy)
        here = dz == 0 and dxy == 0
        return pltpu.make_async_remote_copy(
            src_ref=self.own if here else self.table.at[block],
            dst_ref=self.table.at[block],
            send_sem=self.send_sem.at[slot],
            recv_sem=self.recv_sem.at[slot],
            device_id=device,
            device_id_type=MESH,
        )

    def far(self, dz):
        return self.copy(dz - 1, 0, 0, self.place.moved(dz=dz))

    def near(self, dz, dxy):
        slot = self.place.deep - 1 + dz * 3 + dxy - 1
        return self.copy(slot, dz, 0, self.place.moved(dxy=dxy))

    def across(self, dz, dxy):
        slot = self.place.deep * 4 - 1 + dz * 4 + dxy
        return self.copy(slot, dz, dxy, self.place.moved(flip=1))

    def corner(self, dz, dxy):
        count = self.table.shape[1]
        middle = -(-count // 32) * 16
        part = pl.ds(0, middle) if dxy == 2 else pl.ds(middle, count - middle)
        slot = self.place.deep - 1 + dz * 3 + 2 if dxy == 2 else self.place.deep * 8 - 1 + dz
        block = self.place.block(dz, dxy)
        return pltpu.make_async_remote_copy(
            src_ref=self.table.at[block, part],
            dst_ref=self.table.at[block, part],
            send_sem=self.send_sem.at[slot],
            recv_sem=self.recv_sem.at[slot],
            device_id=self.place.moved(dxy=3 - dxy),
            device_id_type=MESH,
        )

    def launch(self, copy):
        copy.start()
        self.started.append(copy)

    def begin_far(self):
        for dz in range(1, self.place.deep):
            self.launch(self.far(dz))

    def begin_near(self):
        for dxy in self.direct:
            self.launch(self.near(0, dxy))
        self.launch(self.across(0, 0))

    def relay_far(self):
        for dz in range(1, self.place.deep):
            self.far(dz).wait_recv()
            for dxy in self.direct:
                self.launch(self.near(dz, dxy))
            self.launch(self.across(dz, 0))

    def relay_near(self, low, high):
        for dz in range(low, high):
            for dxy in self.direct:
                self.near(dz, dxy).wait_recv()
                if 3 not in self.direct:
                    self.launch(self.corner(dz, dxy))
                self.launch(self.across(dz, dxy))

    def relay_corner(self, low, high):
        for dz in range(low, high):
            for dxy in (1, 2):
                self.corner(dz, dxy).wait_recv()
            self.launch(self.across(dz, 3))

    def arrive(self):
        for dz in range(self.place.deep):
            for dxy in range(4):
                self.across(dz, dxy).wait_recv()

    def drain(self):
        deep = self.place.deep
        for dz in range(1, deep):
            self.far(dz).wait_send()
        for dz in range(deep):
            for dxy in self.direct:
                self.near(dz, dxy).wait_send()
            if 3 not in self.direct:
                for dxy in (1, 2):
                    self.corner(dz, dxy).wait_send()
        for dz in range(deep):
            for dxy in range(4):
                self.across(dz, dxy).wait_send()


def small_tile(vectors, long):
    wide = lambda v: jnp.concatenate([v, jnp.zeros((1, 128 - v.shape[1]), F32)], axis=1)
    long = long.astype(F32).reshape(1, -1)
    lines = [wide(v.astype(F32).reshape(1, -1)) for v in vectors]
    lines += [wide(long[:, 16 * c : 16 * c + 16]) for c in range(4)]
    lines.append(jnp.zeros((128 - len(lines), 128), F32))
    return jnp.concatenate(lines, axis=0).T[:16].astype(BF16)


def small_lines(tiles):
    width = 16 * tiles.shape[0]
    columns = tiles.reshape(width, 128).astype(F32).T
    quarters = width // 128
    rows = [
        jnp.concatenate(
            [columns[8 + c : 9 + c, 128 * j : 128 * j + 128] for c in range(4)], axis=1
        )
        for j in range(quarters)
    ]
    rows.append(jnp.zeros((8 - quarters, width), F32))
    source = lax.broadcasted_iota(jnp.int32, (width, width), 0)
    target = lax.broadcasted_iota(jnp.int32, (width, width), 1)
    goal = source // 16 % 8 * 64 + source // 128 * 16 + source % 16
    moved = jnp.where(goal == target, 1.0, 0.0).astype(BF16)
    long = dot(jnp.concatenate(rows, axis=0).astype(BF16), moved, NN)
    return jnp.concatenate([long, columns[:8]], axis=0)


def matrix(table, first, count=16):
    part = table[:, first : first + count, :]
    return part.reshape(part.shape[0] * count, part.shape[2])


def attend_kernel(frames, mesh_shape, *refs):
    x_in = refs[0]
    if mesh_shape is None:
        table, small_ref = refs[1:3]
        refs = refs[3:]
    else:
        wq_own, wk_own, wv_own, wo_own, wu_own, wd_own = refs[1:7]
        short_own = refs[7:16]
        refs = refs[16:]
    outputs, refs = refs[:6], refs[6:]
    if mesh_shape is not None:
        small_ref, first_ref, second_ref = refs[:3]
        refs = refs[3:]
    results, refs = refs[:6], refs[6:]
    qa_ref, ka_ref, vt_ref, ht_ref, ot_ref, qe_ref = results
    x_ref, units, rows_low, scores, peaks, key_ext, log_rows, load, store = refs[:9]
    padded, width = units.shape
    depth = width // HEADS
    read = pltpu.make_async_copy(x_in, x_ref, load)
    read.start()

    def unit_rows():
        read.wait()
        for start in range(0, padded, ROWS):
            count = min(ROWS, frames - start)
            units[start : start + count, :] = normalize(
                x_ref[start : start + count, :].astype(F32)
            )[0]
        units[frames:, :] = jnp.zeros((padded - frames, width), F32)

    if mesh_shape is None:
        unit_rows()
    else:
        table_a, table_b, own, *sems, keep = refs[9:]
        place = Place(mesh_shape)
        place.greet()
        part_a = Spread(place, table_a.at[place.me], table_a, *sems[0:2])
        part_b = Spread(place, table_b.at[place.me], table_b, *sems[2:4])
        second = Spread(place, own, second_ref, *sems[4:6], relayed=True)
        early = EARLY_HEADS * depth
        if early > 128:
            table_a[place.me, 48:64, 128:] = jnp.zeros((16, early - 128), BF16)
        for i, weight_own in enumerate((wq_own, wk_own, wv_own)):
            table_a[place.me, 16 * i : 16 * i + 16, :] = weight_own[:, :early]
            table_b[place.me, 16 * i : 16 * i + 16, :] = weight_own[:, early:]
        table_a[place.me, 48:64, 0:128] = small_tile(
            [ref[...] for ref in short_own[:8]], short_own[8][...]
        )
        place.meet()
        part_a.begin_far()
        part_a.begin_near()
        own[0:16, :] = wo_own[...]
        chunks = wu_own.shape[1] // FF_CHUNK
        for j in range(chunks):
            own[16 + 16 * j : 32 + 16 * j, :] = wu_own[:, j * FF_CHUNK : (j + 1) * FF_CHUNK]
        own[16 + 16 * chunks :, :] = wd_own[...]
        unit_rows()
        part_a.relay_far()
        part_b.begin_far()
        part_a.relay_near(0, place.deep)
        part_b.begin_near()
        second.begin_far()
        second.begin_near()
        keep_own = pltpu.make_async_copy(own, second_ref.at[place.me], keep.at[0])
        keep_own.start()
        part_a.arrive()
        keep_a = pltpu.make_async_copy(
            table_a.at[:, 0:48], first_ref.at[:, :, pl.ds(0, early)], keep.at[1]
        )
        keep_a.start()
        keep_b = pltpu.make_async_copy(
            table_b, first_ref.at[:, :, pl.ds(early, width - early)], keep.at[2]
        )
        small_ref[...] = small_lines(table_a[:, 48:64, 0:128])

    writes = [
        pltpu.make_async_copy(results[i], outputs[i], store.at[i]) for i in (0, 1, 2, 3)
    ]
    last_write = pltpu.make_async_copy(qe_ref, outputs[5], store.at[4])

    def head_write(head):
        rows = pl.ds(pl.multiple_of(head * depth, depth), depth)
        return pltpu.make_async_copy(ot_ref.at[rows], outputs[4].at[rows], store.at[5 + head])

    bq, bv, gain, shift = (small_ref[r : r + 1, :] for r in (8, 9, 12, 13))

    def project(heads, i, carry):
        low, high = heads
        lanes = slice(low * depth, high * depth)

        def weight(which):
            if mesh_shape is None:
                return matrix(table[:, :, lanes], 16 * which)
            return matrix(table_a if low == 0 else table_b, 16 * which)

        rows = pl.ds(pl.multiple_of(i * PROJECT_ROWS, PROJECT_ROWS), PROJECT_ROWS)
        if low == 0:
            h1 = (units[rows, :] * gain + shift).astype(BF16)
            rows_low[rows, :] = h1
            ht_ref[:, rows] = h1.T
        else:
            h1 = rows_low[rows, :]
        q = (dot(h1, weight(0), NN) + bq[:, lanes]).astype(BF16)
        k = dot(h1, weight(1), NN).astype(BF16).astype(F32)
        k = k * (LOG2E / math.sqrt(depth))
        v = (dot(h1, weight(2), NN) + bv[:, lanes]).astype(BF16)
        k_high = k.astype(BF16)
        k_low = (k - k_high.astype(F32)).astype(BF16)
        vt_ref[lanes, rows] = v.T
        for h in range(low, high):
            cols = slice((h - low) * depth, (h - low + 1) * depth)
            qa_ref[h, rows, :] = jnp.concatenate([q[:, cols], q[:, cols]], axis=1)
            ka_ref[h, rows, :] = jnp.concatenate([k_high[:, cols], k_low[:, cols]], axis=1)
        return carry

    lax.fori_loop(0, padded // PROJECT_ROWS, functools.partial(project, (0, EARLY_HEADS)), 0)

    def project_rest():
        if mesh_shape is not None:
            part_b.arrive()
            keep_b.start()
        lax.fori_loop(0, padded // PROJECT_ROWS, functools.partial(project, (EARLY_HEADS, HEADS)), 0)
        for copy in writes:
            copy.start()

    blocks = padded // QUERIES
    steps = HEADS * blocks
    lane = lax.broadcasted_iota(jnp.int32, (QUERIES, 128), 1)
    query_ext = jnp.where(lane % 16 == 0, 1.0, 0.0).astype(BF16)

    def score(step, slot):
        head = step // blocks
        rows = pl.ds(pl.multiple_of((step % blocks) * QUERIES, QUERIES), QUERIES)
        key_ext[slot] = key_extra(head, padded, frames)
        left = jnp.concatenate([ka_ref[head], key_ext[slot]], axis=1)
        right = jnp.concatenate([qa_ref[head, rows, :], query_ext], axis=1)
        s = dot(left, right, NT)
        scores[slot] = s
        peaks[slot] = jnp.max(s, axis=0, keepdims=True)

    def finish(step, slot):
        head = step // blocks
        cols = pl.ds(pl.multiple_of((step % blocks) * QUERIES, QUERIES), QUERIES)
        peak = peaks[slot]
        weights = jnp.exp2(scores[slot] - peak).astype(BF16)
        rows = pl.ds(pl.multiple_of(head * depth, depth), depth)
        ones = jnp.ones((16, padded), BF16)
        mixed = dot(jnp.concatenate([vt_ref[rows, :], ones], axis=0), weights, NN)
        total = mixed[depth : depth + 1, :]
        ot_ref[rows, cols] = (mixed[:depth, :] * (1.0 / total)).astype(BF16)
        log_rows[head, :, cols] = peak + jnp.log2(total)

    score(0, 0)

    def pair(i, carry):
        if mesh_shape is not None:
            pl.when(i == B_FAR_AT)(part_b.relay_far)
            pl.when(i == B_NEAR_AT)(functools.partial(part_b.relay_near, 0, place.deep))
            pl.when(i == FAR_AT)(second.relay_far)
            pl.when(i == NEAR_AT)(functools.partial(second.relay_near, 0, 2))
            pl.when(i == NEAR_AT + 1)(functools.partial(second.relay_near, 2, place.deep))
            pl.when(i == CORNER_AT)(functools.partial(second.relay_corner, 0, 2))
        pl.when(i == EARLY_HEADS - 1)(project_rest)
        score(i * 2 + 1, 1)
        finish(i * 2, 0)
        score(jnp.minimum(i * 2 + 2, steps - 1), 0)
        finish(i * 2 + 1, 1)
        head_write(i).start()
        return carry

    lax.fori_loop(0, steps // 2, pair, 0)

    def extend(i, carry):
        rows = pl.ds(pl.multiple_of(i * ROWS, ROWS), ROWS)
        pieces = []
        for h in range(HEADS):
            high, middle, low = in_three(-log_rows[h, :, rows])
            pieces += [jnp.ones((1, ROWS), F32), high, middle, low, jnp.zeros((12, ROWS), F32)]
        qe_ref[rows, :] = jnp.concatenate(pieces, axis=0).T.astype(BF16)
        return carry

    if mesh_shape is not None:
        second.relay_corner(2, place.deep)
    lax.fori_loop(0, padded // ROWS, extend, 0)
    last_write.start()
    for copy in writes + [last_write] + [head_write(head) for head in range(HEADS)]:
        copy.wait()
    if mesh_shape is not None:
        second.arrive()
        keep_own.wait()
        keep_a.wait()
        keep_b.wait()
        part_a.drain()
        part_b.drain()
        second.drain()


def attend(mesh_shape, x, *rest):
    frames, width = x.shape
    padded = -(-frames // QUERIES) * QUERIES
    blocks = width // 16
    vmem = pl.BlockSpec(memory_space=pltpu.VMEM)
    hbm = pl.BlockSpec(memory_space=pltpu.HBM)
    out_shape = [
        jax.ShapeDtypeStruct((HEADS, padded, 128), BF16),
        jax.ShapeDtypeStruct((HEADS, padded, 128), BF16),
        jax.ShapeDtypeStruct((width, padded), BF16),
        jax.ShapeDtypeStruct((width, padded), BF16),
        jax.ShapeDtypeStruct((width, padded), BF16),
        jax.ShapeDtypeStruct((padded, 128), BF16),
    ]
    scratch = [pltpu.VMEM(shape.shape, shape.dtype) for shape in out_shape]
    scratch += [
        pltpu.VMEM((frames, width), BF16),
        pltpu.VMEM((padded, width), F32),
        pltpu.VMEM((padded, width), BF16),
        pltpu.VMEM((2, padded, QUERIES), F32),
        pltpu.VMEM((2, 1, QUERIES), F32),
        pltpu.VMEM((2, padded, 128), BF16),
        pltpu.VMEM((HEADS, 1, padded), F32),
        pltpu.SemaphoreType.DMA,
        pltpu.SemaphoreType.DMA((5 + HEADS,)),
    ]
    out_specs = [hbm] * 6
    options = {}
    if mesh_shape is not None:
        early = EARLY_HEADS * (width // HEADS)
        hidden = rest[4].shape[1]
        own_rows = 16 + hidden // FF_CHUNK * 16 + rest[5].shape[0]
        out_shape += [
            jax.ShapeDtypeStruct((16, width), F32),
            jax.ShapeDtypeStruct((blocks, 48, width), BF16),
            jax.ShapeDtypeStruct((blocks, own_rows, width), BF16),
        ]
        out_specs += [vmem, hbm, hbm]
        scratch += [
            pltpu.VMEM((blocks, 64, early), BF16),
            pltpu.VMEM((blocks, 48, width - early), BF16),
            pltpu.VMEM((own_rows, width), BF16),
        ]
        scratch += [pltpu.SemaphoreType.DMA((blocks - 1,)) for _ in range(4)]
        scratch += [pltpu.SemaphoreType.DMA((mesh_shape[0] * 4 + 3,)) for _ in range(2)]
        scratch += [pltpu.SemaphoreType.DMA((3,))]
        options = dict(collective_id=0, has_side_effects=True)
    return pl.pallas_call(
        functools.partial(attend_kernel, frames, mesh_shape),
        out_shape=out_shape,
        in_specs=[hbm] + [vmem] * len(rest),
        out_specs=out_specs,
        scratch_shapes=scratch,
        compiler_params=pltpu.CompilerParams(vmem_limit_bytes=60 << 20, **options),
        name="attend",
    )(x, *rest)


def mlp_kernel(
    frames,
    flag_ref,
    x_ref,
    cot_ref,
    ot_ref,
    table_in,
    vec_ref,
    out_ref,
    dx_ref,
    do_ref,
    de_ref,
    grads_out,
    small_ref,
    gwo,
    gwu,
    gwd,
    table,
    grads_ref,
    load,
    store,
):
    step = pl.program_id(0)
    rows, width = x_ref.shape
    chunks = gwu.shape[0]
    depth = width // HEADS
    down = table.shape[1] - 16 - 16 * chunks
    per_chunk = FF_CHUNK // down

    def up_part(j):
        return matrix(table, 16 + 16 * j)

    def down_part(j):
        part = table[j * per_chunk : (j + 1) * per_chunk, 16 + 16 * chunks :, :]
        return part.reshape(FF_CHUNK, width)

    bounds = (0, 16, 16 + 16 * chunks, table.shape[1])
    loads = [
        pltpu.make_async_copy(table_in.at[:, low:high], table.at[:, low:high], load.at[i])
        for i, (low, high) in enumerate(zip(bounds, bounds[1:]))
    ]

    @pl.when(step == 0)
    def _():
        for copy in loads:
            copy.start()
        small_ref[...] = jnp.zeros_like(small_ref)
        loads[0].wait()

    def kept(ref, *index):
        return jnp.where(step == 0, 0.0, ref[index] if index else ref[...])

    flag = flag_ref[0].astype(F32)
    inside = step * rows + lax.broadcasted_iota(jnp.int32, (rows, width), 0) < frames
    x = jnp.where(inside, x_ref[...].astype(F32), 0.0)
    dy = jnp.where(inside, cot_ref[...].astype(F32), 0.0) * flag
    dy_low = dy.astype(BF16)
    bo, bd, gain, shift = (vec_ref[r : r + 1, :] for r in (10, 11, 14, 15))
    wo = matrix(table, 0)
    ot = ot_ref[...]
    o = ot.T
    x1 = x + (dot(o, wo, NN) + bo)
    unit, inv_std = normalize(x1)
    h2 = (unit * gain + shift).astype(BF16)
    h2t = h2.T

    @pl.when(step == 0)
    def _():
        loads[1].wait()
        loads[2].wait()

    z_next = dot(h2, up_part(0), NN)
    out = x1 + bd
    dh2 = jnp.zeros((rows, width), F32)
    for j in range(chunks):
        z = z_next + vec_ref[j : j + 1, :]
        if j + 1 < chunks:
            z_next = dot(h2, up_part(j + 1), NN)
        dg = dot(dy_low, down_part(j), NT)
        g, slope = gelu_and_slope(z)
        g = g.astype(BF16)
        dz = (dg * slope).astype(BF16)
        out = out + dot(g, down_part(j), NN)
        gwd[j] = kept(gwd, j) + dot(g, dy_low, TN)
        gwu[j] = kept(gwu, j) + dot(h2t, dz, NN)
        small_ref[j : j + 1, :] += column_sums(dz.astype(F32))
        dh2 = dh2 + dot(dz, up_part(j), NT)
    store_rows(out_ref, 0, out * flag)
    dx1 = dy + normalize_back(dh2, unit, inv_std, gain)
    dx_ref[...] = dx1
    da = dx1.astype(BF16)
    gwo[...] = kept(gwo) + dot(ot, da, NN)
    do = dot(da, wo, NT).astype(BF16)
    small_ref[10:11, :] += column_sums(da.astype(F32))
    small_ref[11:12, :] += column_sums(dy)
    small_ref[14:15, :] += column_sums(dh2 * unit)
    small_ref[15:16, :] += column_sums(dh2)
    do_ref[...] = do
    prod = do.astype(F32) * o.astype(F32)
    high = prod.astype(BF16)
    low = (prod - high.astype(F32)).astype(BF16)
    owner = lax.broadcasted_iota(jnp.int32, (width, 128), 0) // depth
    pick = lax.broadcasted_iota(jnp.int32, (width, 128), 1) // 16
    pick = jnp.where(owner == pick, 1.0, 0.0).astype(BF16)
    high, middle, low = in_three(-(dot(high, pick, NN) + dot(low, pick, NN)))
    lane = lax.broadcasted_iota(jnp.int32, (rows, 128), 1) % 16
    extra = jnp.where(lane == 1, middle, jnp.where(lane == 2, low, 0.0))
    de_ref[...] = jnp.where(lane == 0, high, extra).astype(BF16)

    @pl.when(step == pl.num_programs(0) - 1)
    def _():
        split = lambda part, count: part.astype(BF16).reshape(-1, count, width)
        copies = []

        def send(*index):
            copies.append(
                pltpu.make_async_copy(
                    grads_ref.at[index], grads_out.at[index], store.at[len(copies)]
                )
            )
            copies[-1].start()

        for j in range(chunks):
            rows_up = slice(16 + 16 * j, 32 + 16 * j)
            grads_ref[:, rows_up, :] = split(gwu[j], 16)
            send(slice(None), rows_up)
            blocks_down = slice(j * per_chunk, (j + 1) * per_chunk)
            rows_down = slice(16 + 16 * chunks, table.shape[1])
            grads_ref[blocks_down, rows_down, :] = split(gwd[j], down)
            send(blocks_down, rows_down)
        grads_ref[:, 0:16, :] = split(gwo[...], 16)
        send(slice(None), slice(0, 16))
        for copy in copies:
            copy.wait()


def mlp(flag, x, cot, ot, table, vectors):
    frames, width = x.shape
    padded = ot.shape[1]
    blocks, rows = table.shape[:2]
    chunks = (rows - 16) * blocks // (2 * FF_CHUNK)
    by_rows = pl.BlockSpec((MLP_ROWS, width), lambda i: (i, 0))
    fixed = lambda shape: pl.BlockSpec(
        shape, lambda i: (0,) * len(shape), pipeline_mode=pl.Buffered(1)
    )
    return pl.pallas_call(
        functools.partial(mlp_kernel, frames),
        grid=(padded // MLP_ROWS,),
        out_shape=[
            jax.ShapeDtypeStruct((frames * width // 128, 128), F32),
            jax.ShapeDtypeStruct((frames, width), F32),
            jax.ShapeDtypeStruct((padded, width), BF16),
            jax.ShapeDtypeStruct((padded, 128), BF16),
            jax.ShapeDtypeStruct(table.shape, BF16),
            jax.ShapeDtypeStruct((16, width), F32),
        ],
        in_specs=[
            pl.BlockSpec(memory_space=pltpu.SMEM),
            by_rows,
            by_rows,
            pl.BlockSpec((width, MLP_ROWS), lambda i: (0, i)),
            pl.BlockSpec(memory_space=pltpu.HBM),
            fixed((16, width)),
        ],
        out_specs=[
            pl.BlockSpec((MLP_ROWS * width // 128, 128), lambda i: (i, 0)),
            by_rows,
            by_rows,
            pl.BlockSpec((MLP_ROWS, 128), lambda i: (i, 0)),
            pl.BlockSpec(memory_space=pltpu.HBM),
            fixed((16, width)),
        ],
        scratch_shapes=[
            pltpu.VMEM((width, width), F32),
            pltpu.VMEM((chunks, width, FF_CHUNK), F32),
            pltpu.VMEM((chunks, FF_CHUNK, width), F32),
            pltpu.VMEM(table.shape, BF16),
            pltpu.VMEM(table.shape, BF16),
            pltpu.SemaphoreType.DMA((3,)),
            pltpu.SemaphoreType.DMA((2 * chunks + 1,)),
        ],
        compiler_params=pltpu.CompilerParams(
            vmem_limit_bytes=60 << 20, dimension_semantics=("arbitrary",)
        ),
        name="mlp",
    )(flag, x, cot, ot, table, vectors)


class Gather:
    def __init__(self, place, source, from_core, halves, from_near, quarter, from_far, sems):
        self.place, self.source = place, source
        self.from_core, self.halves = from_core, halves
        self.from_near, self.quarter = from_near, quarter
        self.from_far = from_far
        self.send_sem, self.recv_sem = sems

    def copy(self, slot, src, dst, device):
        return pltpu.make_async_remote_copy(
            src_ref=src,
            dst_ref=dst,
            send_sem=self.send_sem.at[slot],
            recv_sem=self.recv_sem.at[slot],
            device_id=device,
            device_id_type=MESH,
        )

    def across(self):
        place = self.place
        return [
            self.copy(
                z, self.source.at[z, :, 1 - place.core], self.from_core.at[z], place.moved(flip=1)
            )
            for z in range(place.deep)
        ]

    def near(self):
        place = self.place
        copies = []
        for dxy in range(1, 4):
            b, s = place.moved(dxy=dxy)
            square = b % 2 * 2 + s // 2
            copies.append(
                self.copy(
                    place.deep + dxy - 1,
                    self.halves.at[:, square],
                    self.from_near.at[dxy - 1],
                    (b, s),
                )
            )
        return copies

    def far(self):
        place = self.place
        copies = []
        for dz in range(1, place.deep):
            z = (place.z + dz) % place.deep
            copies.append(
                self.copy(
                    place.deep + 2 + dz,
                    self.quarter.at[z],
                    self.from_far.at[dz - 1],
                    place.moved(dz=dz),
                )
            )
        return copies

    def fold_across(self, own):
        for copy in self.across():
            copy.wait_recv()

        def one(i, carry):
            z, q = i // 4, i % 4
            total = own(z, q).astype(F32) + self.from_core[z, q].astype(F32)
            self.halves[z, q] = total.astype(BF16)
            return carry

        lax.fori_loop(0, self.place.deep * 4, one, 0)
        for copy in self.near():
            copy.start()

    def fold_near(self):
        for copy in self.near():
            copy.wait_recv()

        def one(z, carry):
            total = self.halves[z, self.place.square].astype(F32)
            for dxy in range(3):
                total = total + self.from_near[dxy, z].astype(F32)
            self.quarter[z] = total.astype(BF16)
            return carry

        lax.fori_loop(0, self.place.deep, one, 0)
        for copy in self.far():
            copy.start()

    def result(self):
        for copy in self.far():
            copy.wait_recv()
        total = self.quarter[self.place.z].astype(F32)
        for dz in range(self.place.deep - 1):
            total = total + self.from_far[dz].astype(F32)
        return total

    def drain(self):
        for copy in self.across() + self.near() + self.far():
            copy.wait_send()


class SmallSum:
    def __init__(self, place, buffers, received, sems):
        self.place, self.buffers, self.received = place, buffers, received
        self.send_sem, self.recv_sem = sems

    def copies(self, stage):
        place = self.place
        if stage == 0:
            devices, first = [place.moved(flip=1)], 0
        elif stage == 1:
            devices, first = [place.moved(dxy=dxy) for dxy in range(1, 4)], 1
        else:
            devices, first = [place.moved(dz=dz) for dz in range(1, place.deep)], 4
        return [
            pltpu.make_async_remote_copy(
                src_ref=self.buffers.at[stage],
                dst_ref=self.received.at[first + i],
                send_sem=self.send_sem.at[first + i],
                recv_sem=self.recv_sem.at[first + i],
                device_id=device,
                device_id_type=MESH,
            )
            for i, device in enumerate(devices)
        ]

    def send(self, stage, value):
        self.buffers[stage] = value
        for copy in self.copies(stage):
            copy.start()

    def receive(self, stage):
        total = self.buffers[stage]
        first = (0, 1, 4)[stage]
        for i, copy in enumerate(self.copies(stage)):
            copy.wait_recv()
            total = total + self.received[first + i]
        return total

    def drain(self):
        for stage in range(3):
            for copy in self.copies(stage):
                copy.wait_send()


def own_small(total, place):
    width = total.shape[1]
    line = lax.broadcasted_iota(jnp.int32, total.shape, 0)
    short = pltpu.roll(total, width - place.me * 16, 1)
    long = jnp.sum(jnp.where(line == place.me // 8, total, 0.0), axis=0, keepdims=True)
    long = pltpu.roll(jnp.broadcast_to(long, total.shape), width - place.me % 8 * 64, 1)
    return jnp.where(line == 0, long, short)[:, :128]


def attend_back_kernel(frames, mesh_shape, *refs):
    x_in, dx_in, qa_in, ka_in, vt_in, ht_in, qe_in, do_in, de_in, table_in = refs[:10]
    vec_ref, small_in = refs[10:12]
    refs = refs[12:]
    if mesh_shape is None:
        dinput_out, source, small_ref = refs[:3]
        refs = refs[3:]
    else:
        grads_ref = refs[0]
        dinput_out, gq_ref, gk_ref, gv_ref, go_ref, gu_ref, gd_ref = refs[1:8]
        short_refs = refs[8:17]
        refs = refs[17:]
    x_ref, dx_ref, qa_ref, ka_ref, vt_ref, ht_ref, qe_ref, do_ref, de_ref, table = refs[:10]
    dinput_ref, load, store = refs[10:13]
    dq, dkt, dvt, sum_k, sum_v, key_ext, value_ext, small = refs[13:21]
    refs = refs[21:]

    padded = qa_ref.shape[1]
    width = ht_ref.shape[0]
    depth = width // HEADS

    def head_loads(head):
        return [
            pltpu.make_async_copy(qa_in.at[head], qa_ref.at[head], load.at[2 * head]),
            pltpu.make_async_copy(ka_in.at[head], ka_ref.at[head], load.at[2 * head + 1]),
        ]

    sources = (vt_in, do_in, de_in, qe_in, ht_in, table_in.at[:, 0:48], x_in, dx_in)
    targets = (vt_ref, do_ref, de_ref, qe_ref, ht_ref, table, x_ref, dx_ref)
    loads = [
        pltpu.make_async_copy(source_ref, target_ref, load.at[2 * HEADS + i])
        for i, (source_ref, target_ref) in enumerate(zip(sources, targets))
    ]
    for copy in head_loads(0) + loads[:4]:
        copy.start()
    for head in range(1, HEADS):
        for copy in head_loads(head):
            copy.start()
    for copy in loads[4:]:
        copy.start()

    if mesh_shape is not None:
        place = Place(mesh_shape)
        place.greet()
        parts = []
        for _ in PARTS:
            parts.append(Gather(place, refs[0], *refs[1:6], refs[6:8]))
            refs = refs[8:]
        second = Gather(place, grads_ref, *refs[:5], refs[5:7])
        shorts = SmallSum(place, refs[7], refs[8], refs[9:11])
        second_half, keep = refs[11:]
        keep_half = pltpu.make_async_copy(grads_ref.at[:, :, place.core], second_half, keep)
        place.meet()
        for copy in second.across():
            copy.start()
        keep_half.start()
    for copy in loads[:4]:
        copy.wait()

    def second_across():
        keep_half.wait()
        second.fold_across(lambda z, q: second_half[z, q])

    lane_half = lax.broadcasted_iota(jnp.int32, (padded, 128), 1) < depth

    def weight_grads(t):
        low, high = PARTS[t]
        cols = slice(low * depth, high * depth)
        wide = (high - low) * depth
        queries = jnp.concatenate(
            [jnp.where(lane_half, dq[h], dq[h + 1]) for h in range(low, high, 2)], axis=1
        )
        ht = ht_ref[...]
        grads = (
            dot(ht, queries, NN),
            dot(ht, dkt[cols, :], NT),
            dot(ht, dvt[cols, :], NT),
        )
        for i, grad in enumerate(grads):
            grad = grad.astype(BF16)
            if mesh_shape is None:
                source[:, 16 * i : 16 * i + 16, cols] = grad.reshape(-1, 16, wide)
            else:
                target = parts[t].source
                target[:, :, :, 16 * i : 16 * i + 16, :] = grad.reshape(
                    target.shape[:3] + (16, wide)
                )
        if mesh_shape is not None:
            for copy in parts[t].across():
                copy.start()

    def fold_part(t):
        parts[t].fold_across(lambda z, q: parts[t].source[z, q, place.core])

    def part_result(t):
        total = parts[t].result()
        for i, ref in enumerate((gq_ref, gk_ref, gv_ref)):
            ref[:, PARTS[t][0] * depth : PARTS[t][1] * depth] = total[16 * i : 16 * i + 16]

    def early_weight_grads(t):
        if t == 0:
            loads[4].wait()
        weight_grads(t)

    last = len(PARTS) - 1

    def one_head(head, carry):
        for t in range(last):
            pl.when(head == PARTS[t][1])(functools.partial(early_weight_grads, t))
            if mesh_shape is not None and PARTS[t][1] + 1 < HEADS:
                pl.when(head == PARTS[t][1] + 1)(functools.partial(fold_part, t))
        if mesh_shape is not None:
            pl.when(head == ACROSS_AT)(second_across)
            pl.when(head == SQUARE_AT)(second.fold_near)
        for copy in head_loads(head):
            copy.wait()
        key_ext[...] = key_extra(head, padded, frames)
        line = lax.broadcasted_iota(jnp.int32, (128, padded), 0)
        mine = pl.ds(pl.multiple_of(head // 2 * 128, 128), 128)
        values = jnp.where(line // depth == head % 2, vt_ref[mine, :].astype(F32), 0.0)
        value_ext[0:128, :] = values.astype(BF16)
        extra = jnp.where((line // 16 == head) & (line % 16 < 3), 1.0, 0.0)
        value_ext[128:256, :] = extra.astype(BF16)
        for i in range(padded // ROWS):
            rows = slice(i * ROWS, (i + 1) * ROWS)
            q = qa_ref[head, rows, :]
            d = do_ref[rows, mine]
            turned = d.T
            turned = jnp.where(head % 2 == 0, turned[:depth], turned[depth:])
            s = dot(
                jnp.concatenate([q, qe_ref[rows, :]], axis=1),
                jnp.concatenate([ka_ref[head], key_ext[...]], axis=1),
                NT,
            )
            p = jnp.exp2(s)
            dp = dot(jnp.concatenate([d, de_ref[rows, :]], axis=1), value_ext[...], NN)
            ds = (p * dp).astype(BF16)
            p = p.astype(BF16)
            new_v = dot(turned, p, NN)
            new_k = dot(q[:, :depth], ds, TN)
            if i == 0:
                sum_v[...] = new_v
                sum_k[...] = new_k
            else:
                sum_v[...] += new_v
                sum_k[...] += new_k
            both = dot(ds, ka_ref[head], NN)
            both = both + pltpu.roll(both, depth, 1)
            dq[head, rows, :] = (both * LN2).astype(BF16)
        out_rows = pl.ds(pl.multiple_of(head * depth, depth), depth)
        dkt[out_rows, :] = (sum_k[...] * (1.0 / math.sqrt(depth))).astype(BF16)
        dvt[out_rows, :] = sum_v[...].astype(BF16)
        return carry

    lax.fori_loop(0, HEADS, one_head, 0)

    weight_grads(last)
    for copy in loads[5:]:
        copy.wait()
    if mesh_shape is not None:
        for t in range(last):
            if PARTS[t][1] + 1 >= HEADS:
                fold_part(t)
            else:
                parts[t].fold_near()
        second_own = second.result()
        chunks = gu_ref.shape[1] // FF_CHUNK
        go_ref[...] = second_own[0:16]
        for j in range(chunks):
            gu_ref[:, j * FF_CHUNK : (j + 1) * FF_CHUNK] = second_own[16 + 16 * j : 32 + 16 * j]
        gd_ref[...] = second_own[16 + 16 * chunks :]

    gain = vec_ref[12:13, :]
    small[...] = small_in[...]
    stores = []
    for index, start in enumerate(range(0, frames, ROWS)):
        if mesh_shape is not None and index == FOLD_AT:
            fold_part(last)
            for t in range(last):
                if PARTS[t][1] + 1 >= HEADS:
                    parts[t].fold_near()
        count = min(ROWS, frames - start)
        rows = slice(start, start + count)
        wide = slice(start, start + ROWS)
        some = lane_half[:ROWS]
        dq_rows = jnp.concatenate(
            [jnp.where(some, dq[h, wide, :], dq[h + 1, wide, :]) for h in range(0, HEADS, 2)],
            axis=1,
        )
        dk_rows = dkt[:, wide].T
        dv_rows = dvt[:, wide].T
        dh1 = (
            dot(dq_rows, matrix(table, 0), NT)
            + dot(dk_rows, matrix(table, 16), NT)
            + dot(dv_rows, matrix(table, 32), NT)
        )
        small[8:9, :] += column_sums(dq_rows.astype(F32))
        small[9:10, :] += column_sums(dv_rows.astype(F32))
        dh1 = dh1[:count]
        unit, inv_std = normalize(x_ref[rows, :].astype(F32))
        small[12:13, :] += column_sums(dh1 * unit)
        small[13:14, :] += column_sums(dh1)
        dinput = dx_ref[rows, :] + normalize_back(dh1, unit, inv_std, gain)
        store_rows(dinput_ref, start, dinput)
        part = pl.ds(start * (width // 128), count * (width // 128))
        stores.append(
            pltpu.make_async_copy(dinput_ref.at[part], dinput_out.at[part], store.at[index])
        )
        stores[-1].start()
    if mesh_shape is None:
        small_ref[...] = small[...]
    else:
        shorts.send(0, small[...])
        for t in range(last):
            part_result(t)
        shorts.send(1, shorts.receive(0))
        parts[last].fold_near()
        shorts.send(2, shorts.receive(1))
        second.drain()
        for t in range(last):
            parts[t].drain()
        part_result(last)
        small_own = own_small(shorts.receive(2), place)
        for i, ref in enumerate(short_refs[:8]):
            ref[...] = small_own[8 + i, :16]
        short_refs[8][...] = small_own[0, :64]
        parts[last].drain()
        shorts.drain()
    for copy in stores:
        copy.wait()


def attend_back(mesh_shape, x, dx, qa, ka, vt, ht, qe, do, de, table, vectors, small, grads):
    frames, width = x.shape
    padded = ht.shape[1]
    blocks = width // 16
    vmem = pl.BlockSpec(memory_space=pltpu.VMEM)
    hbm = pl.BlockSpec(memory_space=pltpu.HBM)
    args = [x, dx, qa, ka, vt, ht, qe, do, de, table, vectors, small]
    in_specs = [hbm] * 10 + [vmem] * 2
    lines = frames * width // 128
    out_shape = [jax.ShapeDtypeStruct((lines, 128), F32)]
    scratch = [pltpu.VMEM(array.shape, array.dtype) for array in args[:9]]
    scratch += [
        pltpu.VMEM((blocks, 48, width), BF16),
        pltpu.VMEM((lines, 128), F32),
        pltpu.SemaphoreType.DMA((2 * HEADS + 8,)),
        pltpu.SemaphoreType.DMA((padded // ROWS,)),
        pltpu.VMEM((HEADS, padded, 128), BF16),
        pltpu.VMEM((width, padded), BF16),
        pltpu.VMEM((width, padded), BF16),
        pltpu.VMEM((width // HEADS, padded), F32),
        pltpu.VMEM((width // HEADS, padded), F32),
        pltpu.VMEM((padded, 128), BF16),
        pltpu.VMEM((256, padded), BF16),
        pltpu.VMEM((16, width), F32),
    ]
    options = {}
    if mesh_shape is None:
        out_shape += [
            jax.ShapeDtypeStruct((blocks, 48, width), BF16),
            jax.ShapeDtypeStruct((16, width), F32),
        ]
    else:
        deep = mesh_shape[0] // 2
        rows = grads.shape[1]
        hidden = (rows - 16) * blocks // 2
        args.append(grads.reshape(deep, 4, 2, rows, width))
        in_specs.append(hbm)
        out_shape += [
            jax.ShapeDtypeStruct((16, width), F32),
            jax.ShapeDtypeStruct((16, width), F32),
            jax.ShapeDtypeStruct((16, width), F32),
            jax.ShapeDtypeStruct((16, width), F32),
            jax.ShapeDtypeStruct((16, hidden), F32),
            jax.ShapeDtypeStruct((hidden // blocks, width), F32),
        ]
        out_shape += [jax.ShapeDtypeStruct((16,), F32)] * 8
        out_shape += [jax.ShapeDtypeStruct((hidden // blocks,), F32)]

        def stages(shape):
            return [
                pltpu.VMEM((deep, 4) + shape, BF16),
                pltpu.VMEM((deep, 4) + shape, BF16),
                pltpu.VMEM((3, deep) + shape, BF16),
                pltpu.VMEM((deep,) + shape, BF16),
                pltpu.VMEM((deep - 1,) + shape, BF16),
                pltpu.SemaphoreType.DMA((2 * deep + 2,)),
                pltpu.SemaphoreType.DMA((2 * deep + 2,)),
            ]

        for low, high in PARTS:
            shape = (48, (high - low) * (width // HEADS))
            scratch += [pltpu.VMEM((deep, 4, 2) + shape, BF16)] + stages(shape)
        scratch += stages((rows, width))
        scratch += [
            pltpu.VMEM((3, 16, width), F32),
            pltpu.VMEM((deep + 3, 16, width), F32),
            pltpu.SemaphoreType.DMA((deep + 3,)),
            pltpu.SemaphoreType.DMA((deep + 3,)),
            pltpu.VMEM((deep, 4, rows, width), BF16),
            pltpu.SemaphoreType.DMA,
        ]
        options = dict(collective_id=1, has_side_effects=True)
    return pl.pallas_call(
        functools.partial(attend_back_kernel, frames, mesh_shape),
        out_shape=out_shape,
        in_specs=in_specs,
        out_specs=[hbm] + [vmem] * (len(out_shape) - 1),
        scratch_shapes=scratch,
        compiler_params=pltpu.CompilerParams(vmem_limit_bytes=60 << 20, **options),
        name="attend_back",
    )(*args)


def hand_over_kernel(count, *refs):
    large, small = refs[0], refs[1 : count + 1]
    large_buf, small_buf = refs[2 * count + 2], refs[2 * count + 3 : 3 * count + 3]
    large_out, small_out = refs[count + 1], refs[count + 2 : 2 * count + 2]
    sem_in, sem_out = refs[3 * count + 3 :]
    pieces = large_buf.shape[0]
    rows = large_buf.shape[1]
    sources = [large.at[pl.ds(i * rows, rows)] for i in range(pieces)] + list(small)
    buffers = [large_buf.at[i] for i in range(pieces)] + list(small_buf)
    targets = [large_out.at[pl.ds(i * rows, rows)] for i in range(pieces)] + list(small_out)
    inward = [
        pltpu.make_async_copy(source, buffer, sem_in.at[i])
        for i, (source, buffer) in enumerate(zip(sources, buffers))
    ]
    outward = [
        pltpu.make_async_copy(buffer, target, sem_out.at[i])
        for i, (buffer, target) in enumerate(zip(buffers, targets))
    ]
    for copy in inward:
        copy.start()
    for first, then in zip(inward, outward):
        first.wait()
        then.start()
    for copy in outward:
        copy.wait()


def hand_over(large, *small):
    anywhere = pl.BlockSpec(memory_space=pltpu.HBM)
    arrays = (large,) + small
    rows = large.shape[0]
    pieces = 6 if rows % 48 == 0 else 1
    return pl.pallas_call(
        functools.partial(hand_over_kernel, len(small)),
        out_shape=[jax.ShapeDtypeStruct(array.shape, array.dtype) for array in arrays],
        in_specs=[anywhere] * len(arrays),
        out_specs=[anywhere] * len(arrays),
        scratch_shapes=[pltpu.VMEM((pieces, rows // pieces) + large.shape[1:], large.dtype)]
        + [pltpu.VMEM(array.shape, array.dtype) for array in small]
        + [pltpu.SemaphoreType.DMA((len(small) + pieces,))] * 2,
        compiler_params=pltpu.CompilerParams(vmem_limit_bytes=60 << 20),
        name="hand_over",
    )(*arrays)


def staged(mesh_shape, windows, cotangent, valid, *owned):
    x, cot = windows[0], cotangent[0]
    bq, bv, bo, bu, bd, gain_one, shift_one, gain_two, shift_two = owned[6:]
    short = [bq, bv, bo, bd, gain_one, shift_one, gain_two, shift_two, bu]
    qa, ka, vt, ht, ot, qe, vectors, first, second = attend(mesh_shape, x, *owned[:6], *short)
    out, dx, do, de, grads, small = mlp(valid, x, cot, ot, second, vectors)
    results = attend_back(
        mesh_shape, x, dx, qa, ka, vt, ht, qe, do, de, first, vectors, small, grads
    )
    dinput, gq, gk, gv, go, gu, gd, *shorts = hand_over(*results)
    gbq, gbv, gbo, gbd, *gains, gbu = shorts
    return (
        out.reshape(windows.shape),
        dinput.reshape(windows.shape),
        *(gq, gk, gv, go, gu, gd, gbq, gbv, gbo, gbu, gbd),
        *gains,
    )


def collective(windows, cotangent, valid, *owned):
    axes = ("batch", "shard")
    wq, wk, wv, wo, wu, wd, bq, bv, bo, bu, bd, gain_one, shift_one, gain_two, shift_two = [
        lax.all_gather(part, axes, axis=0, tiled=True) for part in owned
    ]
    x, cot = windows[0], cotangent[0]
    width, hidden = wu.shape
    blocks, chunks = width // 16, hidden // FF_CHUNK
    split = lambda part: part.reshape(blocks, -1, width)
    vectors = jnp.concatenate(
        [jnp.pad(bu.reshape(chunks, FF_CHUNK), ((0, 8 - chunks), (0, 0)))]
        + [v[None] for v in (bq, bv, bo, bd, gain_one, shift_one, gain_two, shift_two)]
    ).astype(F32)
    first = jnp.concatenate([split(wq), split(wk), split(wv)], axis=1)
    ups = wu.reshape(blocks, 16, chunks, FF_CHUNK).transpose(0, 2, 1, 3)
    ups = ups.reshape(blocks, 16 * chunks, FF_CHUNK)
    second = jnp.concatenate([split(wo), ups, split(wd)], axis=1)
    qa, ka, vt, ht, ot, qe = attend(None, x, first, vectors)
    out, dx, do, de, grads, small = mlp(valid, x, cot, ot, second, vectors)
    dinput, first_grads, small = attend_back(
        None, x, dx, qa, ka, vt, ht, qe, do, de, first, vectors, small, None
    )
    first_grads, grads = first_grads.astype(F32), grads.astype(F32)
    joined = lambda part: part.reshape(-1, width)
    gwu = grads[:, 16 : 16 + 16 * chunks].reshape(blocks, chunks, 16, FF_CHUNK)
    gwu = gwu.transpose(0, 2, 1, 3).reshape(width, hidden)
    totals = (
        joined(first_grads[:, 0:16]),
        joined(first_grads[:, 16:32]),
        joined(first_grads[:, 32:48]),
        joined(grads[:, 0:16]),
        gwu,
        joined(grads[:, 16 + 16 * chunks :]),
        small[8],
        small[9],
        small[10],
        small[:chunks].reshape(hidden),
        small[11],
        small[12],
        small[13],
        small[14],
        small[15],
    )
    grads = [lax.psum_scatter(total, axes, scatter_dimension=0, tiled=True) for total in totals]
    return (out.reshape(windows.shape), dinput.reshape(windows.shape), *grads)


def solution(mesh):
    both = ("batch", "shard")
    windows_spec, matrix_spec, vector_spec = P(both, None, None), P(both, None), P(both)
    params = (matrix_spec,) * 6 + (vector_spec,) * 9
    mesh_shape = (mesh.shape["batch"], mesh.shape["shard"])

    def per_device(windows, cotangent, valid, *owned):
        if mesh_shape[1] == 4 and mesh_shape[0] % 2 == 0 and owned[0].shape[0] == 16:
            return staged(mesh_shape, windows, cotangent, valid, *owned)
        return collective(windows, cotangent, valid, *owned)

    return jax.shard_map(
        per_device,
        mesh=mesh,
        in_specs=(windows_spec, windows_spec, vector_spec) + params,
        out_specs=(windows_spec, windows_spec) + params,
        check_vma=False,
    )
```

```python
import functools
import math

import jax
import jax.numpy as jnp
from jax import lax
from jax.experimental import pallas as pl
from jax.experimental.pallas import tpu as pltpu
from jax.sharding import PartitionSpec as P

HEADS = 8
NORM_EPS = 1e-05
LOG2E = math.log2(math.e)
LN2 = math.log(2.0)
F32 = jnp.float32
BF16 = jnp.bfloat16
MESH = pl.DeviceIdType.MESH
ROWS = 256
MLP_ROWS = 512
PROJECT_ROWS = 768
EARLY_HEADS = 4
B_FAR_AT = 0
B_NEAR_AT = 2
FAR_AT = 2
NEAR_AT = 5
CORNER_AT = 7
FOLD_AT = 2
ACROSS_AT = 1
SQUARE_AT = 5
PARTS = ((0, 4), (4, 8))
QUERIES = 768
FF_CHUNK = 512
MASKED = -1e30

NN = (((1,), (0,)), ((), ()))
NT = (((1,), (1,)), ((), ()))
TN = (((0,), (0,)), ((), ()))

TAIL_RATE = 0.3
TAIL = (
    0.1196320072075501,
    0.12071213658889111,
    0.10017594509547065,
    0.12769178078587456,
    -0.0520340331315144,
    0.2045568015805396,
    -0.1561584571261984,
    0.03542373729935703,
)


def dot(left, right, dims):
    return lax.dot_general(left, right, dims, preferred_element_type=F32)


def normalize(values):
    centred = values - jnp.mean(values, axis=-1, keepdims=True)
    variance = jnp.mean(centred * centred, axis=-1, keepdims=True)
    inv_std = lax.rsqrt(variance + NORM_EPS)
    return centred * inv_std, inv_std


def normalize_back(grad_rows, unit_rows, inv_std, gain):
    scaled = grad_rows * gain
    first_mean = jnp.mean(scaled, axis=-1, keepdims=True)
    second_mean = jnp.mean(scaled * unit_rows, axis=-1, keepdims=True)
    return inv_std * (scaled - first_mean - unit_rows * second_mean)


def store_rows(ref, start, rows):
    count, width = rows.shape
    parts = width // 128
    for j in range(parts):
        ref[pl.ds(start * parts + j, count, stride=parts), :] = rows[:, j * 128 : (j + 1) * 128]


def column_sums(rows):
    return jnp.sum(rows, axis=0, keepdims=True)


def in_three(values):
    high = values.astype(BF16).astype(F32)
    rest = values - high
    middle = rest.astype(BF16).astype(F32)
    return high, middle, rest - middle


def gelu_and_slope(z):
    size = jnp.abs(z)
    t = 1.0 / (1.0 + TAIL_RATE * size)
    poly = jnp.full_like(t, TAIL[-1])
    for coefficient in TAIL[-2::-1]:
        poly = poly * t + coefficient
    bell = jnp.exp2(z * z * (-0.5 * LOG2E))
    tail = poly * t * bell
    cdf = jnp.where(z > 0, 1.0 - tail, tail)
    return z * cdf, cdf + z * bell * (1.0 / math.sqrt(2.0 * math.pi))


def key_extra(head, keys, frames):
    row = lax.broadcasted_iota(jnp.int32, (keys, 128), 0)
    lane = lax.broadcasted_iota(jnp.int32, (keys, 128), 1) - head * 16
    mask = jnp.where(row < frames, 0.0, MASKED)
    ones = jnp.where((lane > 0) & (lane < 4), 1.0, 0.0)
    return jnp.where(lane == 0, mask, ones).astype(BF16)


class Place:
    def __init__(self, mesh_shape):
        self.batch, self.shard = mesh_shape
        self.deep = self.batch // 2
        b, s = lax.axis_index("batch"), lax.axis_index("shard")
        self.z, self.x, self.y, self.core = b // 2, b % 2, s // 2, s % 2
        self.me = b * self.shard + s
        self.square = self.x * 2 + self.y

    def moved(self, dz=0, dxy=0, flip=0):
        dx, dy = dxy // 2, dxy % 2
        x = 1 - self.x if dx else self.x
        y = 1 - self.y if dy else self.y
        core = 1 - self.core if flip else self.core
        return (self.z + self.deep + dz) % self.deep * 2 + x, y * 2 + core

    def block(self, dz=0, dxy=0, flip=0):
        b, s = self.moved(-dz, dxy, flip)
        return b * self.shard + s

    def partners(self):
        far = [self.moved(dz=dz) for dz in range(1, self.deep)]
        near = [self.moved(dxy=dxy) for dxy in range(1, 4)]
        return far + near + [self.moved(flip=1)]

    def greet(self):
        barrier = pltpu.get_barrier_semaphore()
        for partner in self.partners():
            pl.semaphore_signal(barrier, inc=1, device_id=partner, device_id_type=MESH)

    def meet(self):
        pl.semaphore_wait(pltpu.get_barrier_semaphore(), self.deep + 3)


class Spread:
    def __init__(self, place, own, table, send_sem, recv_sem, relayed=False):
        self.place, self.own, self.table = place, own, table
        self.direct = range(1, 3) if relayed else range(1, 4)
        self.send_sem, self.recv_sem = send_sem, recv_sem
        self.started = []

    def copy(self, slot, dz, dxy, device):
        block = self.place.block(dz, dxy)
        here = dz == 0 and dxy == 0
        return pltpu.make_async_remote_copy(
            src_ref=self.own if here else self.table.at[block],
            dst_ref=self.table.at[block],
            send_sem=self.send_sem.at[slot],
            recv_sem=self.recv_sem.at[slot],
            device_id=device,
            device_id_type=MESH,
        )

    def far(self, dz):
        return self.copy(dz - 1, 0, 0, self.place.moved(dz=dz))

    def near(self, dz, dxy):
        slot = self.place.deep - 1 + dz * 3 + dxy - 1
        return self.copy(slot, dz, 0, self.place.moved(dxy=dxy))

    def across(self, dz, dxy):
        slot = self.place.deep * 4 - 1 + dz * 4 + dxy
        return self.copy(slot, dz, dxy, self.place.moved(flip=1))

    def corner(self, dz, dxy):
        count = self.table.shape[1]
        middle = -(-count // 32) * 16
        part = pl.ds(0, middle) if dxy == 2 else pl.ds(middle, count - middle)
        slot = self.place.deep - 1 + dz * 3 + 2 if dxy == 2 else self.place.deep * 8 - 1 + dz
        block = self.place.block(dz, dxy)
        return pltpu.make_async_remote_copy(
            src_ref=self.table.at[block, part],
            dst_ref=self.table.at[block, part],
            send_sem=self.send_sem.at[slot],
            recv_sem=self.recv_sem.at[slot],
            device_id=self.place.moved(dxy=3 - dxy),
            device_id_type=MESH,
        )

    def launch(self, copy):
        copy.start()
        self.started.append(copy)

    def begin_far(self):
        for dz in range(1, self.place.deep):
            self.launch(self.far(dz))

    def begin_near(self):
        for dxy in self.direct:
            self.launch(self.near(0, dxy))
        self.launch(self.across(0, 0))

    def relay_far(self):
        for dz in range(1, self.place.deep):
            self.far(dz).wait_recv()
            for dxy in self.direct:
                self.launch(self.near(dz, dxy))
            self.launch(self.across(dz, 0))

    def relay_near(self, low, high):
        for dz in range(low, high):
            for dxy in self.direct:
                self.near(dz, dxy).wait_recv()
                if 3 not in self.direct:
                    self.launch(self.corner(dz, dxy))
                self.launch(self.across(dz, dxy))

    def relay_corner(self, low, high):
        for dz in range(low, high):
            for dxy in (1, 2):
                self.corner(dz, dxy).wait_recv()
            self.launch(self.across(dz, 3))

    def arrive(self):
        for dz in range(self.place.deep):
            for dxy in range(4):
                self.across(dz, dxy).wait_recv()

    def drain(self):
        deep = self.place.deep
        for dz in range(1, deep):
            self.far(dz).wait_send()
        for dz in range(deep):
            for dxy in self.direct:
                self.near(dz, dxy).wait_send()
            if 3 not in self.direct:
                for dxy in (1, 2):
                    self.corner(dz, dxy).wait_send()
        for dz in range(deep):
            for dxy in range(4):
                self.across(dz, dxy).wait_send()


def small_tile(vectors, long):
    wide = lambda v: jnp.concatenate([v, jnp.zeros((1, 128 - v.shape[1]), F32)], axis=1)
    long = long.astype(F32).reshape(1, -1)
    lines = [wide(v.astype(F32).reshape(1, -1)) for v in vectors]
    lines += [wide(long[:, 16 * c : 16 * c + 16]) for c in range(4)]
    lines.append(jnp.zeros((128 - len(lines), 128), F32))
    return jnp.concatenate(lines, axis=0).T[:16].astype(BF16)


def small_lines(tiles):
    width = 16 * tiles.shape[0]
    columns = tiles.reshape(width, 128).astype(F32).T
    quarters = width // 128
    rows = [
        jnp.concatenate(
            [columns[8 + c : 9 + c, 128 * j : 128 * j + 128] for c in range(4)], axis=1
        )
        for j in range(quarters)
    ]
    rows.append(jnp.zeros((8 - quarters, width), F32))
    source = lax.broadcasted_iota(jnp.int32, (width, width), 0)
    target = lax.broadcasted_iota(jnp.int32, (width, width), 1)
    goal = source // 16 % 8 * 64 + source // 128 * 16 + source % 16
    moved = jnp.where(goal == target, 1.0, 0.0).astype(BF16)
    long = dot(jnp.concatenate(rows, axis=0).astype(BF16), moved, NN)
    return jnp.concatenate([long, columns[:8]], axis=0)


def matrix(table, first, count=16):
    part = table[:, first : first + count, :]
    return part.reshape(part.shape[0] * count, part.shape[2])


def attend_kernel(frames, mesh_shape, *refs):
    x_in = refs[0]
    if mesh_shape is None:
        table, small_ref = refs[1:3]
        refs = refs[3:]
    else:
        wq_own, wk_own, wv_own, wo_own, wu_own, wd_own = refs[1:7]
        short_own = refs[7:16]
        refs = refs[16:]
    outputs, refs = refs[:6], refs[6:]
    if mesh_shape is not None:
        small_ref, first_ref, second_ref = refs[:3]
        refs = refs[3:]
    results, refs = refs[:6], refs[6:]
    qa_ref, ka_ref, vt_ref, ht_ref, ot_ref, qe_ref = results
    x_ref, units, rows_low, scores, peaks, key_ext, log_rows, load, store = refs[:9]
    padded, width = units.shape
    depth = width // HEADS
    read = pltpu.make_async_copy(x_in, x_ref, load)
    read.start()

    def unit_rows():
        read.wait()
        for start in range(0, padded, ROWS):
            count = min(ROWS, frames - start)
            units[start : start + count, :] = normalize(
                x_ref[start : start + count, :].astype(F32)
            )[0]
        units[frames:, :] = jnp.zeros((padded - frames, width), F32)

    if mesh_shape is None:
        unit_rows()
    else:
        table_a, table_b, own, *sems, keep = refs[9:]
        place = Place(mesh_shape)
        place.greet()
        part_a = Spread(place, table_a.at[place.me], table_a, *sems[0:2])
        part_b = Spread(place, table_b.at[place.me], table_b, *sems[2:4])
        second = Spread(place, own, second_ref, *sems[4:6], relayed=True)
        early = EARLY_HEADS * depth
        if early > 128:
            table_a[place.me, 48:64, 128:] = jnp.zeros((16, early - 128), BF16)
        for i, weight_own in enumerate((wq_own, wk_own, wv_own)):
            table_a[place.me, 16 * i : 16 * i + 16, :] = weight_own[:, :early]
            table_b[place.me, 16 * i : 16 * i + 16, :] = weight_own[:, early:]
        table_a[place.me, 48:64, 0:128] = small_tile(
            [ref[...] for ref in short_own[:8]], short_own[8][...]
        )
        place.meet()
        part_a.begin_far()
        part_a.begin_near()
        own[0:16, :] = wo_own[...]
        chunks = wu_own.shape[1] // FF_CHUNK
        for j in range(chunks):
            own[16 + 16 * j : 32 + 16 * j, :] = wu_own[:, j * FF_CHUNK : (j + 1) * FF_CHUNK]
        own[16 + 16 * chunks :, :] = wd_own[...]
        unit_rows()
        part_a.relay_far()
        part_b.begin_far()
        part_a.relay_near(0, place.deep)
        part_b.begin_near()
        second.begin_far()
        second.begin_near()
        keep_own = pltpu.make_async_copy(own, second_ref.at[place.me], keep.at[0])
        keep_own.start()
        part_a.arrive()
        keep_a = pltpu.make_async_copy(
            table_a.at[:, 0:48], first_ref.at[:, :, pl.ds(0, early)], keep.at[1]
        )
        keep_a.start()
        keep_b = pltpu.make_async_copy(
            table_b, first_ref.at[:, :, pl.ds(early, width - early)], keep.at[2]
        )
        small_ref[...] = small_lines(table_a[:, 48:64, 0:128])

    writes = [
        pltpu.make_async_copy(results[i], outputs[i], store.at[i]) for i in (0, 1, 2, 3)
    ]
    last_write = pltpu.make_async_copy(qe_ref, outputs[5], store.at[4])

    def head_write(head):
        rows = pl.ds(pl.multiple_of(head * depth, depth), depth)
        return pltpu.make_async_copy(ot_ref.at[rows], outputs[4].at[rows], store.at[5 + head])

    bq, bv, gain, shift = (small_ref[r : r + 1, :] for r in (8, 9, 12, 13))

    def project(heads, i, carry):
        low, high = heads
        lanes = slice(low * depth, high * depth)

        def weight(which):
            if mesh_shape is None:
                return matrix(table[:, :, lanes], 16 * which)
            return matrix(table_a if low == 0 else table_b, 16 * which)

        rows = pl.ds(pl.multiple_of(i * PROJECT_ROWS, PROJECT_ROWS), PROJECT_ROWS)
        if low == 0:
            h1 = (units[rows, :] * gain + shift).astype(BF16)
            rows_low[rows, :] = h1
            ht_ref[:, rows] = h1.T
        else:
            h1 = rows_low[rows, :]
        q = (dot(h1, weight(0), NN) + bq[:, lanes]).astype(BF16)
        k = dot(h1, weight(1), NN).astype(BF16).astype(F32)
        k = k * (LOG2E / math.sqrt(depth))
        v = (dot(h1, weight(2), NN) + bv[:, lanes]).astype(BF16)
        k_high = k.astype(BF16)
        k_low = (k - k_high.astype(F32)).astype(BF16)
        vt_ref[lanes, rows] = v.T
        for h in range(low, high):
            cols = slice((h - low) * depth, (h - low + 1) * depth)
            qa_ref[h, rows, :] = jnp.concatenate([q[:, cols], q[:, cols]], axis=1)
            ka_ref[h, rows, :] = jnp.concatenate([k_high[:, cols], k_low[:, cols]], axis=1)
        return carry

    lax.fori_loop(0, padded // PROJECT_ROWS, functools.partial(project, (0, EARLY_HEADS)), 0)

    def project_rest():
        if mesh_shape is not None:
            part_b.arrive()
            keep_b.start()
        lax.fori_loop(0, padded // PROJECT_ROWS, functools.partial(project, (EARLY_HEADS, HEADS)), 0)
        for copy in writes:
            copy.start()

    blocks = padded // QUERIES
    steps = HEADS * blocks
    lane = lax.broadcasted_iota(jnp.int32, (QUERIES, 128), 1)
    query_ext = jnp.where(lane % 16 == 0, 1.0, 0.0).astype(BF16)

    def score(step, slot):
        head = step // blocks
        rows = pl.ds(pl.multiple_of((step % blocks) * QUERIES, QUERIES), QUERIES)
        key_ext[slot] = key_extra(head, padded, frames)
        left = jnp.concatenate([ka_ref[head], key_ext[slot]], axis=1)
        right = jnp.concatenate([qa_ref[head, rows, :], query_ext], axis=1)
        s = dot(left, right, NT)
        scores[slot] = s
        peaks[slot] = jnp.max(s, axis=0, keepdims=True)

    def finish(step, slot):
        head = step // blocks
        cols = pl.ds(pl.multiple_of((step % blocks) * QUERIES, QUERIES), QUERIES)
        peak = peaks[slot]
        weights = jnp.exp2(scores[slot] - peak).astype(BF16)
        rows = pl.ds(pl.multiple_of(head * depth, depth), depth)
        ones = jnp.ones((16, padded), BF16)
        mixed = dot(jnp.concatenate([vt_ref[rows, :], ones], axis=0), weights, NN)
        total = mixed[depth : depth + 1, :]
        ot_ref[rows, cols] = (mixed[:depth, :] * (1.0 / total)).astype(BF16)
        log_rows[head, :, cols] = peak + jnp.log2(total)

    score(0, 0)

    def pair(i, carry):
        if mesh_shape is not None:
            pl.when(i == B_FAR_AT)(part_b.relay_far)
            pl.when(i == B_NEAR_AT)(functools.partial(part_b.relay_near, 0, place.deep))
            pl.when(i == FAR_AT)(second.relay_far)
            pl.when(i == NEAR_AT)(functools.partial(second.relay_near, 0, 2))
            pl.when(i == NEAR_AT + 1)(functools.partial(second.relay_near, 2, place.deep))
            pl.when(i == CORNER_AT)(functools.partial(second.relay_corner, 0, 2))
        pl.when(i == EARLY_HEADS - 1)(project_rest)
        score(i * 2 + 1, 1)
        finish(i * 2, 0)
        score(jnp.minimum(i * 2 + 2, steps - 1), 0)
        finish(i * 2 + 1, 1)
        head_write(i).start()
        return carry

    lax.fori_loop(0, steps // 2, pair, 0)

    def extend(i, carry):
        rows = pl.ds(pl.multiple_of(i * ROWS, ROWS), ROWS)
        pieces = []
        for h in range(HEADS):
            high, middle, low = in_three(-log_rows[h, :, rows])
            pieces += [jnp.ones((1, ROWS), F32), high, middle, low, jnp.zeros((12, ROWS), F32)]
        qe_ref[rows, :] = jnp.concatenate(pieces, axis=0).T.astype(BF16)
        return carry

    if mesh_shape is not None:
        second.relay_corner(2, place.deep)
    lax.fori_loop(0, padded // ROWS, extend, 0)
    last_write.start()
    for copy in writes + [last_write] + [head_write(head) for head in range(HEADS)]:
        copy.wait()
    if mesh_shape is not None:
        second.arrive()
        keep_own.wait()
        keep_a.wait()
        keep_b.wait()
        part_a.drain()
        part_b.drain()
        second.drain()


def attend(mesh_shape, x, *rest):
    frames, width = x.shape
    padded = -(-frames // QUERIES) * QUERIES
    blocks = width // 16
    vmem = pl.BlockSpec(memory_space=pltpu.VMEM)
    hbm = pl.BlockSpec(memory_space=pltpu.HBM)
    out_shape = [
        jax.ShapeDtypeStruct((HEADS, padded, 128), BF16),
        jax.ShapeDtypeStruct((HEADS, padded, 128), BF16),
        jax.ShapeDtypeStruct((width, padded), BF16),
        jax.ShapeDtypeStruct((width, padded), BF16),
        jax.ShapeDtypeStruct((width, padded), BF16),
        jax.ShapeDtypeStruct((padded, 128), BF16),
    ]
    scratch = [pltpu.VMEM(shape.shape, shape.dtype) for shape in out_shape]
    scratch += [
        pltpu.VMEM((frames, width), BF16),
        pltpu.VMEM((padded, width), F32),
        pltpu.VMEM((padded, width), BF16),
        pltpu.VMEM((2, padded, QUERIES), F32),
        pltpu.VMEM((2, 1, QUERIES), F32),
        pltpu.VMEM((2, padded, 128), BF16),
        pltpu.VMEM((HEADS, 1, padded), F32),
        pltpu.SemaphoreType.DMA,
        pltpu.SemaphoreType.DMA((5 + HEADS,)),
    ]
    out_specs = [hbm] * 6
    options = {}
    if mesh_shape is not None:
        early = EARLY_HEADS * (width // HEADS)
        hidden = rest[4].shape[1]
        own_rows = 16 + hidden // FF_CHUNK * 16 + rest[5].shape[0]
        out_shape += [
            jax.ShapeDtypeStruct((16, width), F32),
            jax.ShapeDtypeStruct((blocks, 48, width), BF16),
            jax.ShapeDtypeStruct((blocks, own_rows, width), BF16),
        ]
        out_specs += [vmem, hbm, hbm]
        scratch += [
            pltpu.VMEM((blocks, 64, early), BF16),
            pltpu.VMEM((blocks, 48, width - early), BF16),
            pltpu.VMEM((own_rows, width), BF16),
        ]
        scratch += [pltpu.SemaphoreType.DMA((blocks - 1,)) for _ in range(4)]
        scratch += [pltpu.SemaphoreType.DMA((mesh_shape[0] * 4 + 3,)) for _ in range(2)]
        scratch += [pltpu.SemaphoreType.DMA((3,))]
        options = dict(collective_id=0, has_side_effects=True)
    return pl.pallas_call(
        functools.partial(attend_kernel, frames, mesh_shape),
        out_shape=out_shape,
        in_specs=[hbm] + [vmem] * len(rest),
        out_specs=out_specs,
        scratch_shapes=scratch,
        compiler_params=pltpu.CompilerParams(vmem_limit_bytes=60 << 20, **options),
        name="attend",
    )(x, *rest)


def mlp_kernel(
    frames,
    flag_ref,
    x_ref,
    cot_ref,
    ot_ref,
    table_in,
    vec_ref,
    out_ref,
    dx_ref,
    do_ref,
    de_ref,
    grads_out,
    small_ref,
    gwo,
    gwu,
    gwd,
    table,
    grads_ref,
    load,
    store,
):
    step = pl.program_id(0)
    rows, width = x_ref.shape
    chunks = gwu.shape[0]
    depth = width // HEADS
    down = table.shape[1] - 16 - 16 * chunks
    per_chunk = FF_CHUNK // down

    def up_part(j):
        return matrix(table, 16 + 16 * j)

    def down_part(j):
        part = table[j * per_chunk : (j + 1) * per_chunk, 16 + 16 * chunks :, :]
        return part.reshape(FF_CHUNK, width)

    bounds = (0, 16, 16 + 16 * chunks, table.shape[1])
    loads = [
        pltpu.make_async_copy(table_in.at[:, low:high], table.at[:, low:high], load.at[i])
        for i, (low, high) in enumerate(zip(bounds, bounds[1:]))
    ]

    @pl.when(step == 0)
    def _():
        for copy in loads:
            copy.start()
        small_ref[...] = jnp.zeros_like(small_ref)
        loads[0].wait()

    def kept(ref, *index):
        return jnp.where(step == 0, 0.0, ref[index] if index else ref[...])

    flag = flag_ref[0].astype(F32)
    inside = step * rows + lax.broadcasted_iota(jnp.int32, (rows, width), 0) < frames
    x = jnp.where(inside, x_ref[...].astype(F32), 0.0)
    dy = jnp.where(inside, cot_ref[...].astype(F32), 0.0) * flag
    dy_low = dy.astype(BF16)
    bo, bd, gain, shift = (vec_ref[r : r + 1, :] for r in (10, 11, 14, 15))
    wo = matrix(table, 0)
    ot = ot_ref[...]
    o = ot.T
    x1 = x + (dot(o, wo, NN) + bo)
    unit, inv_std = normalize(x1)
    h2 = (unit * gain + shift).astype(BF16)
    h2t = h2.T

    @pl.when(step == 0)
    def _():
        loads[1].wait()
        loads[2].wait()

    z_next = dot(h2, up_part(0), NN)
    out = x1 + bd
    dh2 = jnp.zeros((rows, width), F32)
    for j in range(chunks):
        z = z_next + vec_ref[j : j + 1, :]
        if j + 1 < chunks:
            z_next = dot(h2, up_part(j + 1), NN)
        dg = dot(dy_low, down_part(j), NT)
        g, slope = gelu_and_slope(z)
        g = g.astype(BF16)
        dz = (dg * slope).astype(BF16)
        out = out + dot(g, down_part(j), NN)
        gwd[j] = kept(gwd, j) + dot(g, dy_low, TN)
        gwu[j] = kept(gwu, j) + dot(h2t, dz, NN)
        small_ref[j : j + 1, :] += column_sums(dz.astype(F32))
        dh2 = dh2 + dot(dz, up_part(j), NT)
    store_rows(out_ref, 0, out * flag)
    dx1 = dy + normalize_back(dh2, unit, inv_std, gain)
    dx_ref[...] = dx1
    da = dx1.astype(BF16)
    gwo[...] = kept(gwo) + dot(ot, da, NN)
    do = dot(da, wo, NT).astype(BF16)
    small_ref[10:11, :] += column_sums(da.astype(F32))
    small_ref[11:12, :] += column_sums(dy)
    small_ref[14:15, :] += column_sums(dh2 * unit)
    small_ref[15:16, :] += column_sums(dh2)
    do_ref[...] = do
    prod = do.astype(F32) * o.astype(F32)
    high = prod.astype(BF16)
    low = (prod - high.astype(F32)).astype(BF16)
    owner = lax.broadcasted_iota(jnp.int32, (width, 128), 0) // depth
    pick = lax.broadcasted_iota(jnp.int32, (width, 128), 1) // 16
    pick = jnp.where(owner == pick, 1.0, 0.0).astype(BF16)
    high, middle, low = in_three(-(dot(high, pick, NN) + dot(low, pick, NN)))
    lane = lax.broadcasted_iota(jnp.int32, (rows, 128), 1) % 16
    extra = jnp.where(lane == 1, middle, jnp.where(lane == 2, low, 0.0))
    de_ref[...] = jnp.where(lane == 0, high, extra).astype(BF16)

    @pl.when(step == pl.num_programs(0) - 1)
    def _():
        split = lambda part, count: part.astype(BF16).reshape(-1, count, width)
        copies = []

        def send(*index):
            copies.append(
                pltpu.make_async_copy(
                    grads_ref.at[index], grads_out.at[index], store.at[len(copies)]
                )
            )
            copies[-1].start()

        for j in range(chunks):
            rows_up = slice(16 + 16 * j, 32 + 16 * j)
            grads_ref[:, rows_up, :] = split(gwu[j], 16)
            send(slice(None), rows_up)
            blocks_down = slice(j * per_chunk, (j + 1) * per_chunk)
            rows_down = slice(16 + 16 * chunks, table.shape[1])
            grads_ref[blocks_down, rows_down, :] = split(gwd[j], down)
            send(blocks_down, rows_down)
        grads_ref[:, 0:16, :] = split(gwo[...], 16)
        send(slice(None), slice(0, 16))
        for copy in copies:
            copy.wait()


def mlp(flag, x, cot, ot, table, vectors):
    frames, width = x.shape
    padded = ot.shape[1]
    blocks, rows = table.shape[:2]
    chunks = (rows - 16) * blocks // (2 * FF_CHUNK)
    by_rows = pl.BlockSpec((MLP_ROWS, width), lambda i: (i, 0))
    fixed = lambda shape: pl.BlockSpec(
        shape, lambda i: (0,) * len(shape), pipeline_mode=pl.Buffered(1)
    )
    return pl.pallas_call(
        functools.partial(mlp_kernel, frames),
        grid=(padded // MLP_ROWS,),
        out_shape=[
            jax.ShapeDtypeStruct((frames * width // 128, 128), F32),
            jax.ShapeDtypeStruct((frames, width), F32),
            jax.ShapeDtypeStruct((padded, width), BF16),
            jax.ShapeDtypeStruct((padded, 128), BF16),
            jax.ShapeDtypeStruct(table.shape, BF16),
            jax.ShapeDtypeStruct((16, width), F32),
        ],
        in_specs=[
            pl.BlockSpec(memory_space=pltpu.SMEM),
            by_rows,
            by_rows,
            pl.BlockSpec((width, MLP_ROWS), lambda i: (0, i)),
            pl.BlockSpec(memory_space=pltpu.HBM),
            fixed((16, width)),
        ],
        out_specs=[
            pl.BlockSpec((MLP_ROWS * width // 128, 128), lambda i: (i, 0)),
            by_rows,
            by_rows,
            pl.BlockSpec((MLP_ROWS, 128), lambda i: (i, 0)),
            pl.BlockSpec(memory_space=pltpu.HBM),
            fixed((16, width)),
        ],
        scratch_shapes=[
            pltpu.VMEM((width, width), F32),
            pltpu.VMEM((chunks, width, FF_CHUNK), F32),
            pltpu.VMEM((chunks, FF_CHUNK, width), F32),
            pltpu.VMEM(table.shape, BF16),
            pltpu.VMEM(table.shape, BF16),
            pltpu.SemaphoreType.DMA((3,)),
            pltpu.SemaphoreType.DMA((2 * chunks + 1,)),
        ],
        compiler_params=pltpu.CompilerParams(
            vmem_limit_bytes=60 << 20, dimension_semantics=("arbitrary",)
        ),
        name="mlp",
    )(flag, x, cot, ot, table, vectors)


class Gather:
    def __init__(self, place, source, from_core, halves, from_near, quarter, from_far, sems):
        self.place, self.source = place, source
        self.from_core, self.halves = from_core, halves
        self.from_near, self.quarter = from_near, quarter
        self.from_far = from_far
        self.send_sem, self.recv_sem = sems

    def copy(self, slot, src, dst, device):
        return pltpu.make_async_remote_copy(
            src_ref=src,
            dst_ref=dst,
            send_sem=self.send_sem.at[slot],
            recv_sem=self.recv_sem.at[slot],
            device_id=device,
            device_id_type=MESH,
        )

    def across(self):
        place = self.place
        return [
            self.copy(
                z, self.source.at[z, :, 1 - place.core], self.from_core.at[z], place.moved(flip=1)
            )
            for z in range(place.deep)
        ]

    def near(self):
        place = self.place
        copies = []
        for dxy in range(1, 4):
            b, s = place.moved(dxy=dxy)
            square = b % 2 * 2 + s // 2
            copies.append(
                self.copy(
                    place.deep + dxy - 1,
                    self.halves.at[:, square],
                    self.from_near.at[dxy - 1],
                    (b, s),
                )
            )
        return copies

    def far(self):
        place = self.place
        copies = []
        for dz in range(1, place.deep):
            z = (place.z + dz) % place.deep
            copies.append(
                self.copy(
                    place.deep + 2 + dz,
                    self.quarter.at[z],
                    self.from_far.at[dz - 1],
                    place.moved(dz=dz),
                )
            )
        return copies

    def fold_across(self, own):
        for copy in self.across():
            copy.wait_recv()

        def one(i, carry):
            z, q = i // 4, i % 4
            total = own(z, q).astype(F32) + self.from_core[z, q].astype(F32)
            self.halves[z, q] = total.astype(BF16)
            return carry

        lax.fori_loop(0, self.place.deep * 4, one, 0)
        for copy in self.near():
            copy.start()

    def fold_near(self):
        for copy in self.near():
            copy.wait_recv()

        def one(z, carry):
            total = self.halves[z, self.place.square].astype(F32)
            for dxy in range(3):
                total = total + self.from_near[dxy, z].astype(F32)
            self.quarter[z] = total.astype(BF16)
            return carry

        lax.fori_loop(0, self.place.deep, one, 0)
        for copy in self.far():
            copy.start()

    def result(self):
        for copy in self.far():
            copy.wait_recv()
        total = self.quarter[self.place.z].astype(F32)
        for dz in range(self.place.deep - 1):
            total = total + self.from_far[dz].astype(F32)
        return total

    def drain(self):
        for copy in self.across() + self.near() + self.far():
            copy.wait_send()


class SmallSum:
    def __init__(self, place, buffers, received, sems):
        self.place, self.buffers, self.received = place, buffers, received
        self.send_sem, self.recv_sem = sems

    def copies(self, stage):
        place = self.place
        if stage == 0:
            devices, first = [place.moved(flip=1)], 0
        elif stage == 1:
            devices, first = [place.moved(dxy=dxy) for dxy in range(1, 4)], 1
        else:
            devices, first = [place.moved(dz=dz) for dz in range(1, place.deep)], 4
        return [
            pltpu.make_async_remote_copy(
                src_ref=self.buffers.at[stage],
                dst_ref=self.received.at[first + i],
                send_sem=self.send_sem.at[first + i],
                recv_sem=self.recv_sem.at[first + i],
                device_id=device,
                device_id_type=MESH,
            )
            for i, device in enumerate(devices)
        ]

    def send(self, stage, value):
        self.buffers[stage] = value
        for copy in self.copies(stage):
            copy.start()

    def receive(self, stage):
        total = self.buffers[stage]
        first = (0, 1, 4)[stage]
        for i, copy in enumerate(self.copies(stage)):
            copy.wait_recv()
            total = total + self.received[first + i]
        return total

    def drain(self):
        for stage in range(3):
            for copy in self.copies(stage):
                copy.wait_send()


def own_small(total, place):
    width = total.shape[1]
    line = lax.broadcasted_iota(jnp.int32, total.shape, 0)
    short = pltpu.roll(total, width - place.me * 16, 1)
    long = jnp.sum(jnp.where(line == place.me // 8, total, 0.0), axis=0, keepdims=True)
    long = pltpu.roll(jnp.broadcast_to(long, total.shape), width - place.me % 8 * 64, 1)
    return jnp.where(line == 0, long, short)[:, :128]


def attend_back_kernel(frames, mesh_shape, *refs):
    x_in, dx_in, qa_in, ka_in, vt_in, ht_in, qe_in, do_in, de_in, table_in = refs[:10]
    vec_ref, small_in = refs[10:12]
    refs = refs[12:]
    if mesh_shape is None:
        dinput_out, source, small_ref = refs[:3]
        refs = refs[3:]
    else:
        grads_ref = refs[0]
        dinput_out, gq_ref, gk_ref, gv_ref, go_ref, gu_ref, gd_ref = refs[1:8]
        short_refs = refs[8:17]
        refs = refs[17:]
    x_ref, dx_ref, qa_ref, ka_ref, vt_ref, ht_ref, qe_ref, do_ref, de_ref, table = refs[:10]
    dinput_ref, load, store = refs[10:13]
    dq, dkt, dvt, sum_k, sum_v, key_ext, value_ext, small = refs[13:21]
    refs = refs[21:]

    padded = qa_ref.shape[1]
    width = ht_ref.shape[0]
    depth = width // HEADS

    def head_loads(head):
        return [
            pltpu.make_async_copy(qa_in.at[head], qa_ref.at[head], load.at[2 * head]),
            pltpu.make_async_copy(ka_in.at[head], ka_ref.at[head], load.at[2 * head + 1]),
        ]

    sources = (vt_in, do_in, de_in, qe_in, ht_in, table_in.at[:, 0:48], x_in, dx_in)
    targets = (vt_ref, do_ref, de_ref, qe_ref, ht_ref, table, x_ref, dx_ref)
    loads = [
        pltpu.make_async_copy(source_ref, target_ref, load.at[2 * HEADS + i])
        for i, (source_ref, target_ref) in enumerate(zip(sources, targets))
    ]
    for copy in head_loads(0) + loads[:4]:
        copy.start()
    for head in range(1, HEADS):
        for copy in head_loads(head):
            copy.start()
    for copy in loads[4:]:
        copy.start()

    if mesh_shape is not None:
        place = Place(mesh_shape)
        place.greet()
        parts = []
        for _ in PARTS:
            parts.append(Gather(place, refs[0], *refs[1:6], refs[6:8]))
            refs = refs[8:]
        second = Gather(place, grads_ref, *refs[:5], refs[5:7])
        shorts = SmallSum(place, refs[7], refs[8], refs[9:11])
        second_half, keep = refs[11:]
        keep_half = pltpu.make_async_copy(grads_ref.at[:, :, place.core], second_half, keep)
        place.meet()
        for copy in second.across():
            copy.start()
        keep_half.start()
    for copy in loads[:4]:
        copy.wait()

    def second_across():
        keep_half.wait()
        second.fold_across(lambda z, q: second_half[z, q])

    lane_half = lax.broadcasted_iota(jnp.int32, (padded, 128), 1) < depth

    def weight_grads(t):
        low, high = PARTS[t]
        cols = slice(low * depth, high * depth)
        wide = (high - low) * depth
        queries = jnp.concatenate(
            [jnp.where(lane_half, dq[h], dq[h + 1]) for h in range(low, high, 2)], axis=1
        )
        ht = ht_ref[...]
        grads = (
            dot(ht, queries, NN),
            dot(ht, dkt[cols, :], NT),
            dot(ht, dvt[cols, :], NT),
        )
        for i, grad in enumerate(grads):
            grad = grad.astype(BF16)
            if mesh_shape is None:
                source[:, 16 * i : 16 * i + 16, cols] = grad.reshape(-1, 16, wide)
            else:
                target = parts[t].source
                target[:, :, :, 16 * i : 16 * i + 16, :] = grad.reshape(
                    target.shape[:3] + (16, wide)
                )
        if mesh_shape is not None:
            for copy in parts[t].across():
                copy.start()

    def fold_part(t):
        parts[t].fold_across(lambda z, q: parts[t].source[z, q, place.core])

    def part_result(t):
        total = parts[t].result()
        for i, ref in enumerate((gq_ref, gk_ref, gv_ref)):
            ref[:, PARTS[t][0] * depth : PARTS[t][1] * depth] = total[16 * i : 16 * i + 16]

    def early_weight_grads(t):
        if t == 0:
            loads[4].wait()
        weight_grads(t)

    last = len(PARTS) - 1

    def one_head(head, carry):
        for t in range(last):
            pl.when(head == PARTS[t][1])(functools.partial(early_weight_grads, t))
            if mesh_shape is not None and PARTS[t][1] + 1 < HEADS:
                pl.when(head == PARTS[t][1] + 1)(functools.partial(fold_part, t))
        if mesh_shape is not None:
            pl.when(head == ACROSS_AT)(second_across)
            pl.when(head == SQUARE_AT)(second.fold_near)
        for copy in head_loads(head):
            copy.wait()
        key_ext[...] = key_extra(head, padded, frames)
        line = lax.broadcasted_iota(jnp.int32, (128, padded), 0)
        mine = pl.ds(pl.multiple_of(head // 2 * 128, 128), 128)
        values = jnp.where(line // depth == head % 2, vt_ref[mine, :].astype(F32), 0.0)
        value_ext[0:128, :] = values.astype(BF16)
        extra = jnp.where((line // 16 == head) & (line % 16 < 3), 1.0, 0.0)
        value_ext[128:256, :] = extra.astype(BF16)
        for i in range(padded // ROWS):
            rows = slice(i * ROWS, (i + 1) * ROWS)
            q = qa_ref[head, rows, :]
            d = do_ref[rows, mine]
            turned = d.T
            turned = jnp.where(head % 2 == 0, turned[:depth], turned[depth:])
            s = dot(
                jnp.concatenate([q, qe_ref[rows, :]], axis=1),
                jnp.concatenate([ka_ref[head], key_ext[...]], axis=1),
                NT,
            )
            p = jnp.exp2(s)
            dp = dot(jnp.concatenate([d, de_ref[rows, :]], axis=1), value_ext[...], NN)
            ds = (p * dp).astype(BF16)
            p = p.astype(BF16)
            new_v = dot(turned, p, NN)
            new_k = dot(q[:, :depth], ds, TN)
            if i == 0:
                sum_v[...] = new_v
                sum_k[...] = new_k
            else:
                sum_v[...] += new_v
                sum_k[...] += new_k
            both = dot(ds, ka_ref[head], NN)
            both = both + pltpu.roll(both, depth, 1)
            dq[head, rows, :] = (both * LN2).astype(BF16)
        out_rows = pl.ds(pl.multiple_of(head * depth, depth), depth)
        dkt[out_rows, :] = (sum_k[...] * (1.0 / math.sqrt(depth))).astype(BF16)
        dvt[out_rows, :] = sum_v[...].astype(BF16)
        return carry

    lax.fori_loop(0, HEADS, one_head, 0)

    weight_grads(last)
    for copy in loads[5:]:
        copy.wait()
    if mesh_shape is not None:
        for t in range(last):
            if PARTS[t][1] + 1 >= HEADS:
                fold_part(t)
            else:
                parts[t].fold_near()
        second_own = second.result()
        chunks = gu_ref.shape[1] // FF_CHUNK
        go_ref[...] = second_own[0:16]
        for j in range(chunks):
            gu_ref[:, j * FF_CHUNK : (j + 1) * FF_CHUNK] = second_own[16 + 16 * j : 32 + 16 * j]
        gd_ref[...] = second_own[16 + 16 * chunks :]

    gain = vec_ref[12:13, :]
    small[...] = small_in[...]
    stores = []
    for index, start in enumerate(range(0, frames, ROWS)):
        if mesh_shape is not None and index == FOLD_AT:
            fold_part(last)
            for t in range(last):
                if PARTS[t][1] + 1 >= HEADS:
                    parts[t].fold_near()
        count = min(ROWS, frames - start)
        rows = slice(start, start + count)
        wide = slice(start, start + ROWS)
        some = lane_half[:ROWS]
        dq_rows = jnp.concatenate(
            [jnp.where(some, dq[h, wide, :], dq[h + 1, wide, :]) for h in range(0, HEADS, 2)],
            axis=1,
        )
        dk_rows = dkt[:, wide].T
        dv_rows = dvt[:, wide].T
        dh1 = (
            dot(dq_rows, matrix(table, 0), NT)
            + dot(dk_rows, matrix(table, 16), NT)
            + dot(dv_rows, matrix(table, 32), NT)
        )
        small[8:9, :] += column_sums(dq_rows.astype(F32))
        small[9:10, :] += column_sums(dv_rows.astype(F32))
        dh1 = dh1[:count]
        unit, inv_std = normalize(x_ref[rows, :].astype(F32))
        small[12:13, :] += column_sums(dh1 * unit)
        small[13:14, :] += column_sums(dh1)
        dinput = dx_ref[rows, :] + normalize_back(dh1, unit, inv_std, gain)
        store_rows(dinput_ref, start, dinput)
        part = pl.ds(start * (width // 128), count * (width // 128))
        stores.append(
            pltpu.make_async_copy(dinput_ref.at[part], dinput_out.at[part], store.at[index])
        )
        stores[-1].start()
    if mesh_shape is None:
        small_ref[...] = small[...]
    else:
        shorts.send(0, small[...])
        shorts.send(1, shorts.receive(0))
        parts[last].fold_near()
        shorts.send(2, shorts.receive(1))
        for t in range(last):
            part_result(t)
        second.drain()
        for t in range(last):
            parts[t].drain()
        part_result(last)
        small_own = own_small(shorts.receive(2), place)
        for i, ref in enumerate(short_refs[:8]):
            ref[...] = small_own[8 + i, :16]
        short_refs[8][...] = small_own[0, :64]
        parts[last].drain()
        shorts.drain()
    for copy in stores:
        copy.wait()


def attend_back(mesh_shape, x, dx, qa, ka, vt, ht, qe, do, de, table, vectors, small, grads):
    frames, width = x.shape
    padded = ht.shape[1]
    blocks = width // 16
    vmem = pl.BlockSpec(memory_space=pltpu.VMEM)
    hbm = pl.BlockSpec(memory_space=pltpu.HBM)
    args = [x, dx, qa, ka, vt, ht, qe, do, de, table, vectors, small]
    in_specs = [hbm] * 10 + [vmem] * 2
    lines = frames * width // 128
    out_shape = [jax.ShapeDtypeStruct((lines, 128), F32)]
    scratch = [pltpu.VMEM(array.shape, array.dtype) for array in args[:9]]
    scratch += [
        pltpu.VMEM((blocks, 48, width), BF16),
        pltpu.VMEM((lines, 128), F32),
        pltpu.SemaphoreType.DMA((2 * HEADS + 8,)),
        pltpu.SemaphoreType.DMA((padded // ROWS,)),
        pltpu.VMEM((HEADS, padded, 128), BF16),
        pltpu.VMEM((width, padded), BF16),
        pltpu.VMEM((width, padded), BF16),
        pltpu.VMEM((width // HEADS, padded), F32),
        pltpu.VMEM((width // HEADS, padded), F32),
        pltpu.VMEM((padded, 128), BF16),
        pltpu.VMEM((256, padded), BF16),
        pltpu.VMEM((16, width), F32),
    ]
    options = {}
    if mesh_shape is None:
        out_shape += [
            jax.ShapeDtypeStruct((blocks, 48, width), BF16),
            jax.ShapeDtypeStruct((16, width), F32),
        ]
    else:
        deep = mesh_shape[0] // 2
        rows = grads.shape[1]
        hidden = (rows - 16) * blocks // 2
        args.append(grads.reshape(deep, 4, 2, rows, width))
        in_specs.append(hbm)
        out_shape += [
            jax.ShapeDtypeStruct((16, width), F32),
            jax.ShapeDtypeStruct((16, width), F32),
            jax.ShapeDtypeStruct((16, width), F32),
            jax.ShapeDtypeStruct((16, width), F32),
            jax.ShapeDtypeStruct((16, hidden), F32),
            jax.ShapeDtypeStruct((hidden // blocks, width), F32),
        ]
        out_shape += [jax.ShapeDtypeStruct((16,), F32)] * 8
        out_shape += [jax.ShapeDtypeStruct((hidden // blocks,), F32)]

        def stages(shape):
            return [
                pltpu.VMEM((deep, 4) + shape, BF16),
                pltpu.VMEM((deep, 4) + shape, BF16),
                pltpu.VMEM((3, deep) + shape, BF16),
                pltpu.VMEM((deep,) + shape, BF16),
                pltpu.VMEM((deep - 1,) + shape, BF16),
                pltpu.SemaphoreType.DMA((2 * deep + 2,)),
                pltpu.SemaphoreType.DMA((2 * deep + 2,)),
            ]

        for low, high in PARTS:
            shape = (48, (high - low) * (width // HEADS))
            scratch += [pltpu.VMEM((deep, 4, 2) + shape, BF16)] + stages(shape)
        scratch += stages((rows, width))
        scratch += [
            pltpu.VMEM((3, 16, width), F32),
            pltpu.VMEM((deep + 3, 16, width), F32),
            pltpu.SemaphoreType.DMA((deep + 3,)),
            pltpu.SemaphoreType.DMA((deep + 3,)),
            pltpu.VMEM((deep, 4, rows, width), BF16),
            pltpu.SemaphoreType.DMA,
        ]
        options = dict(collective_id=1, has_side_effects=True)
    return pl.pallas_call(
        functools.partial(attend_back_kernel, frames, mesh_shape),
        out_shape=out_shape,
        in_specs=in_specs,
        out_specs=[hbm] + [vmem] * (len(out_shape) - 1),
        scratch_shapes=scratch,
        compiler_params=pltpu.CompilerParams(vmem_limit_bytes=60 << 20, **options),
        name="attend_back",
    )(*args)


def hand_over_kernel(count, *refs):
    large, small = refs[0], refs[1 : count + 1]
    large_buf, small_buf = refs[2 * count + 2], refs[2 * count + 3 : 3 * count + 3]
    large_out, small_out = refs[count + 1], refs[count + 2 : 2 * count + 2]
    sem_in, sem_out = refs[3 * count + 3 :]
    pieces = large_buf.shape[0]
    rows = large_buf.shape[1]
    sources = [large.at[pl.ds(i * rows, rows)] for i in range(pieces)] + list(small)
    buffers = [large_buf.at[i] for i in range(pieces)] + list(small_buf)
    targets = [large_out.at[pl.ds(i * rows, rows)] for i in range(pieces)] + list(small_out)
    inward = [
        pltpu.make_async_copy(source, buffer, sem_in.at[i])
        for i, (source, buffer) in enumerate(zip(sources, buffers))
    ]
    outward = [
        pltpu.make_async_copy(buffer, target, sem_out.at[i])
        for i, (buffer, target) in enumerate(zip(buffers, targets))
    ]
    for copy in inward:
        copy.start()
    for first, then in zip(inward, outward):
        first.wait()
        then.start()
    for copy in outward:
        copy.wait()


def hand_over(large, *small):
    anywhere = pl.BlockSpec(memory_space=pltpu.HBM)
    arrays = (large,) + small
    rows = large.shape[0]
    pieces = 6 if rows % 48 == 0 else 1
    return pl.pallas_call(
        functools.partial(hand_over_kernel, len(small)),
        out_shape=[jax.ShapeDtypeStruct(array.shape, array.dtype) for array in arrays],
        in_specs=[anywhere] * len(arrays),
        out_specs=[anywhere] * len(arrays),
        scratch_shapes=[pltpu.VMEM((pieces, rows // pieces) + large.shape[1:], large.dtype)]
        + [pltpu.VMEM(array.shape, array.dtype) for array in small]
        + [pltpu.SemaphoreType.DMA((len(small) + pieces,))] * 2,
        compiler_params=pltpu.CompilerParams(vmem_limit_bytes=60 << 20),
        name="hand_over",
    )(*arrays)


def staged(mesh_shape, windows, cotangent, valid, *owned):
    x, cot = windows[0], cotangent[0]
    bq, bv, bo, bu, bd, gain_one, shift_one, gain_two, shift_two = owned[6:]
    short = [bq, bv, bo, bd, gain_one, shift_one, gain_two, shift_two, bu]
    qa, ka, vt, ht, ot, qe, vectors, first, second = attend(mesh_shape, x, *owned[:6], *short)
    out, dx, do, de, grads, small = mlp(valid, x, cot, ot, second, vectors)
    results = attend_back(
        mesh_shape, x, dx, qa, ka, vt, ht, qe, do, de, first, vectors, small, grads
    )
    dinput, gq, gk, gv, go, gu, gd, *shorts = hand_over(*results)
    gbq, gbv, gbo, gbd, *gains, gbu = shorts
    return (
        out.reshape(windows.shape),
        dinput.reshape(windows.shape),
        *(gq, gk, gv, go, gu, gd, gbq, gbv, gbo, gbu, gbd),
        *gains,
    )


def collective(windows, cotangent, valid, *owned):
    axes = ("batch", "shard")
    wq, wk, wv, wo, wu, wd, bq, bv, bo, bu, bd, gain_one, shift_one, gain_two, shift_two = [
        lax.all_gather(part, axes, axis=0, tiled=True) for part in owned
    ]
    x, cot = windows[0], cotangent[0]
    width, hidden = wu.shape
    blocks, chunks = width // 16, hidden // FF_CHUNK
    split = lambda part: part.reshape(blocks, -1, width)
    vectors = jnp.concatenate(
        [jnp.pad(bu.reshape(chunks, FF_CHUNK), ((0, 8 - chunks), (0, 0)))]
        + [v[None] for v in (bq, bv, bo, bd, gain_one, shift_one, gain_two, shift_two)]
    ).astype(F32)
    first = jnp.concatenate([split(wq), split(wk), split(wv)], axis=1)
    ups = wu.reshape(blocks, 16, chunks, FF_CHUNK).transpose(0, 2, 1, 3)
    ups = ups.reshape(blocks, 16 * chunks, FF_CHUNK)
    second = jnp.concatenate([split(wo), ups, split(wd)], axis=1)
    qa, ka, vt, ht, ot, qe = attend(None, x, first, vectors)
    out, dx, do, de, grads, small = mlp(valid, x, cot, ot, second, vectors)
    dinput, first_grads, small = attend_back(
        None, x, dx, qa, ka, vt, ht, qe, do, de, first, vectors, small, None
    )
    first_grads, grads = first_grads.astype(F32), grads.astype(F32)
    joined = lambda part: part.reshape(-1, width)
    gwu = grads[:, 16 : 16 + 16 * chunks].reshape(blocks, chunks, 16, FF_CHUNK)
    gwu = gwu.transpose(0, 2, 1, 3).reshape(width, hidden)
    totals = (
        joined(first_grads[:, 0:16]),
        joined(first_grads[:, 16:32]),
        joined(first_grads[:, 32:48]),
        joined(grads[:, 0:16]),
        gwu,
        joined(grads[:, 16 + 16 * chunks :]),
        small[8],
        small[9],
        small[10],
        small[:chunks].reshape(hidden),
        small[11],
        small[12],
        small[13],
        small[14],
        small[15],
    )
    grads = [lax.psum_scatter(total, axes, scatter_dimension=0, tiled=True) for total in totals]
    return (out.reshape(windows.shape), dinput.reshape(windows.shape), *grads)


def solution(mesh):
    both = ("batch", "shard")
    windows_spec, matrix_spec, vector_spec = P(both, None, None), P(both, None), P(both)
    params = (matrix_spec,) * 6 + (vector_spec,) * 9
    mesh_shape = (mesh.shape["batch"], mesh.shape["shard"])

    def per_device(windows, cotangent, valid, *owned):
        if mesh_shape[1] == 4 and mesh_shape[0] % 2 == 0 and owned[0].shape[0] == 16:
            return staged(mesh_shape, windows, cotangent, valid, *owned)
        return collective(windows, cotangent, valid, *owned)

    return jax.shard_map(
        per_device,
        mesh=mesh,
        in_specs=(windows_spec, windows_spec, vector_spec) + params,
        out_specs=(windows_spec, windows_spec) + params,
        check_vma=False,
    )
```
